128 devices in a mesh: dp: 16 (over z, y), mp: 8 (over x, core).
Axes of the slice: x: 4, y: 4, z: 4, core: 2. Of those that a mesh axis runs over, the one named last changes fastest.
Arguments:
- residual: bfloat16 [2048, 4096], P('dp', 'mp'), may hold values from -18 to 18
- queries: bfloat16 [2048, 4096], P('dp', 'mp'), may hold values from -20 to 20
- new_keys: bfloat16 [2048, 1024], P('dp', 'mp'), may hold values from -6 to 6
- new_values: bfloat16 [2048, 1024], P('dp', 'mp'), may hold values from -6 to 6
- cache_keys: bfloat16 [2048, 16, 1024], P('dp', None, 'mp'), may hold values from -6 to 6
- cache_values: bfloat16 [2048, 16, 1024], P('dp', None, 'mp'), may hold values from -6 to 6
- cache_len: int32 [1024], replicated, may hold values from 1 to 128, 16384 in all
- page_order: int32 [2048], replicated, may hold values from 0 to 2047, each once
- out_proj: bfloat16 [4096, 4096], P('mp'), may hold values from -0.09375 to 0.09375
- attn_gain: float32 [4096], replicated, may hold values from 0.25 to 1.75
- routes: int32 [2048, 2], P('dp'), may hold values from 0 to 7, all different within a row; in each aligned block of 128 rows (0 to 127, 128 to 255, ...) at most 48 rows name the same one
- route_weight: float32 [2048, 2], P('dp'), may hold values from 0.1 to 1
- gate_proj: bfloat16 [4096, 98304], P(None, ('dp', 'mp')), may hold values from -0.09375 to 0.09375
- up_proj: bfloat16 [4096, 98304], P(None, ('dp', 'mp')), may hold values from -0.09375 to 0.09375
- down_proj: bfloat16 [98304, 4096], P(('dp', 'mp')), may hold values from -0.0546875 to 0.0546875
- final_gain: float32 [4096], P('mp'), may hold values from 0.25 to 1.75
Outputs:
- layer_out: bfloat16 [2048, 4096], P('dp', 'mp')
The draws below stay inside these ranges and needn't reach their ends.
Inputs may be any that keep to these rules, and one draw needn't show every extreme that they name: `routes`: in each aligned block of 128 rows (the rows of one dp group) no expert is named by more than 48 rows, a bound that some block reaches; a row's two experts differ. `cache_len`: the lengths sum to 16384, and the longest is exactly 128. `page_order`: each page number appears once; pages past the last request's are unused.
All inputs are finite; a program needn't handle non-finite values.
Results may differ from the reference program's by a relative error of at most 0.008.
Values may be sent and summed in bfloat16 or wider, within the bound.
A program may use at most 128 MiB of HBM per device.

```python
import math
import jax
import jax.numpy as jnp
import numpy as np
from jax import lax

D = 4096
HQ = 32
KVH = 8
HD = 128
E = 8
FF = 12288
PAGE = 16
MAXLEN = 128
MEANLEN = 16
DEC = 64
PRE = 64
TOK_DEV = 128
TOKENS = 2048
DECODES = 1024
C = 48
POOL = 2048
N_DP = 16
N_MP = 8


def drawn_keys(key, leading, salt):
    own_key = jax.random.fold_in(key, salt)
    shape = leading + (KVH, HD)
    drawn = jnp.clip(jax.random.normal(jax.random.fold_in(own_key, 1), shape, jnp.float32), -6.0, 6.0)
    return drawn


def draw_queries(key, part):
    own_key = jax.random.fold_in(key, 13)
    shape = (TOKENS, HQ, HD)
    drawn = jnp.clip(jax.random.normal(jax.random.fold_in(own_key, 1), shape, jnp.float32), -6.0, 6.0)
    return drawn.reshape(TOKENS, HQ * HD).astype(jnp.bfloat16)


def draw_new_keys(key, part):
    return drawn_keys(key, (TOKENS,), 11).reshape(TOKENS, KVH * HD).astype(jnp.bfloat16)


def draw_cache_keys(key, part):
    return drawn_keys(key, (POOL, PAGE), 17).reshape(POOL, PAGE, KVH * HD).astype(jnp.bfloat16)


def draw_residual(key, part):
    own_key = jax.random.fold_in(key, 29)
    shape = (TOKENS, D)
    position = lax.broadcasted_iota(jnp.float32, (1, D), 1) / (D - 1.0)
    drawn = jnp.clip(jax.random.normal(jax.random.fold_in(own_key, 1), shape, jnp.float32), -6.0, 6.0)
    ramp = jnp.exp(jnp.log(0.6) + (jnp.log(3.0) - jnp.log(0.6)) * position)
    return (drawn * ramp).astype(jnp.bfloat16)


def shard_levels(stream_key, extent, split, low, largest):
    def one(axis_at, shards_of):
        heights = jax.random.uniform(jax.random.fold_in(jax.random.fold_in(stream_key, 6), axis_at), (shards_of,), jnp.float32, low / len(split), largest / len(split))
        return jnp.repeat(jnp.exp(heights), extent[axis_at] // shards_of).reshape((-1,) + (1,) * (len(extent) - axis_at - 1))

    loudness = one(*split[0])
    for cut in split[1:]:
        loudness = loudness * one(*cut)
    return loudness


def split_up(count, total, reach, slope):
    loads = [(1 << 20) // math.isqrt(grade ** slope) + 1 for grade in range(2, count + 1)]
    surplus, given = total - reach - (count - 1), [1] * (count - 1)
    while surplus > 0:
        free = [i for i in range(count - 1) if given[i] < reach]
        pool, budget = sum([loads[i] for i in free]), surplus
        for i in free:
            more = min(reach - given[i], max(1, budget * loads[i] // pool), surplus)
            given[i] = given[i] + more
            surplus = surplus - more
    return np.array([reach] + given)


def ragged(stream_key, amount, total, reach, lean):
    if amount == 2:
        one = jax.random.randint(stream_key, (), max(1, total - reach), min(reach, total - 1) + 1)
        return jnp.stack([one, total - one])
    tallies = jnp.asarray(split_up(amount, total, reach, lean), jnp.int32)
    twos = (amount - 1) // 2
    giver, sink = tallies[1:1 + 2 * twos:2], tallies[2:2 + 2 * twos:2]
    slack = jnp.minimum(giver - 1, reach - sink)
    shifted = jax.random.randint(jax.random.fold_in(stream_key, 1), (twos,), 0, 1 << 20) % (slack + 1)
    tallies = tallies.at[1:1 + 2 * twos:2].set(giver - shifted).at[2:2 + 2 * twos:2].set(sink + shifted)
    return tallies[jax.random.permutation(jax.random.fold_in(stream_key, 2), amount)]


def routed_block(key, own, number, rows, amount, top, most, lean):
    ranking = jax.random.permutation(key, amount)
    crowded, ordinary = portions_of(amount, rows * top, most, lean, True), portions_of(amount, rows * top, most, lean, False)
    places = jnp.arange(amount)

    def named(lengths, offset_by):
        used = int((lengths > 0).sum())
        fixed = max(1, used // 4)
        passed = fixed + (places - fixed + offset_by * (used - fixed)) % max(1, amount - fixed)
        return jnp.zeros((amount,), jnp.int32).at[ranking[jnp.where(places < fixed, places, passed)]].set(jnp.asarray(lengths, jnp.int32))

    lengths = jnp.where(number % 4 == 0, named(crowded, number // 4), named(ordinary, number - number // 4 - 1))
    mixed = jax.random.permutation(jax.random.fold_in(own, 3), amount)
    source_of, sink = mixed[0:amount // 2 * 2:2], mixed[1:amount // 2 * 2:2]
    slack = jnp.minimum(lengths[source_of] - 1, most - lengths[sink]) // 2
    slack = jnp.where((source_of == ranking[0]) | (sink == ranking[0]) | (lengths[sink] == 0), 0, jnp.maximum(slack, 0))
    passed = jax.random.randint(jax.random.fold_in(own, 4), (amount // 2,), 0, 1 << 20) % (slack + 1)
    lengths = lengths.at[source_of].add(-passed).at[sink].add(passed)
    members = jnp.searchsorted(jnp.cumsum(lengths), jnp.arange(rows * top), side="right").astype(jnp.int32)
    table = members.reshape(top, rows).T
    table = table[jax.random.permutation(jax.random.fold_in(own, 1), rows)]
    offset_by = jax.random.randint(jax.random.fold_in(own, 2), (rows, 1), 0, top)
    return jnp.take_along_axis(table, (jnp.arange(top)[None, :] + offset_by) % top, axis=1)


def portions_of(number_of, total, limit, skew, full):
    portions = [(1 << 20) // math.isqrt(standing ** skew) + 1 for standing in range(1, number_of + 1)]
    largest = limit if full else min(limit, max(-(-total // number_of), total * portions[0] // sum(portions)))
    least = 1 if total - largest >= number_of - 1 else 0
    holding, rest = [largest] + [least] * (number_of - 1), total - largest - least * (number_of - 1)
    while rest > 0:
        movable = [i for i in range(1, number_of) if holding[i] < largest] or [i for i in range(1, number_of) if holding[i] < limit]
        mass, budget = sum([portions[i] for i in movable]), rest
        for i in movable:
            more = min(limit - holding[i], max(1, budget * portions[i] // mass), rest)
            holding[i] = holding[i] + more
            rest = rest - more
    return np.array(holding)


def noise(key, dims, deviation, reach, split=(), held_as=jnp.bfloat16):
    factor_of = shard_levels(key, dims, split, -0.22, 0.18) if split else 1.0
    entries = jax.random.normal(key, dims, jnp.float32) * deviation * factor_of
    return jnp.minimum(jnp.maximum(entries, -reach), reach).astype(held_as)


def setup_inputs(seed: int = 0) -> dict:
    key_of = jax.random.split(jax.random.key(seed), 17)
    residual = draw_residual(jax.random.fold_in(key_of[16], 71), 0)
    queries = draw_queries(jax.random.fold_in(key_of[16], 71), 0)
    new_keys = draw_new_keys(jax.random.fold_in(key_of[16], 71), 0)
    new_values = noise(key_of[3], (TOKENS, KVH * HD), 1.0, 6.0, ((0, 16), (1, 8)))
    cache_keys = draw_cache_keys(jax.random.fold_in(key_of[16], 71), 0)
    cache_values = noise(key_of[5], (POOL, PAGE, KVH * HD), 1.0, 6.0, ((0, 16), (2, 8)))
    cache_len = ragged(key_of[6], DECODES, MEANLEN * DECODES, MAXLEN, 3).astype(jnp.int32)
    page_order = jax.random.permutation(key_of[7], POOL).astype(jnp.int32)
    out_proj = noise(key_of[8], (HQ * HD, D), (HQ * HD) ** -0.5, 0.09375, ((0, 8),))
    attn_gain = jnp.clip(1.0 + 0.15 * jax.random.normal(key_of[9], (D,), jnp.float32), 0.25, 1.75)
    routes_keys = jax.random.split(jax.random.fold_in(key_of[10], 1), TOKENS // TOK_DEV)
    routes_turns = jax.random.permutation(jax.random.fold_in(key_of[10], 3), TOKENS // TOK_DEV)
    routes = jax.vmap(lambda own, number: routed_block(jax.random.fold_in(key_of[10], 2), own, number, TOK_DEV, E, 2, C, 2))(routes_keys, routes_turns).reshape((TOKENS, 2))
    route_weight = jnp.clip(0.1 + 0.9 * jax.random.uniform(key_of[11], (TOKENS, 2), jnp.float32) ** shard_levels(key_of[11], (TOKENS, 2), ((0, 16),), -0.2, 0.2), 0.1, 1.0)
    gate_proj = noise(key_of[12], (D, E * FF), D ** -0.5, 0.09375, ((1, 128),))
    up_proj = noise(key_of[13], (D, E * FF), D ** -0.5, 0.09375, ((1, 128),))
    down_proj = noise(key_of[14], (E * FF, D), FF ** -0.5, 0.0546875, ((0, 128),))
    final_gain = jnp.clip(1.0 + 0.15 * jax.random.normal(key_of[15], (D,), jnp.float32), 0.25, 1.75)
    return dict(residual=residual, queries=queries, new_keys=new_keys, new_values=new_values, cache_keys=cache_keys, cache_values=cache_values, cache_len=cache_len, page_order=page_order, out_proj=out_proj, attn_gain=attn_gain, routes=routes, route_weight=route_weight, gate_proj=gate_proj, up_proj=up_proj, down_proj=down_proj, final_gain=final_gain)


neg_big = -1e+30
eps_norm = 1e-05

def rms_scale(values):
    return lax.rsqrt(lax.optimization_barrier(jnp.mean(values * values, axis=-1, keepdims=True)) + eps_norm)

def reference(residual, queries, new_keys, new_values, cache_keys, cache_values, cache_len, page_order, out_proj, attn_gain, routes, route_weight, gate_proj, up_proj, down_proj, final_gain):
    highest = lax.Precision.HIGHEST
    scale = HD ** (-0.5)
    group_size = HQ // KVH
    page_count = ((cache_len + PAGE - 1) // PAGE).astype(jnp.int32)
    page_first = (jnp.cumsum(page_count) - page_count).astype(jnp.int32)
    slots_max = MAXLEN // PAGE
    page_slot = jnp.minimum(page_first[:, None] + jnp.arange(slots_max, dtype=jnp.int32)[None, :], POOL - 1).astype(jnp.int32)
    request_pages = page_order[page_slot]
    query_all = queries.reshape(N_DP, TOK_DEV, KVH, group_size, HD)
    key_all = new_keys.reshape(N_DP, TOK_DEV, KVH, HD)
    value_all = new_values.reshape(N_DP, TOK_DEV, KVH, HD)

    def decode_group(packed):
        group_queries, group_keys, group_values, group_pages, group_lengths = packed
        cached_keys = cache_keys[group_pages].reshape(DEC, MAXLEN, KVH, HD).astype(jnp.float32)
        cached_values = cache_values[group_pages].reshape(DEC, MAXLEN, KVH, HD).astype(jnp.float32)
        query_float = group_queries.astype(jnp.float32)
        cache_scores = jnp.einsum('rkgh,rjkh->rkgj', query_float, cached_keys, precision=highest) * scale
        self_score = jnp.einsum('rkgh,rkh->rkg', query_float, group_keys.astype(jnp.float32), precision=highest) * scale
        valid = (jnp.arange(MAXLEN, dtype=jnp.int32)[None, :] < group_lengths[:, None])[:, None, None, :]
        masked = jnp.where(valid, cache_scores, neg_big)
        top_score = jnp.maximum(lax.optimization_barrier(jnp.max(masked, axis=-1)), self_score)
        cache_weights = jnp.where(valid, jnp.exp(masked - top_score[..., None]), 0.0)
        self_weight = jnp.exp(self_score - top_score)
        numerator = jnp.einsum('rkgj,rjkh->rkgh', cache_weights, cached_values, precision=highest)
        numerator = numerator + self_weight[..., None] * group_values.astype(jnp.float32)[:, :, None, :]
        denominator = lax.optimization_barrier(jnp.sum(cache_weights, axis=-1)) + self_weight
        return (numerator / denominator[..., None]).astype(jnp.bfloat16)
    decode_out = lax.map(decode_group, (query_all[:, :DEC], key_all[:, :DEC], value_all[:, :DEC], request_pages.reshape(N_DP, DEC, slots_max), cache_len.reshape(N_DP, DEC)))
    prompt_q = query_all[:, DEC:].astype(jnp.float32)
    prompt_k = key_all[:, DEC:].astype(jnp.float32)
    prompt_v = value_all[:, DEC:].astype(jnp.float32)
    prompt_scores = jnp.einsum('nqkgh,ntkh->nkgqt', prompt_q, prompt_k, precision=highest) * scale
    causal = jnp.arange(PRE, dtype=jnp.int32)[:, None] >= jnp.arange(PRE, dtype=jnp.int32)[None, :]
    masked = jnp.where(causal, prompt_scores, neg_big)
    top_prompt = lax.optimization_barrier(jnp.max(masked, axis=-1, keepdims=True))
    prompt_weights = jnp.where(causal, jnp.exp(masked - top_prompt), 0.0)
    numerator = jnp.einsum('nkgqt,ntkh->nqkgh', prompt_weights, prompt_v, precision=highest)
    denominator = lax.optimization_barrier(jnp.sum(prompt_weights, axis=-1)).transpose(0, 3, 1, 2)
    prompt_out = (numerator / denominator[..., None]).astype(jnp.bfloat16)
    attn = jnp.concatenate([decode_out, prompt_out], axis=1).reshape(TOKENS, HQ * HD)
    hidden_state = residual.astype(jnp.float32) + jnp.dot(attn, out_proj, preferred_element_type=jnp.float32)
    normed = (hidden_state * rms_scale(hidden_state) * attn_gain).astype(jnp.bfloat16)
    pairs = routes.reshape(N_DP, TOK_DEV * 2).astype(jnp.int32)
    onehot = (pairs[..., None] == jnp.arange(E, dtype=jnp.int32)[None, None, :]).astype(jnp.int32)
    slots = lax.optimization_barrier(jnp.sum((jnp.cumsum(onehot, axis=1) - onehot) * onehot, axis=-1)).astype(jnp.int32)
    group_ids = jnp.broadcast_to(jnp.arange(N_DP, dtype=jnp.int32)[:, None], pairs.shape)
    pair_rows = jnp.repeat(normed.reshape(N_DP, TOK_DEV, D), 2, axis=1)
    buffer = jnp.zeros((E, N_DP, C, D), jnp.bfloat16).at[pairs, group_ids, slots].set(pair_rows)
    blocks = N_DP // E * N_MP
    block_width = FF // blocks

    def run_expert(expert_no):
        rows = lax.dynamic_index_in_dim(buffer, expert_no, 0, keepdims=False).reshape(N_DP * C, D)
        gate_cols = lax.dynamic_slice_in_dim(gate_proj, expert_no * FF, FF, 1)
        up_cols = lax.dynamic_slice_in_dim(up_proj, expert_no * FF, FF, 1)
        gate_sum = jnp.dot(rows, gate_cols, preferred_element_type=jnp.float32)
        up_sum = jnp.dot(rows, up_cols, preferred_element_type=jnp.float32)
        hidden = (jax.nn.silu(gate_sum) * up_sum).astype(jnp.bfloat16)
        down_rows = lax.dynamic_slice_in_dim(down_proj, expert_no * FF, FF, 0)

        def add_block(total, block_no):
            hidden_block = lax.dynamic_slice_in_dim(hidden, block_no * block_width, block_width, 1)
            weight_block = lax.dynamic_slice_in_dim(down_rows, block_no * block_width, block_width, 0)
            partial_value = jnp.dot(hidden_block, weight_block, preferred_element_type=jnp.float32).astype(jnp.bfloat16)
            partial_value = lax.optimization_barrier(partial_value)
            return (total + partial_value.astype(jnp.float32), None)
        total, unused = lax.scan(add_block, jnp.zeros((N_DP * C, D), jnp.float32), jnp.arange(blocks, dtype=jnp.int32))
        return total.reshape(N_DP, C, D)
    expert_out = lax.map(run_expert, jnp.arange(E, dtype=jnp.int32))
    picked = expert_out[pairs, group_ids, slots]
    weights = route_weight.reshape(N_DP, TOK_DEV * 2)
    moe_rows = (picked * weights[..., None]).reshape(N_DP, TOK_DEV, 2, D).sum(axis=2).reshape(TOKENS, D)
    mixed = hidden_state + moe_rows
    return (mixed * rms_scale(mixed) * final_gain).astype(jnp.bfloat16)
```

```python
import functools

import jax
import jax.numpy as jnp
from jax import lax
from jax.experimental import pallas as pl
from jax.experimental.pallas import tpu as pltpu
from jax.sharding import PartitionSpec as P

D = 4096
HQ = 32
KVH = 8
HD = 128
E = 8
PAGE = 16
DEC = 64
PRE = 64
C = 48
NDP = 16
NCH = 3
SL = C // NCH
RC = NDP * SL
FW = 512
HID = 768

MESH = pl.DeviceIdType.MESH
DMA = pltpu.SemaphoreType.DMA
BF = jnp.bfloat16
F32 = jnp.float32

neg_big = -1e30
eps_norm = 1e-05


def remote(src, dst, send_sem, recv_sem, device):
    return pltpu.make_async_remote_copy(
        src_ref=src,
        dst_ref=dst,
        send_sem=send_sem,
        recv_sem=recv_sem,
        device_id=device,
        device_id_type=MESH,
    )


def greet(devices):
    barrier = pltpu.get_barrier_semaphore()
    for device in devices:
        pl.semaphore_signal(barrier, inc=1, device_id=device, device_id_type=MESH)
    pl.semaphore_wait(barrier, len(devices))


def comm_params(collective_id):
    return pltpu.CompilerParams(
        collective_id=collective_id, has_side_effects=True, vmem_limit_bytes=60 << 20
    )


def vmem(count):
    return [pl.BlockSpec(memory_space=pltpu.VMEM)] * count


def gather_kernel(src, dst, send, recv, own_sem):
    me = lax.axis_index("dp")
    peers = [lax.rem(me + k, NDP) for k in range(1, NDP)]
    greet([{"dp": p} for p in peers])
    own = pltpu.make_async_copy(src, dst.at[me], own_sem)
    own.start()
    copies = []
    for k, p in enumerate(peers):
        copies.append(remote(src, dst.at[me], send.at[k], recv.at[k], {"dp": p}))
        copies[-1].start()
    for copy in copies:
        copy.wait()
    own.wait()


def gather_dp(x, collective_id):
    return pl.pallas_call(
        gather_kernel,
        out_shape=jax.ShapeDtypeStruct((NDP,) + x.shape, x.dtype),
        in_specs=vmem(1),
        out_specs=vmem(1)[0],
        scratch_shapes=[DMA((NDP - 1,)), DMA((NDP - 1,)), DMA],
        compiler_params=comm_params(collective_id),
        name="gather_queries",
    )(x)


def swap_kernel(values, stats, values_out, stats_out, send, recv, own_sems):
    me = lax.axis_index("dp")
    peers = [lax.rem(me + k, NDP) for k in range(1, NDP)]
    greet([{"dp": p} for p in peers])
    own = [
        pltpu.make_async_copy(values.at[me], values_out.at[me], own_sems.at[0]),
        pltpu.make_async_copy(stats.at[me], stats_out.at[me], own_sems.at[1]),
    ]
    for copy in own:
        copy.start()
    copies = []
    for k, p in enumerate(peers):
        copies.append(
            remote(stats.at[p], stats_out.at[me], send.at[1, k], recv.at[1, k], {"dp": p})
        )
        copies.append(
            remote(values.at[p], values_out.at[me], send.at[0, k], recv.at[0, k], {"dp": p})
        )
    for copy in copies:
        copy.start()
    for copy in copies:
        copy.wait()
    for copy in own:
        copy.wait()


def swap_partials(values, stats, collective_id):
    return pl.pallas_call(
        swap_kernel,
        out_shape=(
            jax.ShapeDtypeStruct(values.shape, values.dtype),
            jax.ShapeDtypeStruct(stats.shape, stats.dtype),
        ),
        in_specs=vmem(2),
        out_specs=tuple(vmem(2)),
        scratch_shapes=[DMA((2, NDP - 1)), DMA((2, NDP - 1)), DMA((2,))],
        compiler_params=comm_params(collective_id),
        name="swap_partials",
    )(values, stats)


def hidden_kernel(parts, residual, gain, hidden, normed, got, squares, send, recv, send2, recv2):
    me = lax.axis_index("mp")
    peers = [lax.rem(me + k, 8) for k in range(1, 8)]
    greet([{"mp": p} for p in peers])
    copies = []
    for k, p in enumerate(peers):
        copies.append(remote(parts.at[p], got.at[k], send.at[k], recv.at[k], {"mp": p}))
        copies[-1].start()
    total = residual[...].astype(F32) + parts[me].astype(F32)
    for k, copy in enumerate(copies):
        copy.wait_recv()
        total = total + got[k].astype(F32)
    hidden[...] = total
    squares[7] = jnp.broadcast_to(jnp.sum(total * total, axis=1, keepdims=True), (128, 128))
    copies2 = []
    for k, p in enumerate(peers):
        copies2.append(remote(squares.at[7], squares.at[k], send2.at[k], recv2.at[k], {"mp": p}))
        copies2[-1].start()
    for copy in copies2:
        copy.wait_recv()
    summed = squares[0]
    for k in range(1, 8):
        summed = summed + squares[k]
    scale = lax.rsqrt(summed[:, :1] / D + eps_norm)
    normed[...] = (hidden[...] * scale * gain[...]).astype(BF)
    for copy in copies + copies2:
        copy.wait_send()


def hidden_and_norm(parts, residual, gain, collective_id):
    rows = residual.shape[0]
    return pl.pallas_call(
        hidden_kernel,
        out_shape=(
            jax.ShapeDtypeStruct((rows, FW), F32),
            jax.ShapeDtypeStruct((rows, FW), BF),
        ),
        in_specs=vmem(3),
        out_specs=tuple(vmem(2)),
        scratch_shapes=[
            pltpu.VMEM((7, rows, FW), BF),
            pltpu.VMEM((8, rows, 128), F32),
            DMA((7,)),
            DMA((7,)),
            DMA((7,)),
            DMA((7,)),
        ],
        compiler_params=comm_params(collective_id),
        name="hidden_and_norm",
    )(parts, residual, gain)


def experts_kernel(
    send,
    wg,
    wu,
    wd,
    ret,
    x_all,
    wg_v,
    wu_v,
    wd_v,
    hid,
    part,
    own_part,
    hop_in,
    hop_out,
    fin,
    out,
    w_sems,
    wp_send,
    wp_recv,
    a_send,
    a_recv,
    a_own,
    g_send,
    g_recv,
    f_send,
    f_recv,
    p_send,
    p_recv,
    h_send,
    h_recv,
    t_send,
    t_recv,
    n_send,
    n_recv,
    r_send,
    r_recv,
    r_own,
):
    dp = lax.axis_index("dp")
    mp = lax.axis_index("mp")
    x, c = mp // 2, lax.rem(mp, 2)
    xr, xo, xl = lax.rem(x + 1, 4), lax.rem(x + 2, 4), lax.rem(x + 3, 4)
    mr, mo, ml = xr * 2 + c, xo * 2 + c, xl * 2 + c
    right, left, mate = {"mp": mr}, {"mp": ml}, {"mp": x * 2 + 1 - c}
    sides = (right, left)
    peers = [lax.rem(dp + k, NDP) for k in range(1, NDP)]
    half = RC // 2

    w_copies = [
        pltpu.make_async_copy(wg, wg_v, w_sems.at[0]),
        pltpu.make_async_copy(wu, wu_v, w_sems.at[1]),
    ]
    for j in range(4):
        w_copies.append(
            pltpu.make_async_copy(
                wd.at[:, pl.ds(pl.multiple_of(j * 1024 + c * FW, FW), FW)],
                wd_v.at[0, :, pl.ds(j * FW, FW)],
                w_sems.at[2 + j],
            )
        )
    greet([{"dp": p} for p in peers] + [right, left, mate])

    def columns(owner):
        return pl.ds(pl.multiple_of(owner * FW, FW), FW)

    sent = []

    def go(copy):
        copy.start()
        sent.append(copy)

    out_copies, own_copies = [], []
    for ch in range(NCH):
        rows = pl.ds(pl.multiple_of(dp * SL, SL), SL)
        own = pltpu.make_async_copy(send.at[ch, dp], x_all.at[ch, rows, columns(mp)], a_own.at[ch])
        own.start()
        own_copies.append(own)
        cs = []
        for k, p in enumerate(peers):
            copy = remote(
                send.at[ch, p],
                x_all.at[ch, rows, columns(mp)],
                a_send.at[ch, k],
                a_recv.at[ch, k],
                {"dp": p},
            )
            go(copy)
            cs.append(copy)
        out_copies.append(cs)
    for copy in w_copies:
        copy.start()
    mate_w = []
    for j in range(4):
        mate_w.append(
            remote(
                wd.at[:, pl.ds(pl.multiple_of(j * 1024 + (1 - c) * FW, FW), FW)],
                wd_v.at[1, :, pl.ds(j * FW, FW)],
                wp_send.at[j],
                wp_recv.at[j],
                mate,
            )
        )
        go(mate_w[j])

    def block(ch, h, owner):
        return x_all.at[ch, pl.ds(h * half, half), columns(owner)]

    def whole(ch, owner):
        return x_all.at[ch, :, columns(owner)]

    def neighbour(ch, side, h):
        return remote(block(ch, h, mp), block(ch, h, mp), g_send.at[ch, side, h], g_recv.at[ch, side, h], sides[side])

    def onward(ch, side):
        owner = (ml, mr)[side]
        return remote(
            block(ch, side, owner), block(ch, side, owner), f_send.at[ch, side], f_recv.at[ch, side], sides[side]
        )

    def to_mate(ch, which):
        owner = (mp, ml, mr, mo)[which]
        return remote(whole(ch, owner), whole(ch, owner), p_send.at[ch, which], p_recv.at[ch, which], mate)

    def spread_own(ch):
        for copy in out_copies[ch]:
            copy.wait_recv()
        own_copies[ch].wait()
        for h in range(2):
            go(neighbour(ch, 0, h))
            go(neighbour(ch, 1, 1 - h))
        go(to_mate(ch, 0))

    def spread_on(ch):
        for side in range(2):
            neighbour(ch, side, side).wait_recv()
            go(onward(ch, side))

    def spread_rest(ch):
        for side in range(2):
            neighbour(ch, side, 1 - side).wait_recv()
            go(to_mate(ch, 1 + side))

    def spread_far(ch):
        for side in range(2):
            onward(ch, side).wait_recv()
        go(to_mate(ch, 3))

    def spread_end(ch):
        for which in range(4):
            to_mate(ch, which).wait_recv()

    def hidden_send(ch):
        return remote(hid.at[ch, 0], hid.at[ch, 1], h_send.at[ch], h_recv.at[ch], mate)

    def gate_up(ch, n):
        cols = pl.ds(n * 256, 256)
        rows = x_all[ch]
        g = jnp.dot(rows, wg_v[:, cols], preferred_element_type=F32)
        u = jnp.dot(rows, wu_v[:, cols], preferred_element_type=F32)
        hid[ch, 0, :, cols] = (g / (1.0 + jnp.exp(-g)) * u).astype(BF)

    def down(ch, owner):
        cols = columns(owner)
        return jnp.dot(hid[ch, 0], wd_v[0, :, cols], preferred_element_type=F32) + jnp.dot(
            hid[ch, 1], wd_v[1, :, cols], preferred_element_type=F32
        )

    def rows_of(h):
        return pl.ds(h * half, half)

    def hop(ch, side):
        return remote(
            part.at[ch, 0, rows_of(side)], hop_in.at[ch, side], t_send.at[ch, side], t_recv.at[ch, side], sides[side]
        )

    def near(ch, side, h, src):
        return remote(src, fin.at[ch, side, rows_of(h)], n_send.at[ch, side, h], n_recv.at[ch, side, h], sides[side])

    def reduce_start(ch):
        part[ch, 0] = down(ch, xo).astype(BF)
        for side in range(2):
            go(hop(ch, side))
        for side in range(2):
            part[ch, 1 + side] = down(ch, (xr, xl)[side]).astype(BF)
            go(near(ch, side, 1 - side, part.at[ch, 1 + side, rows_of(1 - side)]))

    def reduce_own(ch):
        own_part[ch] = down(ch, x)

    def reduce_hop(ch):
        for side in range(2):
            hop(ch, side).wait_recv()
            hop_out[ch, side] = (
                part[ch, 1 + side, rows_of(side), :].astype(F32) + hop_in[ch, side].astype(F32)
            ).astype(BF)
            go(near(ch, side, side, hop_out.at[ch, side]))

    ret_copies = []

    def reduce_end(ch):
        for side in range(2):
            for h in range(2):
                near(ch, side, h, hop_out.at[ch, side]).wait_recv()
        total = own_part[ch] + fin[ch, 0].astype(F32) + fin[ch, 1].astype(F32)
        out[ch] = total.astype(BF)
        own = pltpu.make_async_copy(
            out.at[ch, pl.ds(pl.multiple_of(dp * SL, SL), SL)], ret.at[ch, dp], r_own.at[ch]
        )
        own.start()
        cs = [own]
        for k, p in enumerate(peers):
            copy = remote(
                out.at[ch, pl.ds(pl.multiple_of(p * SL, SL), SL)],
                ret.at[ch, dp],
                r_send.at[ch, k],
                r_recv.at[ch, k],
                {"dp": p},
            )
            copy.start()
            cs.append(copy)
        ret_copies.extend(cs)

    spread_own(0)
    spread_on(0)
    spread_own(1)
    spread_rest(0)
    spread_far(0)
    for copy in w_copies[:2]:
        copy.wait()
    spread_on(1)
    spread_own(2)
    spread_end(0)
    for ch in range(NCH):
        gate_up(ch, 0)
        if ch == 0:
            spread_rest(1)
        if ch == 1:
            reduce_hop(0)
        if ch == 2:
            reduce_hop(1)
        gate_up(ch, 1)
        if ch == 0:
            spread_far(1)
        if ch == 1:
            spread_rest(2)
        gate_up(ch, 2)
        go(hidden_send(ch))
        if ch == 0:
            spread_on(2)
            for copy in w_copies[2:]:
                copy.wait()
            for copy in mate_w:
                copy.wait_recv()
        if ch == 1:
            spread_far(2)
            reduce_end(0)
        if ch == 2:
            reduce_end(1)
        hidden_send(ch).wait_recv()
        reduce_start(ch)
        reduce_own(ch)
        if ch < 2:
            spread_end(ch + 1)
    reduce_hop(2)
    reduce_end(2)
    for copy in ret_copies:
        copy.wait()
    for copy in sent:
        copy.wait_send()


def experts(send, wg, wu, wd, collective_id):
    anyspace = pl.BlockSpec(memory_space=pl.ANY)
    return pl.pallas_call(
        experts_kernel,
        out_shape=jax.ShapeDtypeStruct((NCH, NDP, SL, FW), BF),
        in_specs=vmem(1) + [anyspace] * 3,
        out_specs=vmem(1)[0],
        scratch_shapes=[
            pltpu.VMEM((NCH, RC, D), BF),
            pltpu.VMEM((D, HID), BF),
            pltpu.VMEM((D, HID), BF),
            pltpu.VMEM((2, HID, D // 2), BF),
            pltpu.VMEM((NCH, 2, RC, HID), BF),
            pltpu.VMEM((NCH, 3, RC, FW), BF),
            pltpu.VMEM((NCH, RC, FW), F32),
            pltpu.VMEM((NCH, 2, RC // 2, FW), BF),
            pltpu.VMEM((NCH, 2, RC // 2, FW), BF),
            pltpu.VMEM((NCH, 2, RC, FW), BF),
            pltpu.VMEM((NCH, RC, FW), BF),
            DMA((6,)),
            DMA((4,)),
            DMA((4,)),
            DMA((NCH, NDP - 1)),
            DMA((NCH, NDP - 1)),
            DMA((NCH,)),
            DMA((NCH, 2, 2)),
            DMA((NCH, 2, 2)),
            DMA((NCH, 2)),
            DMA((NCH, 2)),
            DMA((NCH, 4)),
            DMA((NCH, 4)),
            DMA((NCH,)),
            DMA((NCH,)),
            DMA((NCH, 2)),
            DMA((NCH, 2)),
            DMA((NCH, 2, 2)),
            DMA((NCH, 2, 2)),
            DMA((NCH, NDP - 1)),
            DMA((NCH, NDP - 1)),
            DMA((NCH,)),
        ],
        compiler_params=comm_params(collective_id),
        name="experts",
    )(send, wg, wu, wd)


def closing_kernel(mixed, gain, out, squares, send, recv):
    me = lax.axis_index("mp")
    peers = [lax.rem(me + k, 8) for k in range(1, 8)]
    greet([{"mp": p} for p in peers])
    rows = mixed[...]
    squares[7] = jnp.broadcast_to(jnp.sum(rows * rows, axis=1, keepdims=True), (128, 128))
    copies = []
    for k, p in enumerate(peers):
        copies.append(remote(squares.at[7], squares.at[k], send.at[k], recv.at[k], {"mp": p}))
        copies[-1].start()
    for copy in copies:
        copy.wait_recv()
    summed = squares[0]
    for k in range(1, 8):
        summed = summed + squares[k]
    scale = lax.rsqrt(summed[:, :1] / D + eps_norm)
    out[...] = (mixed[...] * scale * gain[...]).astype(BF)
    for copy in copies:
        copy.wait_send()


def closing_norm(mixed, gain, collective_id):
    rows = mixed.shape[0]
    return pl.pallas_call(
        closing_kernel,
        out_shape=jax.ShapeDtypeStruct((rows, FW), BF),
        in_specs=vmem(2),
        out_specs=vmem(1)[0],
        scratch_shapes=[pltpu.VMEM((8, rows, 128), F32), DMA((7,)), DMA((7,))],
        compiler_params=comm_params(collective_id),
        name="closing_norm",
    )(mixed, gain)


def page_owner(page_ids, page_order, cache_len):
    page_count = (cache_len + PAGE - 1) // PAGE
    page_ends = jnp.cumsum(page_count)
    page_first = page_ends - page_count
    pool_iota = lax.broadcasted_iota(jnp.int32, (1, page_order.shape[0]), 1)
    order_pos = jnp.sum(jnp.where(page_order[None, :] == page_ids[:, None], pool_iota, 0), axis=1)
    owners = jnp.sum((page_ends[None, :] <= order_pos[:, None]).astype(jnp.int32), axis=1)
    request_iota = lax.broadcasted_iota(jnp.int32, (1, cache_len.shape[0]), 1)
    chosen = request_iota == owners[:, None]
    first_own = jnp.sum(jnp.where(chosen, page_first[None, :], 0), axis=1)
    length_own = jnp.sum(jnp.where(chosen, cache_len[None, :], 0), axis=1)
    offsets = lax.broadcasted_iota(jnp.int32, (1, PAGE), 1)
    key_pos = (order_pos - first_own)[:, None] * PAGE + offsets
    return (owners, key_pos < length_own[:, None])


def page_partials(page_queries, key_pages, value_pages, key_ok, scale):
    scores = (
        jnp.einsum("pkgh,pokh->pkgo", page_queries, key_pages, preferred_element_type=jnp.float32)
        * scale
    )
    wide_mask = key_ok[:, None, None, :]
    masked = jnp.where(wide_mask, scores, neg_big)
    maxima = jnp.max(masked, axis=3)
    weights = jnp.where(wide_mask, jnp.exp(masked - maxima[..., None]), 0.0)
    totals = jnp.sum(weights, axis=3)
    weighted = jnp.einsum(
        "pkgo,pokh->pkgh",
        weights,
        value_pages.astype(jnp.float32),
        precision=lax.Precision.HIGHEST,
        preferred_element_type=jnp.float32,
    )
    return (maxima, totals, weighted)


def fold_pages(maxima, totals, weighted, owned, local_owner):
    top_score = jnp.max(jnp.where(owned[:, :, None, None], maxima[:, None], neg_big), axis=0)
    page_top = top_score[local_owner]
    factors = jnp.exp(maxima - page_top)
    owned_float = owned.astype(jnp.float32)
    sums = jnp.einsum("pr,pkg->rkg", owned_float, totals * factors, precision=lax.Precision.HIGHEST)
    values = jnp.einsum(
        "pr,pkgh->rkgh", owned_float, weighted * factors[..., None], precision=lax.Precision.HIGHEST
    )
    return (top_score, sums, values)


def local(
    residual,
    queries,
    new_keys,
    new_values,
    cache_keys,
    cache_values,
    cache_len,
    page_order,
    out_proj,
    attn_gain,
    routes,
    route_weight,
    gate_proj,
    up_proj,
    down_proj,
    final_gain,
):
    dp_count = lax.axis_size("dp")
    dp_index = lax.axis_index("dp")
    mp_index = lax.axis_index("mp")
    scale = HD ** (-0.5)
    kv_local = new_keys.shape[1] // HD
    group_size = HQ // KVH
    width_local = residual.shape[1]
    pool_local = cache_keys.shape[0]
    request_total = cache_len.shape[0]
    query_heads = queries[:DEC].reshape(DEC, kv_local, group_size, HD)
    gathered = gather_dp(queries[:DEC], 0)
    gathered_heads = gathered.reshape(request_total, kv_local, group_size, HD)
    page_ids = dp_index * pool_local + lax.broadcasted_iota(jnp.int32, (pool_local,), 0)
    owners, key_ok = page_owner(page_ids, page_order, cache_len)
    live = owners < request_total
    local_owner = jnp.minimum(owners, request_total - 1)
    key_ok = key_ok & live[:, None]
    key_pages = cache_keys.reshape(pool_local, PAGE, kv_local, HD)
    value_pages = cache_values.reshape(pool_local, PAGE, kv_local, HD)
    page_queries = gathered_heads[local_owner]
    maxima, totals, weighted = page_partials(page_queries, key_pages, value_pages, key_ok, scale)
    owned = (local_owner[:, None] == lax.broadcasted_iota(jnp.int32, (1, request_total), 1)) & live[
        :, None
    ]
    maxima, totals, weighted = fold_pages(maxima, totals, weighted, owned, local_owner)
    stats = jnp.concatenate([maxima.reshape(request_total, 4), totals.reshape(request_total, 4)], axis=1)
    stats = stats.reshape(dp_count, DEC, 8).transpose(0, 2, 1)
    stats = jnp.pad(stats, ((0, 0), (0, 0), (0, 128 - DEC)))
    values_in, stats_in = swap_partials(
        weighted.reshape(dp_count, DEC, FW).astype(BF), stats, 1
    )
    stats_in = stats_in[:, :, :DEC].transpose(0, 2, 1)
    maxima = stats_in[:, :, :4].reshape(dp_count, DEC, kv_local, group_size)
    totals = stats_in[:, :, 4:].reshape(dp_count, DEC, kv_local, group_size)
    weighted = values_in.reshape(dp_count, DEC, kv_local, group_size, HD).astype(F32)
    top_cache = jnp.max(maxima, axis=0)
    factors = jnp.exp(maxima - top_cache[None])
    cache_state = (
        top_cache,
        jnp.sum(totals * factors, axis=0),
        jnp.sum(weighted * factors[..., None], axis=0),
    )
    self_keys = new_keys[:DEC].reshape(DEC, kv_local, HD)
    self_values = new_values[:DEC].reshape(DEC, kv_local, HD).astype(jnp.float32)
    self_score = (
        jnp.einsum("rkgh,rkh->rkg", query_heads, self_keys, preferred_element_type=jnp.float32)
        * scale
    )
    cache_top, cache_total, cache_sum = cache_state
    top_score = jnp.maximum(cache_top, self_score)
    cache_factor = jnp.exp(cache_top - top_score)
    self_factor = jnp.exp(self_score - top_score)
    numerator = (
        cache_sum * cache_factor[..., None] + self_factor[..., None] * self_values[:, :, None, :]
    )
    denominator = cache_total * cache_factor + self_factor
    decode_out = (numerator / denominator[..., None]).astype(jnp.bfloat16).reshape(DEC, -1)
    prompt_q = queries[DEC:].reshape(PRE, kv_local, group_size, HD)
    prompt_k = new_keys[DEC:].reshape(PRE, kv_local, HD)
    prompt_v = new_values[DEC:].reshape(PRE, kv_local, HD).astype(jnp.float32)
    prompt_scores = (
        jnp.einsum("qkgh,tkh->kgqt", prompt_q, prompt_k, preferred_element_type=jnp.float32) * scale
    )
    causal = lax.broadcasted_iota(jnp.int32, (PRE, PRE), 0) >= lax.broadcasted_iota(
        jnp.int32, (PRE, PRE), 1
    )
    masked = jnp.where(causal, prompt_scores, neg_big)
    top_prompt = jnp.max(masked, axis=-1, keepdims=True)
    prompt_weights = jnp.where(causal, jnp.exp(masked - top_prompt), 0.0)
    prompt_num = jnp.einsum(
        "kgqt,tkh->qkgh",
        prompt_weights,
        prompt_v,
        precision=lax.Precision.HIGHEST,
        preferred_element_type=jnp.float32,
    )
    prompt_den = jnp.sum(prompt_weights, axis=-1).transpose(2, 0, 1)
    prompt_out = (prompt_num / prompt_den[..., None]).astype(jnp.bfloat16).reshape(PRE, -1)
    attn = jnp.concatenate([decode_out, prompt_out], axis=0)
    parts = jnp.einsum(
        "th,hpc->ptc", attn, out_proj.reshape(FW, 8, FW), preferred_element_type=jnp.float32
    ).astype(BF)
    column_start = mp_index * width_local
    gain_cols = lax.dynamic_slice_in_dim(attn_gain, column_start, width_local, 0)
    hidden_cols, normed = hidden_and_norm(parts, residual, gain_cols[None, :], 2)
    tok_rows = residual.shape[0]
    pairs = routes.reshape(-1)
    onehot = (pairs[:, None] == lax.broadcasted_iota(jnp.int32, (1, E), 1)).astype(jnp.int32)
    slots = jnp.sum((jnp.cumsum(onehot, axis=0) - onehot) * onehot, axis=1)
    target = (slots // SL) * (E * SL) + pairs * SL + slots % SL
    cells = lax.broadcasted_iota(jnp.int32, (1, E * C), 1)
    hits = (target[:, None] == cells).reshape(tok_rows, 2, E * C)
    dispatch = jnp.any(hits, axis=1).astype(jnp.bfloat16)
    combine = jnp.sum(jnp.where(hits, route_weight[:, :, None], 0.0), axis=1)
    buffer = lax.dot_general(
        dispatch, normed, (((0,), (0,)), ((), ())), preferred_element_type=jnp.float32
    ).astype(jnp.bfloat16)
    send = jnp.repeat(buffer.reshape(NCH, E, SL, width_local), dp_count // E, axis=1)
    returned = experts(send, gate_proj, up_proj, down_proj, 3)
    back = (
        returned.astype(F32)
        .reshape(NCH, E, dp_count // E, SL, width_local)
        .sum(axis=2)
        .reshape(E * C, width_local)
    )
    moe_rows = jnp.dot(
        combine, back, precision=lax.Precision.HIGHEST, preferred_element_type=jnp.float32
    )
    mixed = hidden_cols + moe_rows
    return closing_norm(mixed, final_gain[None, :], 4)


def solution(mesh):
    return jax.shard_map(
        local,
        mesh=mesh,
        in_specs=(
            P("dp", "mp"),
            P("dp", "mp"),
            P("dp", "mp"),
            P("dp", "mp"),
            P("dp", None, "mp"),
            P("dp", None, "mp"),
            P(),
            P(),
            P("mp", None),
            P(),
            P("dp", None),
            P("dp", None),
            P(None, ("dp", "mp")),
            P(None, ("dp", "mp")),
            P(("dp", "mp"), None),
            P("mp"),
        ),
        out_specs=P("dp", "mp"),
        check_vma=False,
    )
```

```python
import functools

import jax
import jax.numpy as jnp
from jax import lax
from jax.experimental import pallas as pl
from jax.experimental.pallas import tpu as pltpu
from jax.sharding import PartitionSpec as P

D = 4096
HQ = 32
KVH = 8
HD = 128
E = 8
PAGE = 16
DEC = 64
PRE = 64
C = 48
NDP = 16
NCH = 3
SL = C // NCH
RC = NDP * SL
FW = 512
HID = 768

MESH = pl.DeviceIdType.MESH
DMA = pltpu.SemaphoreType.DMA
BF = jnp.bfloat16
F32 = jnp.float32

neg_big = -1e30
eps_norm = 1e-05


def remote(src, dst, send_sem, recv_sem, device):
    return pltpu.make_async_remote_copy(
        src_ref=src,
        dst_ref=dst,
        send_sem=send_sem,
        recv_sem=recv_sem,
        device_id=device,
        device_id_type=MESH,
    )


def greet(devices):
    barrier = pltpu.get_barrier_semaphore()
    for device in devices:
        pl.semaphore_signal(barrier, inc=1, device_id=device, device_id_type=MESH)
    pl.semaphore_wait(barrier, len(devices))


def comm_params(collective_id):
    return pltpu.CompilerParams(
        collective_id=collective_id, has_side_effects=True, vmem_limit_bytes=60 << 20
    )


def vmem(count):
    return [pl.BlockSpec(memory_space=pltpu.VMEM)] * count


def iota(shape, axis):
    return lax.broadcasted_iota(jnp.int32, shape, axis)


def square_sums(rows):
    ones = jnp.ones((8, FW), F32)
    return lax.dot_general(
        ones,
        rows * rows,
        (((1,), (1,)), ((), ())),
        precision=lax.Precision.HIGHEST,
        preferred_element_type=F32,
    )


def as_columns(row):
    wide = jnp.broadcast_to(row[0:1, :], (128, 128)).T
    return jnp.concatenate([wide] * (FW // 128), axis=1)


def to_columns(stack):
    return stack.T


def attend_kernel(
    queries,
    new_keys,
    new_values,
    keys,
    values,
    lengths,
    order,
    out_proj,
    residual,
    gain,
    routes,
    send,
    hidden,
    picks,
    q_all,
    keys_v,
    values_v,
    proj_v,
    owners,
    scores,
    weights,
    page_q,
    page_w,
    val_out,
    val_in,
    stat_out,
    stat_in,
    attn,
    part,
    got,
    squares,
    l_sems,
    s1,
    r1,
    s2,
    r2,
    vs,
    vr,
    ts,
    tr,
    ps,
    pr,
    qs,
    qr,
):
    dp = lax.axis_index("dp")
    mp = lax.axis_index("mp")
    z, y = dp // 4, lax.rem(dp, 4)
    scale = HD ** (-0.5)
    dp_peers = [lax.rem(dp + k, NDP) for k in range(1, NDP)]
    mp_peers = [lax.rem(mp + k, 8) for k in range(1, 8)]
    loads = [
        pltpu.make_async_copy(keys, keys_v, l_sems.at[0]),
        pltpu.make_async_copy(values, values_v, l_sems.at[1]),
        pltpu.make_async_copy(out_proj, proj_v, l_sems.at[2]),
    ]
    q_rows = DEC // 2

    def q_half(owner, h):
        return q_all.at[pl.ds(pl.multiple_of(owner * DEC + h * q_rows, q_rows), q_rows), :]

    own_q = pltpu.make_async_copy(
        queries.at[pl.ds(0, DEC), :],
        q_all.at[pl.ds(pl.multiple_of(dp * DEC, DEC), DEC), :],
        l_sems.at[3],
    )
    own_q.start()
    loads[2].start()
    loads[0].start()
    loads[1].start()
    own_q.wait()
    greet([{"dp": p} for p in dp_peers] + [{"mp": p} for p in mp_peers])
    sent = []

    def go(copy):
        copy.start()
        sent.append(copy)

    def group(along, step, across):
        zz = lax.rem(z + (step if along == 0 else across) + 8, 4)
        yy = lax.rem(y + (across if along == 0 else step) + 8, 4)
        return zz * 4 + yy

    def first(h, k):
        return remote(q_half(dp, h), q_half(dp, h), s1.at[h, k - 1], r1.at[h, k - 1], {"dp": group(h, k, 0)})

    def second(h, j, k):
        owner = group(h, -j, 0)
        return remote(
            q_half(owner, h), q_half(owner, h), s2.at[h, j, k - 1], r2.at[h, j, k - 1], {"dp": group(h, 0, k)}
        )

    for k in (1, 3, 2):
        for h in range(2):
            go(first(h, k))
    for h in range(2):
        for k in range(1, 4):
            go(second(h, 0, k))

    lane = iota((128, 128), 1)
    row = iota((128, 128), 0)
    counts = lax.shift_right_logical(lengths[...] + (PAGE - 1), 4)
    upto = (row <= lane).astype(BF)
    within = jnp.dot(counts.astype(F32).astype(BF), upto, preferred_element_type=F32)
    place = jnp.zeros((128, 128), F32)
    ids = dp * 128 + row
    for q in range(16):
        place = place + jnp.where(order[q : q + 1, :] == ids, (lane + q * 128).astype(F32), 0.0)
    place = jnp.sum(place, axis=1, keepdims=True)
    before = jnp.zeros((1, 1), F32)
    passed = jnp.zeros((128, 128), F32)
    ends = []
    for i in range(8):
        ends.append(within[i : i + 1, :] + before)
        before = before + within[i : i + 1, 127:128]
        passed = passed + jnp.where(ends[i] <= place, 1.0, 0.0)
    owner = jnp.sum(passed, axis=1, keepdims=True)

    for k in range(1, 4):
        for h in range(2):
            remote(q_half(dp, h), q_half(group(h, -k, 0), h), s1.at[h, k - 1], r1.at[h, k - 1], {"dp": dp_peers[0]}).wait_recv()
            for kk in range(1, 4):
                go(second(h, k, kk))

    begin = jnp.zeros((128, 128), F32)
    length = jnp.zeros((128, 128), F32)
    for i in range(8):
        mine = (lane + i * 128).astype(F32) == owner
        cnt = counts[i : i + 1, :].astype(F32)
        begin = begin + jnp.where(mine, ends[i] - cnt, 0.0)
        length = length + jnp.where(mine, lengths[i : i + 1, :].astype(F32), 0.0)
        owners[:, i * 128 : (i + 1) * 128] = jnp.where(mine, 1.0, 0.0).astype(BF)
    begin = jnp.sum(begin, axis=1, keepdims=True)
    length = jnp.sum(length, axis=1, keepdims=True)
    valid = length - (place - begin) * PAGE
    key_ok = (lax.shift_right_logical(lane, 4) == (row & 7)) & ((lane & 15).astype(F32) < valid)
    owner_row = jnp.broadcast_to(owner, (128, 128)).T
    same = owner_row == owner
    leader = jnp.sum(jnp.where(same & (lane < row), 1.0, 0.0), axis=1, keepdims=True) == 0.0

    below = (lane < row).astype(BF)
    route = [routes[:, 0:1], routes[:, 1:2]]
    named = [(lane == r).astype(F32) for r in route]
    ahead = [jnp.dot(below, n.astype(BF), preferred_element_type=F32) for n in named]
    ahead[1] = ahead[1] + jnp.sum(named[0], axis=0, keepdims=True)
    cells = iota((128, E * C), 1)
    for k in range(2):
        slot = jnp.sum(named[k] * ahead[k], axis=1, keepdims=True).astype(jnp.int32)
        target = lax.shift_right_logical(slot, 4) * (E * SL) + route[k] * SL + (slot & (SL - 1))
        picks[k] = jnp.where(cells == target, 1.0, 0.0).astype(BF)

    causal = iota((PRE, PRE), 0) >= iota((PRE, PRE), 1)
    for g in range(4):
        cols = slice(g * HD, (g + 1) * HD)
        s = lax.dot_general(
            queries[DEC:, cols], new_keys[DEC:, :], (((1,), (1,)), ((), ())), preferred_element_type=F32
        )
        s = jnp.where(causal, s * scale, neg_big)
        w = jnp.where(causal, jnp.exp(s - jnp.max(s, axis=1, keepdims=True)), 0.0)
        den = jnp.sum(w, axis=1, keepdims=True)
        num = jnp.dot(w.astype(BF), new_values[DEC:, :], preferred_element_type=F32)
        attn[DEC:, cols] = (num / den).astype(BF)
    loads[2].wait()

    def project(t):
        rows = slice(t * 64, (t + 1) * 64)
        a = attn[rows, :]
        for k, p in enumerate(mp_peers):
            cols = pl.ds(pl.multiple_of(p * FW, FW), FW)
            part[t, k] = jnp.dot(a, proj_v[:, cols], preferred_element_type=F32).astype(BF)
            go(remote(part.at[t, k], got.at[t, k], ps.at[t, k], pr.at[t, k], {"mp": p}))
        cols = pl.ds(pl.multiple_of(mp * FW, FW), FW)
        own = jnp.dot(a, proj_v[:, cols], preferred_element_type=F32)
        hidden[rows, :] = own + residual[rows, :].astype(F32)

    def collect(t):
        rows = slice(t * 64, (t + 1) * 64)
        total = hidden[rows, :]
        for k in range(7):
            remote(part.at[t, k], got.at[t, k], ps.at[t, k], pr.at[t, k], {"mp": mp_peers[k]}).wait_recv()
            total = total + got[t, k].astype(F32)
        hidden[rows, :] = total

    project(1)

    own_cols = jnp.zeros((64, 128), F32)
    lane64 = iota((64, 128), 1)
    for g in range(4):
        prod = queries[:DEC, g * HD : (g + 1) * HD].astype(F32) * new_keys[:DEC, :].astype(F32)
        own_cols = jnp.where(lane64 == g, jnp.sum(prod, axis=1, keepdims=True) * scale, own_cols)
    own_score = to_columns(jnp.concatenate([own_cols, jnp.zeros((64, 128), F32)], axis=0))[0:8, :]

    for j in range(4):
        for k in range(1, 4):
            for h in range(2):
                remote(
                    q_half(dp, h), q_half(group(h, -j, -k), h), s2.at[h, j, k - 1], r2.at[h, j, k - 1], {"dp": dp_peers[0]}
                ).wait_recv()

    page_q[...] = jnp.dot(owners[...], q_all[...], preferred_element_type=F32)
    loads[0].wait()
    loads[1].wait()
    for k in range(16):
        qk = jnp.concatenate([page_q[8 * k : 8 * k + 8, g * HD : (g + 1) * HD] for g in range(4)], axis=0)
        s = lax.dot_general(
            qk.astype(BF), keys_v[128 * k : 128 * (k + 1), :], (((1,), (1,)), ((), ())), preferred_element_type=F32
        )
        for g in range(4):
            scores[g, 8 * k : 8 * k + 8, :] = s[8 * g : 8 * g + 8, :]
    tops = jnp.zeros((128, 128), F32)
    sums = []
    for g in range(4):
        s = jnp.where(key_ok, scores[g] * scale, neg_big)
        m = jnp.max(s, axis=1, keepdims=True)
        w = jnp.where(key_ok, jnp.exp(s - m), 0.0)
        weights[g] = w
        sums.append(jnp.sum(w, axis=1, keepdims=True))
        tops = jnp.where(lane == g, m, tops)
    for k in range(16):
        wk = jnp.concatenate([weights[g, 8 * k : 8 * k + 8, :] for g in range(4)], axis=0)
        v = jnp.dot(wk.astype(BF), values_v[128 * k : 128 * (k + 1), :], preferred_element_type=F32)
        for g in range(4):
            scores[g, 8 * k : 8 * k + 8, :] = v[8 * g : 8 * g + 8, :]
    top_rows = tops.T
    stat = jnp.zeros((128, 128), F32)
    for g in range(4):
        top = jnp.max(jnp.where(same, top_rows[g : g + 1, :], neg_big), axis=1, keepdims=True)
        factor = jnp.exp(tops[:, g : g + 1] - top)
        page_w[:, g * HD : (g + 1) * HD] = (scores[g] * factor).astype(BF)
        stat = jnp.where(lane == g, jnp.where(leader, top, 0.0), stat)
        stat = jnp.where(lane == 4 + g, sums[g] * factor, stat)
    stat8 = stat.T[0:8, :]
    for i in range(8):
        stat_out[i] = jnp.dot(
            stat8,
            owners[:, i * 128 : (i + 1) * 128].astype(F32),
            precision=lax.Precision.HIGHEST,
            preferred_element_type=F32,
        )
    for i in range(4):
        val_out[i * 256 : (i + 1) * 256, :] = lax.dot_general(
            owners[:, i * 256 : (i + 1) * 256], page_w[...], (((0,), (0,)), ((), ())), preferred_element_type=F32
        ).astype(BF)

    def val_rows(p):
        return val_out.at[pl.ds(pl.multiple_of(p * DEC, DEC), DEC), :]

    def swap_stat(k):
        p = dp_peers[k]
        return remote(stat_out.at[p // 2], stat_in.at[k], ts.at[k], tr.at[k], {"dp": p})

    def swap_val(k):
        p = dp_peers[k]
        return remote(val_rows(p), val_in.at[k], vs.at[k], vr.at[k], {"dp": p})

    for k in range(NDP - 1):
        go(swap_stat(k))
        go(swap_val(k))

    collect(1)
    for k in range(NDP - 1):
        swap_stat(k).wait_recv()
    stat_in[NDP - 1] = stat_out[dp // 2]
    odd = lax.rem(dp, 2) == 1
    got_stats = stat_in[...].reshape(128, 128)
    got_stats = jnp.where(odd, pltpu.roll(got_stats, 64, 1), got_stats).reshape(NDP, 8, 128)
    l_in = pltpu.roll(got_stats, 4, 1)
    m_in = jnp.where(l_in > 0.0, got_stats, neg_big)
    top = jnp.maximum(jnp.max(m_in, axis=0), own_score)
    f_in = jnp.where(l_in > 0.0, jnp.exp(jnp.minimum(m_in - top[None], 0.0)), 0.0)
    f_own = jnp.exp(own_score - top)
    inv = 1.0 / (jnp.sum(l_in * f_in, axis=0) + f_own)
    f_cols = to_columns((f_in * inv[None]).reshape(128, 128))
    own_f = to_columns(jnp.concatenate([f_own * inv, jnp.zeros((120, 128), F32)], axis=0))
    nums = [own_f[:DEC, g : g + 1] * new_values[:DEC, :].astype(F32) for g in range(4)]
    mine = val_out[pl.ds(pl.multiple_of(dp * DEC, DEC), DEC), :]
    for k in range(NDP):
        if k < NDP - 1:
            swap_val(k).wait_recv()
        v = (val_in[k] if k < NDP - 1 else mine).astype(F32)
        for g in range(4):
            nums[g] = nums[g] + v[:, g * HD : (g + 1) * HD] * f_cols[:DEC, 8 * k + g : 8 * k + g + 1]
    for g in range(4):
        attn[:DEC, g * HD : (g + 1) * HD] = nums[g].astype(BF)
    project(0)
    collect(0)

    squares[7] = square_sums(hidden[...])
    for k, p in enumerate(mp_peers):
        go(remote(squares.at[7], squares.at[k], qs.at[k], qr.at[k], {"mp": p}))
    summed = squares[7]
    for k, p in enumerate(mp_peers):
        remote(squares.at[7], squares.at[k], qs.at[k], qr.at[k], {"mp": p}).wait_recv()
        summed = summed + squares[k]
    normed = (hidden[...] * as_columns(lax.rsqrt(summed / D + eps_norm)) * gain[...]).astype(BF)
    dispatch = picks[0] + picks[1]
    for ch in range(NCH):
        rows = lax.dot_general(
            dispatch[:, ch * 128 : (ch + 1) * 128], normed, (((0,), (0,)), ((), ())), preferred_element_type=F32
        ).astype(BF)
        send[ch] = rows.reshape(E, SL, FW)
    for copy in sent:
        copy.wait_send()


def attend(queries, new_keys, new_values, keys, values, lengths, order, out_proj, residual, gain, routes, collective_id):
    anyspace = pl.BlockSpec(memory_space=pl.ANY)
    return pl.pallas_call(
        attend_kernel,
        out_shape=(
            jax.ShapeDtypeStruct((NCH, E, SL, FW), BF),
            jax.ShapeDtypeStruct((128, FW), F32),
            jax.ShapeDtypeStruct((2, 128, E * C), BF),
        ),
        in_specs=vmem(3) + [anyspace] * 2 + vmem(2) + [anyspace] + vmem(3),
        out_specs=tuple(vmem(3)),
        scratch_shapes=[
            pltpu.VMEM((NDP * DEC, FW), BF),
            pltpu.VMEM((2048, HD), BF),
            pltpu.VMEM((2048, HD), BF),
            pltpu.VMEM((FW, D), BF),
            pltpu.VMEM((128, NDP * DEC), BF),
            pltpu.VMEM((4, 128, 128), F32),
            pltpu.VMEM((4, 128, 128), F32),
            pltpu.VMEM((128, FW), F32),
            pltpu.VMEM((128, FW), BF),
            pltpu.VMEM((NDP * DEC, FW), BF),
            pltpu.VMEM((NDP - 1, DEC, FW), BF),
            pltpu.VMEM((8, 8, 128), F32),
            pltpu.VMEM((NDP, 8, 128), F32),
            pltpu.VMEM((128, FW), BF),
            pltpu.VMEM((2, 7, 64, FW), BF),
            pltpu.VMEM((2, 7, 64, FW), BF),
            pltpu.VMEM((8, 8, 128), F32),
            DMA((4,)),
            DMA((2, 3)),
            DMA((2, 3)),
            DMA((2, 4, 3)),
            DMA((2, 4, 3)),
            DMA((NDP - 1,)),
            DMA((NDP - 1,)),
            DMA((NDP - 1,)),
            DMA((NDP - 1,)),
            DMA((2, 7)),
            DMA((2, 7)),
            DMA((7,)),
            DMA((7,)),
        ],
        compiler_params=comm_params(collective_id),
        name="attend",
    )(queries, new_keys, new_values, keys, values, lengths, order, out_proj, residual, gain, routes)


def experts_kernel(
    send,
    wg,
    wu,
    wd,
    ret,
    x_all,
    wg_v,
    wu_v,
    wd_v,
    hid,
    part,
    own_part,
    hop_in,
    hop_out,
    fin,
    out,
    w_sems,
    wp_send,
    wp_recv,
    a_send,
    a_recv,
    a_own,
    g_send,
    g_recv,
    f_send,
    f_recv,
    p_send,
    p_recv,
    h_send,
    h_recv,
    t_send,
    t_recv,
    n_send,
    n_recv,
    r_send,
    r_recv,
    r_own,
):
    dp = lax.axis_index("dp")
    mp = lax.axis_index("mp")
    x, c = mp // 2, lax.rem(mp, 2)
    xr, xo, xl = lax.rem(x + 1, 4), lax.rem(x + 2, 4), lax.rem(x + 3, 4)
    mr, mo, ml = xr * 2 + c, xo * 2 + c, xl * 2 + c
    right, left, mate = {"mp": mr}, {"mp": ml}, {"mp": x * 2 + 1 - c}
    sides = (right, left)
    peers = [lax.rem(dp + k, NDP) for k in range(1, NDP)]
    half = RC // 2

    w_copies = [
        pltpu.make_async_copy(wg, wg_v, w_sems.at[0]),
        pltpu.make_async_copy(wu, wu_v, w_sems.at[1]),
    ]
    for j in range(4):
        w_copies.append(
            pltpu.make_async_copy(
                wd.at[:, pl.ds(pl.multiple_of(j * 1024 + c * FW, FW), FW)],
                wd_v.at[0, :, pl.ds(j * FW, FW)],
                w_sems.at[2 + j],
            )
        )
    greet([{"dp": p} for p in peers] + [right, left, mate])

    def columns(owner):
        return pl.ds(pl.multiple_of(owner * FW, FW), FW)

    sent = []

    def go(copy):
        copy.start()
        sent.append(copy)

    out_copies, own_copies = [], []
    for ch in range(NCH):
        rows = pl.ds(pl.multiple_of(dp * SL, SL), SL)
        own = pltpu.make_async_copy(send.at[ch, dp // 2], x_all.at[ch, rows, columns(mp)], a_own.at[ch])
        own.start()
        own_copies.append(own)
        cs = []
        for k, p in enumerate(peers):
            copy = remote(
                send.at[ch, p // 2],
                x_all.at[ch, rows, columns(mp)],
                a_send.at[ch, k],
                a_recv.at[ch, k],
                {"dp": p},
            )
            go(copy)
            cs.append(copy)
        out_copies.append(cs)
    for copy in w_copies:
        copy.start()
    mate_w = []
    for j in range(4):
        mate_w.append(
            remote(
                wd.at[:, pl.ds(pl.multiple_of(j * 1024 + (1 - c) * FW, FW), FW)],
                wd_v.at[1, :, pl.ds(j * FW, FW)],
                wp_send.at[j],
                wp_recv.at[j],
                mate,
            )
        )
        go(mate_w[j])

    def block(ch, h, owner):
        return x_all.at[ch, pl.ds(h * half, half), columns(owner)]

    def whole(ch, owner):
        return x_all.at[ch, :, columns(owner)]

    def neighbour(ch, side, h):
        return remote(block(ch, h, mp), block(ch, h, mp), g_send.at[ch, side, h], g_recv.at[ch, side, h], sides[side])

    def onward(ch, side):
        owner = (ml, mr)[side]
        return remote(
            block(ch, side, owner), block(ch, side, owner), f_send.at[ch, side], f_recv.at[ch, side], sides[side]
        )

    def to_mate(ch, which):
        owner = (mp, ml, mr, mo)[which]
        return remote(whole(ch, owner), whole(ch, owner), p_send.at[ch, which], p_recv.at[ch, which], mate)

    def spread_own(ch):
        for copy in out_copies[ch]:
            copy.wait_recv()
        own_copies[ch].wait()
        for h in range(2):
            go(neighbour(ch, 0, h))
            go(neighbour(ch, 1, 1 - h))
        go(to_mate(ch, 0))

    def spread_on(ch):
        for side in range(2):
            neighbour(ch, side, side).wait_recv()
            go(onward(ch, side))

    def spread_rest(ch):
        for side in range(2):
            neighbour(ch, side, 1 - side).wait_recv()
            go(to_mate(ch, 1 + side))

    def spread_far(ch):
        for side in range(2):
            onward(ch, side).wait_recv()
        go(to_mate(ch, 3))

    def spread_end(ch):
        for which in range(4):
            to_mate(ch, which).wait_recv()

    def hidden_send(ch):
        return remote(hid.at[ch, 0], hid.at[ch, 1], h_send.at[ch], h_recv.at[ch], mate)

    def gate_up(ch, n):
        cols = pl.ds(n * 256, 256)
        rows = x_all[ch]
        g = jnp.dot(rows, wg_v[:, cols], preferred_element_type=F32)
        u = jnp.dot(rows, wu_v[:, cols], preferred_element_type=F32)
        hid[ch, 0, :, cols] = (g / (1.0 + jnp.exp(-g)) * u).astype(BF)

    def down(ch, owner):
        cols = columns(owner)
        return jnp.dot(hid[ch, 0], wd_v[0, :, cols], preferred_element_type=F32) + jnp.dot(
            hid[ch, 1], wd_v[1, :, cols], preferred_element_type=F32
        )

    def rows_of(h):
        return pl.ds(h * half, half)

    def hop(ch, side):
        return remote(
            part.at[ch, 0, rows_of(side)], hop_in.at[ch, side], t_send.at[ch, side], t_recv.at[ch, side], sides[side]
        )

    def near(ch, side, h, src):
        return remote(src, fin.at[ch, side, rows_of(h)], n_send.at[ch, side, h], n_recv.at[ch, side, h], sides[side])

    def reduce_start(ch):
        part[ch, 0] = down(ch, xo).astype(BF)
        for side in range(2):
            go(hop(ch, side))
        for side in range(2):
            part[ch, 1 + side] = down(ch, (xr, xl)[side]).astype(BF)
            go(near(ch, side, 1 - side, part.at[ch, 1 + side, rows_of(1 - side)]))

    def reduce_own(ch):
        own_part[ch] = down(ch, x)

    def reduce_hop(ch):
        for side in range(2):
            hop(ch, side).wait_recv()
            hop_out[ch, side] = (
                part[ch, 1 + side, rows_of(side), :].astype(F32) + hop_in[ch, side].astype(F32)
            ).astype(BF)
            go(near(ch, side, side, hop_out.at[ch, side]))

    ret_copies = []

    def reduce_end(ch):
        for side in range(2):
            for h in range(2):
                near(ch, side, h, hop_out.at[ch, side]).wait_recv()
        total = own_part[ch] + fin[ch, 0].astype(F32) + fin[ch, 1].astype(F32)
        out[ch] = total.astype(BF)
        own = pltpu.make_async_copy(
            out.at[ch, pl.ds(pl.multiple_of(dp * SL, SL), SL)], ret.at[ch, dp], r_own.at[ch]
        )
        own.start()
        cs = [own]
        for k, p in enumerate(peers):
            copy = remote(
                out.at[ch, pl.ds(pl.multiple_of(p * SL, SL), SL)],
                ret.at[ch, dp],
                r_send.at[ch, k],
                r_recv.at[ch, k],
                {"dp": p},
            )
            copy.start()
            cs.append(copy)
        ret_copies.extend(cs)

    spread_own(0)
    spread_on(0)
    spread_own(1)
    spread_rest(0)
    spread_far(0)
    for copy in w_copies[:2]:
        copy.wait()
    spread_on(1)
    spread_own(2)
    spread_end(0)
    for ch in range(NCH):
        gate_up(ch, 0)
        if ch == 0:
            spread_rest(1)
        if ch == 1:
            reduce_hop(0)
        if ch == 2:
            reduce_hop(1)
        gate_up(ch, 1)
        if ch == 0:
            spread_far(1)
        if ch == 1:
            spread_rest(2)
        gate_up(ch, 2)
        go(hidden_send(ch))
        if ch == 0:
            spread_on(2)
            for copy in w_copies[2:]:
                copy.wait()
            for copy in mate_w:
                copy.wait_recv()
        if ch == 1:
            spread_far(2)
            reduce_end(0)
        if ch == 2:
            reduce_end(1)
        hidden_send(ch).wait_recv()
        reduce_start(ch)
        reduce_own(ch)
        if ch < 2:
            spread_end(ch + 1)
    reduce_hop(2)
    reduce_end(2)
    for copy in ret_copies:
        copy.wait()
    for copy in sent:
        copy.wait_send()


def experts(send, wg, wu, wd, collective_id):
    anyspace = pl.BlockSpec(memory_space=pl.ANY)
    return pl.pallas_call(
        experts_kernel,
        out_shape=jax.ShapeDtypeStruct((NCH, NDP, SL, FW), BF),
        in_specs=vmem(1) + [anyspace] * 3,
        out_specs=vmem(1)[0],
        scratch_shapes=[
            pltpu.VMEM((NCH, RC, D), BF),
            pltpu.VMEM((D, HID), BF),
            pltpu.VMEM((D, HID), BF),
            pltpu.VMEM((2, HID, D // 2), BF),
            pltpu.VMEM((NCH, 2, RC, HID), BF),
            pltpu.VMEM((NCH, 3, RC, FW), BF),
            pltpu.VMEM((NCH, RC, FW), F32),
            pltpu.VMEM((NCH, 2, RC // 2, FW), BF),
            pltpu.VMEM((NCH, 2, RC // 2, FW), BF),
            pltpu.VMEM((NCH, 2, RC, FW), BF),
            pltpu.VMEM((NCH, RC, FW), BF),
            DMA((6,)),
            DMA((4,)),
            DMA((4,)),
            DMA((NCH, NDP - 1)),
            DMA((NCH, NDP - 1)),
            DMA((NCH,)),
            DMA((NCH, 2, 2)),
            DMA((NCH, 2, 2)),
            DMA((NCH, 2)),
            DMA((NCH, 2)),
            DMA((NCH, 4)),
            DMA((NCH, 4)),
            DMA((NCH,)),
            DMA((NCH,)),
            DMA((NCH, 2)),
            DMA((NCH, 2)),
            DMA((NCH, 2, 2)),
            DMA((NCH, 2, 2)),
            DMA((NCH, NDP - 1)),
            DMA((NCH, NDP - 1)),
            DMA((NCH,)),
        ],
        compiler_params=comm_params(collective_id),
        name="experts",
    )(send, wg, wu, wd)


def closing_kernel(ret, picks, weight, hidden, gain, out, squares, send, recv):
    me = lax.axis_index("mp")
    peers = [lax.rem(me + k, 8) for k in range(1, 8)]
    greet([{"mp": p} for p in peers])
    mixed = hidden[...]
    for k in range(2):
        rows = jnp.zeros((128, FW), F32)
        for j in range(2):
            back = ret[:, j].reshape(E * C, FW)
            rows = rows + jnp.dot(picks[k], back, preferred_element_type=F32)
        mixed = mixed + weight[:, k : k + 1] * rows
    squares[7] = square_sums(mixed)
    copies = []
    for k, p in enumerate(peers):
        copies.append(remote(squares.at[7], squares.at[k], send.at[k], recv.at[k], {"mp": p}))
        copies[-1].start()
    summed = squares[7]
    for k, copy in enumerate(copies):
        copy.wait_recv()
        summed = summed + squares[k]
    out[...] = (mixed * as_columns(lax.rsqrt(summed / D + eps_norm)) * gain[...]).astype(BF)
    for copy in copies:
        copy.wait_send()


def closing_norm(ret, picks, weight, hidden, gain, collective_id):
    return pl.pallas_call(
        closing_kernel,
        out_shape=jax.ShapeDtypeStruct((128, FW), BF),
        in_specs=vmem(5),
        out_specs=vmem(1)[0],
        scratch_shapes=[pltpu.VMEM((8, 8, 128), F32), DMA((7,)), DMA((7,))],
        compiler_params=comm_params(collective_id),
        name="closing_norm",
    )(ret, picks, weight, hidden, gain)


def local(
    residual,
    queries,
    new_keys,
    new_values,
    cache_keys,
    cache_values,
    cache_len,
    page_order,
    out_proj,
    attn_gain,
    routes,
    route_weight,
    gate_proj,
    up_proj,
    down_proj,
    final_gain,
):
    column_start = lax.axis_index("mp") * FW
    gain_cols = lax.dynamic_slice_in_dim(attn_gain, column_start, FW, 0)
    send, hidden, picks = attend(
        queries,
        new_keys,
        new_values,
        cache_keys.reshape(-1, HD),
        cache_values.reshape(-1, HD),
        cache_len.reshape(8, 128),
        page_order.reshape(16, 128),
        out_proj,
        residual,
        gain_cols[None, :],
        routes,
        0,
    )
    returned = experts(send, gate_proj, up_proj, down_proj, 1)
    return closing_norm(
        returned.reshape(NCH * E, 2, SL, FW), picks, route_weight, hidden, final_gain[None, :], 2
    )


def solution(mesh):
    return jax.shard_map(
        local,
        mesh=mesh,
        in_specs=(
            P("dp", "mp"),
            P("dp", "mp"),
            P("dp", "mp"),
            P("dp", "mp"),
            P("dp", None, "mp"),
            P("dp", None, "mp"),
            P(),
            P(),
            P("mp", None),
            P(),
            P("dp", None),
            P("dp", None),
            P(None, ("dp", "mp")),
            P(None, ("dp", "mp")),
            P(("dp", "mp"), None),
            P("mp"),
        ),
        out_specs=P("dp", "mp"),
        check_vma=False,
    )
```

```python
import functools

import jax
import jax.numpy as jnp
from jax import lax
from jax.experimental import pallas as pl
from jax.experimental.pallas import tpu as pltpu
from jax.sharding import PartitionSpec as P

D = 4096
HQ = 32
KVH = 8
HD = 128
E = 8
PAGE = 16
DEC = 64
PRE = 64
C = 48
NDP = 16
NCH = 3
NA = 2
NB = 2
SL = C // NCH
RC = NDP * SL
FW = 512
HID = 768

MESH = pl.DeviceIdType.MESH
DMA = pltpu.SemaphoreType.DMA
BF = jnp.bfloat16
F32 = jnp.float32

neg_big = -1e30
eps_norm = 1e-05


def remote(src, dst, send_sem, recv_sem, device):
    return pltpu.make_async_remote_copy(
        src_ref=src,
        dst_ref=dst,
        send_sem=send_sem,
        recv_sem=recv_sem,
        device_id=device,
        device_id_type=MESH,
    )


def greet(devices):
    barrier = pltpu.get_barrier_semaphore()
    for device in devices:
        pl.semaphore_signal(barrier, inc=1, device_id=device, device_id_type=MESH)
    pl.semaphore_wait(barrier, len(devices))


def comm_params(collective_id):
    return pltpu.CompilerParams(
        collective_id=collective_id, has_side_effects=True, vmem_limit_bytes=60 << 20
    )


def vmem(count):
    return [pl.BlockSpec(memory_space=pltpu.VMEM)] * count


def iota(shape, axis):
    return lax.broadcasted_iota(jnp.int32, shape, axis)


def square_sums(rows):
    ones = jnp.ones((8, FW), F32)
    return lax.dot_general(
        ones,
        rows * rows,
        (((1,), (1,)), ((), ())),
        precision=lax.Precision.HIGHEST,
        preferred_element_type=F32,
    )


def as_columns(row):
    wide = jnp.broadcast_to(row[0:1, :], (128, 128)).T
    return jnp.concatenate([wide] * (FW // 128), axis=1)


def to_columns(stack):
    return stack.T


def attend_kernel(
    queries,
    new_keys,
    new_values,
    keys,
    values,
    lengths,
    order,
    out_proj,
    residual,
    gain,
    routes,
    send,
    normed_out,
    hidden,
    picks,
    q_all,
    keys_v,
    values_v,
    proj_v,
    owners,
    scores,
    weights,
    page_q,
    page_w,
    val_out,
    val_in,
    stat_out,
    stat_in,
    attn,
    part,
    got,
    squares,
    l_sems,
    s1,
    r1,
    s2,
    r2,
    vs,
    vr,
    ts,
    tr,
    ps,
    pr,
    qs,
    qr,
):
    dp = lax.axis_index("dp")
    mp = lax.axis_index("mp")
    z, y = dp // 4, lax.rem(dp, 4)
    scale = HD ** (-0.5)
    dp_peers = [lax.rem(dp + k, NDP) for k in range(1, NDP)]
    mp_peers = [lax.rem(mp + k, 8) for k in range(1, 8)]
    loads = [
        pltpu.make_async_copy(keys, keys_v, l_sems.at[0]),
        pltpu.make_async_copy(values, values_v, l_sems.at[1]),
        pltpu.make_async_copy(out_proj, proj_v, l_sems.at[2]),
    ]
    q_rows = DEC // 2

    def q_half(owner, h):
        return q_all.at[pl.ds(pl.multiple_of(owner * DEC + h * q_rows, q_rows), q_rows), :]

    own_q = pltpu.make_async_copy(
        queries.at[pl.ds(0, DEC), :],
        q_all.at[pl.ds(pl.multiple_of(dp * DEC, DEC), DEC), :],
        l_sems.at[3],
    )
    own_q.start()
    loads[2].start()
    loads[0].start()
    loads[1].start()
    own_q.wait()
    greet([{"dp": p} for p in dp_peers] + [{"mp": p} for p in mp_peers])
    sent = []

    def go(copy):
        copy.start()
        sent.append(copy)

    def group(along, step, across):
        zz = lax.rem(z + (step if along == 0 else across) + 8, 4)
        yy = lax.rem(y + (across if along == 0 else step) + 8, 4)
        return zz * 4 + yy

    def first(h, k):
        return remote(q_half(dp, h), q_half(dp, h), s1.at[h, k - 1], r1.at[h, k - 1], {"dp": group(h, k, 0)})

    def second(h, j, k):
        owner = group(h, -j, 0)
        return remote(
            q_half(owner, h), q_half(owner, h), s2.at[h, j, k - 1], r2.at[h, j, k - 1], {"dp": group(h, 0, k)}
        )

    for k in (1, 3, 2):
        for h in range(2):
            go(first(h, k))
    for h in range(2):
        for k in range(1, 4):
            go(second(h, 0, k))

    lane = iota((128, 128), 1)
    row = iota((128, 128), 0)
    counts = lax.shift_right_logical(lengths[...] + (PAGE - 1), 4)
    upto = (row <= lane).astype(BF)
    within = jnp.dot(counts.astype(F32).astype(BF), upto, preferred_element_type=F32)
    place = jnp.zeros((128, 128), F32)
    ids = dp * 128 + row
    for q in range(16):
        place = place + jnp.where(order[q : q + 1, :] == ids, (lane + q * 128).astype(F32), 0.0)
    place = jnp.sum(place, axis=1, keepdims=True)
    before = jnp.zeros((1, 1), F32)
    passed = jnp.zeros((128, 128), F32)
    ends = []
    for i in range(8):
        ends.append(within[i : i + 1, :] + before)
        before = before + within[i : i + 1, 127:128]
        passed = passed + jnp.where(ends[i] <= place, 1.0, 0.0)
    owner = jnp.sum(passed, axis=1, keepdims=True)

    for k in range(1, 4):
        for h in range(2):
            remote(q_half(dp, h), q_half(group(h, -k, 0), h), s1.at[h, k - 1], r1.at[h, k - 1], {"dp": dp_peers[0]}).wait_recv()
            for kk in range(1, 4):
                go(second(h, k, kk))

    begin = jnp.zeros((128, 128), F32)
    length = jnp.zeros((128, 128), F32)
    for i in range(8):
        mine = (lane + i * 128).astype(F32) == owner
        cnt = counts[i : i + 1, :].astype(F32)
        begin = begin + jnp.where(mine, ends[i] - cnt, 0.0)
        length = length + jnp.where(mine, lengths[i : i + 1, :].astype(F32), 0.0)
        owners[:, i * 128 : (i + 1) * 128] = jnp.where(mine, 1.0, 0.0).astype(BF)
    begin = jnp.sum(begin, axis=1, keepdims=True)
    length = jnp.sum(length, axis=1, keepdims=True)
    valid = length - (place - begin) * PAGE
    key_ok = (lax.shift_right_logical(lane, 4) == (row & 7)) & ((lane & 15).astype(F32) < valid)
    owner_row = jnp.broadcast_to(owner, (128, 128)).T
    same = owner_row == owner
    leader = jnp.sum(jnp.where(same & (lane < row), 1.0, 0.0), axis=1, keepdims=True) == 0.0

    below = (lane < row).astype(BF)
    route = [
        jnp.broadcast_to(routes[k : k + 1, :].astype(F32), (128, 128)).T[:, 0:1].astype(jnp.int32) for k in range(2)
    ]
    named = [(lane == r).astype(F32) for r in route]
    ahead = [jnp.dot(below, n.astype(BF), preferred_element_type=F32) for n in named]
    ahead[1] = ahead[1] + jnp.sum(named[0], axis=0, keepdims=True)
    cells = iota((128, E * C), 1)
    for k in range(2):
        slot = jnp.sum(named[k] * ahead[k], axis=1, keepdims=True).astype(jnp.int32)
        target = lax.shift_right_logical(slot, 4) * (E * SL) + route[k] * SL + (slot & (SL - 1))
        picks[k] = jnp.where(cells == target, 1.0, 0.0).astype(BF)

    causal = iota((PRE, PRE), 0) >= iota((PRE, PRE), 1)
    for g in range(4):
        cols = slice(g * HD, (g + 1) * HD)
        s = lax.dot_general(
            queries[DEC:, cols], new_keys[DEC:, :], (((1,), (1,)), ((), ())), preferred_element_type=F32
        )
        s = jnp.where(causal, s * scale, neg_big)
        w = jnp.where(causal, jnp.exp(s - jnp.max(s, axis=1, keepdims=True)), 0.0)
        den = jnp.sum(w, axis=1, keepdims=True)
        num = jnp.dot(w.astype(BF), new_values[DEC:, :], preferred_element_type=F32)
        attn[DEC:, cols] = (num / den).astype(BF)
    loads[2].wait()

    def project(t):
        rows = slice(t * 64, (t + 1) * 64)
        a = attn[rows, :]
        for k, p in enumerate(mp_peers):
            cols = pl.ds(pl.multiple_of(p * FW, FW), FW)
            part[t, k] = jnp.dot(a, proj_v[:, cols], preferred_element_type=F32).astype(BF)
            go(remote(part.at[t, k], got.at[t, k], ps.at[t, k], pr.at[t, k], {"mp": p}))
        cols = pl.ds(pl.multiple_of(mp * FW, FW), FW)
        own = jnp.dot(a, proj_v[:, cols], preferred_element_type=F32)
        hidden[rows, :] = own + residual[rows, :].astype(F32)

    def collect(t):
        rows = slice(t * 64, (t + 1) * 64)
        total = hidden[rows, :]
        for k in range(7):
            remote(part.at[t, k], got.at[t, k], ps.at[t, k], pr.at[t, k], {"mp": mp_peers[k]}).wait_recv()
            total = total + got[t, k].astype(F32)
        hidden[rows, :] = total

    project(1)

    own_cols = jnp.zeros((64, 128), F32)
    lane64 = iota((64, 128), 1)
    for g in range(4):
        prod = queries[:DEC, g * HD : (g + 1) * HD].astype(F32) * new_keys[:DEC, :].astype(F32)
        own_cols = jnp.where(lane64 == g, jnp.sum(prod, axis=1, keepdims=True) * scale, own_cols)
    own_score = to_columns(jnp.concatenate([own_cols, jnp.zeros((64, 128), F32)], axis=0))[0:8, :]

    for j in range(4):
        for k in range(1, 4):
            for h in range(2):
                remote(
                    q_half(dp, h), q_half(group(h, -j, -k), h), s2.at[h, j, k - 1], r2.at[h, j, k - 1], {"dp": dp_peers[0]}
                ).wait_recv()

    page_q[...] = jnp.dot(owners[...], q_all[...], preferred_element_type=F32)
    loads[0].wait()
    loads[1].wait()
    for k in range(16):
        qk = jnp.concatenate([page_q[8 * k : 8 * k + 8, g * HD : (g + 1) * HD] for g in range(4)], axis=0)
        s = lax.dot_general(
            qk.astype(BF), keys_v[128 * k : 128 * (k + 1), :], (((1,), (1,)), ((), ())), preferred_element_type=F32
        )
        for g in range(4):
            scores[g, 8 * k : 8 * k + 8, :] = s[8 * g : 8 * g + 8, :]
    tops = jnp.zeros((128, 128), F32)
    sums = []
    for g in range(4):
        s = jnp.where(key_ok, scores[g] * scale, neg_big)
        m = jnp.max(s, axis=1, keepdims=True)
        w = jnp.where(key_ok, jnp.exp(s - m), 0.0)
        weights[g] = w
        sums.append(jnp.sum(w, axis=1, keepdims=True))
        tops = jnp.where(lane == g, m, tops)
    for k in range(16):
        wk = jnp.concatenate([weights[g, 8 * k : 8 * k + 8, :] for g in range(4)], axis=0)
        v = jnp.dot(wk.astype(BF), values_v[128 * k : 128 * (k + 1), :], preferred_element_type=F32)
        for g in range(4):
            scores[g, 8 * k : 8 * k + 8, :] = v[8 * g : 8 * g + 8, :]
    top_rows = tops.T
    stat = jnp.zeros((128, 128), F32)
    for g in range(4):
        top = jnp.max(jnp.where(same, top_rows[g : g + 1, :], neg_big), axis=1, keepdims=True)
        factor = jnp.exp(tops[:, g : g + 1] - top)
        page_w[:, g * HD : (g + 1) * HD] = (scores[g] * factor).astype(BF)
        stat = jnp.where(lane == g, jnp.where(leader, top, 0.0), stat)
        stat = jnp.where(lane == 4 + g, sums[g] * factor, stat)
    stat8 = stat.T[0:8, :]
    for i in range(8):
        stat_out[i] = jnp.dot(
            stat8,
            owners[:, i * 128 : (i + 1) * 128].astype(F32),
            precision=lax.Precision.HIGHEST,
            preferred_element_type=F32,
        )
    for i in range(4):
        val_out[i * 256 : (i + 1) * 256, :] = lax.dot_general(
            owners[:, i * 256 : (i + 1) * 256], page_w[...], (((0,), (0,)), ((), ())), preferred_element_type=F32
        ).astype(BF)

    def val_rows(p):
        return val_out.at[pl.ds(pl.multiple_of(p * DEC, DEC), DEC), :]

    def swap_stat(k):
        p = dp_peers[k]
        return remote(stat_out.at[p // 2], stat_in.at[k], ts.at[k], tr.at[k], {"dp": p})

    def swap_val(k):
        p = dp_peers[k]
        return remote(val_rows(p), val_in.at[k], vs.at[k], vr.at[k], {"dp": p})

    for k in range(NDP - 1):
        go(swap_stat(k))
        go(swap_val(k))

    collect(1)
    for k in range(NDP - 1):
        swap_stat(k).wait_recv()
    stat_in[NDP - 1] = stat_out[dp // 2]
    odd = lax.rem(dp, 2) == 1
    got_stats = stat_in[...].reshape(128, 128)
    got_stats = jnp.where(odd, pltpu.roll(got_stats, 64, 1), got_stats).reshape(NDP, 8, 128)
    l_in = pltpu.roll(got_stats, 4, 1)
    m_in = jnp.where(l_in > 0.0, got_stats, neg_big)
    top = jnp.maximum(jnp.max(m_in, axis=0), own_score)
    f_in = jnp.where(l_in > 0.0, jnp.exp(jnp.minimum(m_in - top[None], 0.0)), 0.0)
    f_own = jnp.exp(own_score - top)
    inv = 1.0 / (jnp.sum(l_in * f_in, axis=0) + f_own)
    f_cols = to_columns((f_in * inv[None]).reshape(128, 128))
    own_f = to_columns(jnp.concatenate([f_own * inv, jnp.zeros((120, 128), F32)], axis=0))
    nums = [own_f[:DEC, g : g + 1] * new_values[:DEC, :].astype(F32) for g in range(4)]
    mine = val_out[pl.ds(pl.multiple_of(dp * DEC, DEC), DEC), :]
    for k in range(NDP):
        if k < NDP - 1:
            swap_val(k).wait_recv()
        v = (val_in[k] if k < NDP - 1 else mine).astype(F32)
        for g in range(4):
            nums[g] = nums[g] + v[:, g * HD : (g + 1) * HD] * f_cols[:DEC, 8 * k + g : 8 * k + g + 1]
    for g in range(4):
        attn[:DEC, g * HD : (g + 1) * HD] = nums[g].astype(BF)
    project(0)
    collect(0)

    squares[7] = square_sums(hidden[...])
    for k, p in enumerate(mp_peers):
        go(remote(squares.at[7], squares.at[k], qs.at[k], qr.at[k], {"mp": p}))
    summed = squares[7]
    for k, p in enumerate(mp_peers):
        remote(squares.at[7], squares.at[k], qs.at[k], qr.at[k], {"mp": p}).wait_recv()
        summed = summed + squares[k]
    gain_rows = gain[pl.ds(mp * 4, 4), :]
    gain_cols = jnp.concatenate([gain_rows[i : i + 1, :] for i in range(4)], axis=1)
    normed = (hidden[...] * as_columns(lax.rsqrt(summed / D + eps_norm)) * gain_cols).astype(BF)
    normed_out[...] = normed
    dispatch = picks[0] + picks[1]
    for ch in range(NA):
        rows = lax.dot_general(
            dispatch[:, ch * 128 : (ch + 1) * 128], normed, (((0,), (0,)), ((), ())), preferred_element_type=F32
        ).astype(BF)
        send[ch] = rows.reshape(E, SL, FW)
    for copy in sent:
        copy.wait_send()


def attend(queries, new_keys, new_values, keys, values, lengths, order, out_proj, residual, gain, routes, collective_id):
    anyspace = pl.BlockSpec(memory_space=pl.ANY)
    return pl.pallas_call(
        attend_kernel,
        out_shape=(
            jax.ShapeDtypeStruct((NA, E, SL, FW), BF),
            jax.ShapeDtypeStruct((128, FW), BF),
            jax.ShapeDtypeStruct((128, FW), F32),
            jax.ShapeDtypeStruct((2, 128, E * C), BF),
        ),
        in_specs=vmem(3) + [anyspace] * 2 + vmem(2) + [anyspace] + vmem(3),
        out_specs=tuple(vmem(4)),
        scratch_shapes=[
            pltpu.VMEM((NDP * DEC, FW), BF),
            pltpu.VMEM((2048, HD), BF),
            pltpu.VMEM((2048, HD), BF),
            pltpu.VMEM((FW, D), BF),
            pltpu.VMEM((128, NDP * DEC), BF),
            pltpu.VMEM((4, 128, 128), F32),
            pltpu.VMEM((4, 128, 128), F32),
            pltpu.VMEM((128, FW), F32),
            pltpu.VMEM((128, FW), BF),
            pltpu.VMEM((NDP * DEC, FW), BF),
            pltpu.VMEM((NDP - 1, DEC, FW), BF),
            pltpu.VMEM((8, 8, 128), F32),
            pltpu.VMEM((NDP, 8, 128), F32),
            pltpu.VMEM((128, FW), BF),
            pltpu.VMEM((2, 7, 64, FW), BF),
            pltpu.VMEM((2, 7, 64, FW), BF),
            pltpu.VMEM((8, 8, 128), F32),
            DMA((4,)),
            DMA((2, 3)),
            DMA((2, 3)),
            DMA((2, 4, 3)),
            DMA((2, 4, 3)),
            DMA((NDP - 1,)),
            DMA((NDP - 1,)),
            DMA((NDP - 1,)),
            DMA((NDP - 1,)),
            DMA((2, 7)),
            DMA((2, 7)),
            DMA((7,)),
            DMA((7,)),
        ],
        compiler_params=comm_params(collective_id),
        name="attend",
    )(queries, new_keys, new_values, keys, values, lengths, order, out_proj, residual, gain, routes)


def experts_kernel(
    send,
    normed,
    picks,
    weight,
    hidden,
    gain,
    wg,
    wu,
    wd,
    result,
    x_all,
    wg_v,
    wu_v,
    wd_v,
    hid,
    part,
    own_part,
    hop_in,
    hop_out,
    fin,
    out,
    ret,
    tokens,
    send_b,
    part_b,
    ret_b,
    moe_out,
    moe_in,
    moe_own,
    squares,
    w_sems,
    wp_send,
    wp_recv,
    a_send,
    a_recv,
    a_own,
    g_send,
    g_recv,
    f_send,
    f_recv,
    p_send,
    p_recv,
    h_send,
    h_recv,
    t_send,
    t_recv,
    n_send,
    n_recv,
    r_send,
    r_recv,
    r_own,
    k_send,
    k_recv,
    m_send,
    m_recv,
    q_send,
    q_recv,
):
    dp = lax.axis_index("dp")
    mp = lax.axis_index("mp")
    x, c = mp // 2, lax.rem(mp, 2)
    xr, xo, xl = lax.rem(x + 1, 4), lax.rem(x + 2, 4), lax.rem(x + 3, 4)
    mr, mo, ml = xr * 2 + c, xo * 2 + c, xl * 2 + c
    right, left, mate = {"mp": mr}, {"mp": ml}, {"mp": x * 2 + 1 - c}
    sides = (right, left)
    peers = [lax.rem(dp + k, NDP) for k in range(1, NDP)]
    mp_peers = [lax.rem(mp + k, 8) for k in range(1, 8)]
    x_peers = [{"mp": lax.rem(x + k, 4) * 2 + c} for k in range(1, 4)]
    half = RC // 2

    def wide(owner):
        return pl.ds(pl.multiple_of((lax.rem(owner, 2) * 4 + owner // 2) * FW, FW), FW)

    def columns(owner):
        return pl.ds(pl.multiple_of(owner * FW, FW), FW)

    dp_rows = pl.ds(pl.multiple_of(dp * SL, SL), SL)
    c_cols = pl.ds(pl.multiple_of(c * 4 * FW, 4 * FW), 4 * FW)
    mate_cols = pl.ds(pl.multiple_of((1 - c) * 4 * FW, 4 * FW), 4 * FW)

    w_copies = []
    for w, (src, dst) in enumerate(((wg, wg_v), (wu, wu_v))):
        for core in range(2):
            for chip in range(4):
                w_copies.append(
                    pltpu.make_async_copy(
                        src.at[pl.ds((chip * 2 + core) * FW, FW), :],
                        dst.at[pl.ds((core * 4 + chip) * FW, FW), :],
                        w_sems.at[w * 8 + core * 4 + chip],
                    )
                )
    for j in range(4):
        w_copies.append(
            pltpu.make_async_copy(
                wd.at[:, pl.ds(pl.multiple_of(j * 1024 + c * FW, FW), FW)],
                wd_v.at[0, :, pl.ds(j * FW, FW)],
                w_sems.at[16 + j],
            )
        )
    own_tokens = pltpu.make_async_copy(normed, tokens.at[x], a_own.at[3])
    own_tokens.start()
    greet([{"dp": p} for p in peers] + [{"mp": p} for p in mp_peers])

    sent = []

    def go(copy):
        copy.start()
        sent.append(copy)

    def token_copy(k):
        return remote(normed, tokens.at[x], k_send.at[k], k_recv.at[k], x_peers[k])

    for k in (0, 2, 1):
        go(token_copy(k))

    out_copies, own_copies = [], []
    for ch in range(NA):
        own = pltpu.make_async_copy(send.at[ch, dp // 2], x_all.at[ch, dp_rows, wide(mp)], a_own.at[ch])
        own.start()
        own_copies.append(own)
        cs = []
        for k, p in enumerate(peers):
            copy = remote(
                send.at[ch, p // 2], x_all.at[ch, dp_rows, wide(mp)], a_send.at[ch, k], a_recv.at[ch, k], {"dp": p}
            )
            go(copy)
            cs.append(copy)
        out_copies.append(cs)
    for copy in w_copies:
        copy.start()
    mate_w = []
    for j in range(4):
        mate_w.append(
            remote(
                wd.at[:, pl.ds(pl.multiple_of(j * 1024 + (1 - c) * FW, FW), FW)],
                wd_v.at[1, :, pl.ds(j * FW, FW)],
                wp_send.at[j],
                wp_recv.at[j],
                mate,
            )
        )

    def block(ch, h, owner):
        return x_all.at[ch, pl.ds(h * half, half), wide(owner)]

    def whole(ch, owner):
        return x_all.at[ch, :, wide(owner)]

    def neighbour(ch, side, h):
        return remote(block(ch, h, mp), block(ch, h, mp), g_send.at[ch, side, h], g_recv.at[ch, side, h], sides[side])

    def onward(ch, side):
        owner = (ml, mr)[side]
        return remote(
            block(ch, side, owner), block(ch, side, owner), f_send.at[ch, side], f_recv.at[ch, side], sides[side]
        )

    def to_mate(ch, which):
        owner = (mp, ml, mr, mo)[which]
        return remote(whole(ch, owner), whole(ch, owner), p_send.at[ch, which], p_recv.at[ch, which], mate)

    def spread_own(ch):
        for copy in out_copies[ch]:
            copy.wait_recv()
        own_copies[ch].wait()
        for h in range(2):
            go(neighbour(ch, 0, h))
            go(neighbour(ch, 1, 1 - h))
        go(to_mate(ch, 0))

    def spread_on(ch):
        for side in range(2):
            neighbour(ch, side, side).wait_recv()
            go(onward(ch, side))

    def spread_rest(ch):
        for side in range(2):
            neighbour(ch, side, 1 - side).wait_recv()
            go(to_mate(ch, 1 + side))

    def spread_far(ch):
        for side in range(2):
            onward(ch, side).wait_recv()
        go(to_mate(ch, 3))

    def spread_end(ch):
        for which in range(4):
            to_mate(ch, which).wait_recv()

    def whole_copy(k):
        p = peers[k]
        return remote(send_b.at[p // 2], x_all.at[2, dp_rows, c_cols], a_send.at[2, k], a_recv.at[2, k], {"dp": p})

    def whole_own():
        return pltpu.make_async_copy(send_b.at[dp // 2], x_all.at[2, dp_rows, c_cols], a_own.at[2])

    def whole_mate():
        return remote(x_all.at[2, :, c_cols], x_all.at[2, :, c_cols], p_send.at[2, 0], p_recv.at[2, 0], mate)

    def whole_start():
        own_tokens.wait()
        for k in range(3):
            token_copy(k).wait_recv()
        dispatch = picks[0, :, NA * 128 :] + picks[1, :, NA * 128 :]
        for chip in range(4):
            rows = lax.dot_general(
                dispatch, tokens[chip], (((0,), (0,)), ((), ())), preferred_element_type=F32
            ).astype(BF)
            send_b[:, :, chip * FW : (chip + 1) * FW] = rows.reshape(E, SL, FW)
        whole_own().start()
        for k in range(NDP - 1):
            go(whole_copy(k))

    def whole_spread():
        for k in range(NDP - 1):
            whole_copy(k).wait_recv()
        whole_own().wait()
        go(whole_mate())

    def hidden_send(ch):
        return remote(hid.at[ch, 0], hid.at[ch, 1], h_send.at[ch], h_recv.at[ch], mate)

    def gate_up(ch, n):
        cols = pl.ds(n * 256, 256)
        rows = x_all[ch]
        g = jnp.dot(rows, wg_v[:, cols], preferred_element_type=F32)
        u = jnp.dot(rows, wu_v[:, cols], preferred_element_type=F32)
        hid[ch, 0, :, cols] = (g / (1.0 + jnp.exp(-g)) * u).astype(BF)

    def down(ch, chip):
        cols = columns(chip)
        return jnp.dot(hid[ch, 0], wd_v[0, :, cols], preferred_element_type=F32) + jnp.dot(
            hid[ch, 1], wd_v[1, :, cols], preferred_element_type=F32
        )

    def rows_of(h):
        return pl.ds(h * half, half)

    def hop(ch, side):
        return remote(
            part.at[ch, 0, rows_of(side)], hop_in.at[ch, side], t_send.at[ch, side], t_recv.at[ch, side], sides[side]
        )

    def near(ch, side, h, src):
        return remote(src, fin.at[ch, side, rows_of(h)], n_send.at[ch, side, h], n_recv.at[ch, side, h], sides[side])

    def reduce_start(ch):
        part[ch, 0] = down(ch, xo).astype(BF)
        for side in range(2):
            go(hop(ch, side))
        for side in range(2):
            part[ch, 1 + side] = down(ch, (xr, xl)[side]).astype(BF)
            go(near(ch, side, 1 - side, part.at[ch, 1 + side, rows_of(1 - side)]))

    def reduce_own(ch):
        own_part[ch] = down(ch, x)

    def reduce_hop(ch):
        for side in range(2):
            hop(ch, side).wait_recv()
            hop_out[ch, side] = (
                part[ch, 1 + side, rows_of(side), :].astype(F32) + hop_in[ch, side].astype(F32)
            ).astype(BF)
            go(near(ch, side, side, hop_out.at[ch, side]))

    e_of, j_of = dp // 2, lax.rem(dp, 2)

    def back_copy(ch, k):
        p = peers[k]
        rows = pl.ds(pl.multiple_of(p * SL, SL), SL)
        return remote(out.at[ch, rows], ret.at[ch, e_of, j_of], r_send.at[ch, k], r_recv.at[ch, k], {"dp": p})

    def back_own(ch):
        return pltpu.make_async_copy(out.at[ch, dp_rows], ret.at[ch, e_of, j_of], r_own.at[ch])

    def reduce_end(ch):
        for side in range(2):
            for h in range(2):
                near(ch, side, h, hop_out.at[ch, side]).wait_recv()
        total = own_part[ch] + fin[ch, 0].astype(F32) + fin[ch, 1].astype(F32)
        out[ch] = total.astype(BF)
        back_own(ch).start()
        for k in range(NDP - 1):
            go(back_copy(ch, k))

    def open_copy(k):
        p = peers[k]
        rows = pl.ds(pl.multiple_of(p * SL, SL), SL)
        return remote(part_b.at[rows], ret_b.at[e_of, j_of], r_send.at[2, k], r_recv.at[2, k], {"dp": p})

    def open_own():
        return pltpu.make_async_copy(part_b.at[dp_rows], ret_b.at[e_of, j_of], r_own.at[2])

    def open_start():
        for chip in range(4):
            part_b[:, chip * FW : (chip + 1) * FW] = down(2, chip).astype(BF)
        open_own().start()
        for k in range(NDP - 1):
            go(open_copy(k))

    def shares(k):
        wide_w = jnp.broadcast_to(weight[k : k + 1, :], (128, 128)).T
        return jnp.concatenate([wide_w] * (FW // 128), axis=1)

    def moe_copy(k):
        return remote(moe_out.at[k], moe_in.at[k], m_send.at[k], m_recv.at[k], x_peers[k])

    def open_end():
        for k in range(NDP - 1):
            open_copy(k).wait_recv()
        open_own().wait()
        w = [shares(k) for k in range(2)]

        def mix(chip):
            both = [ret_b[:, j, :, columns(chip)].reshape(128, FW) for j in range(2)]
            total = jnp.zeros((128, FW), F32)
            for k in range(2):
                pick = picks[k, :, NA * 128 :]
                rows = jnp.dot(pick, both[0], preferred_element_type=F32)
                rows = rows + jnp.dot(pick, both[1], preferred_element_type=F32)
                total = total + w[k] * rows
            return total

        for k in (1, 0, 2):
            moe_out[k] = mix(lax.rem(x + 1 + k, 4)).astype(BF)
            go(moe_copy(k))
        moe_own[...] = mix(x) + hidden[...]

    def combine(ch):
        for k in range(NDP - 1):
            back_copy(ch, k).wait_recv()
        back_own(ch).wait()
        total = moe_own[...]
        for k in range(2):
            pick = picks[k, :, ch * 128 : (ch + 1) * 128]
            rows = jnp.dot(pick, ret[ch, :, 0].reshape(128, FW), preferred_element_type=F32)
            rows = rows + jnp.dot(pick, ret[ch, :, 1].reshape(128, FW), preferred_element_type=F32)
            total = total + shares(k) * rows
        moe_own[...] = total

    spread_own(0)
    for copy in mate_w:
        go(copy)
    whole_start()
    spread_on(0)
    spread_own(1)
    spread_rest(0)
    spread_far(0)
    for copy in w_copies[:16]:
        copy.wait()
    spread_end(0)

    gate_up(0, 0)
    spread_on(1)
    gate_up(0, 1)
    whole_spread()
    gate_up(0, 2)
    go(hidden_send(0))
    spread_rest(1)
    for copy in w_copies[16:]:
        copy.wait()
    for copy in mate_w:
        copy.wait_recv()
    hidden_send(0).wait_recv()
    reduce_start(0)
    reduce_own(0)
    spread_far(1)
    whole_mate().wait_recv()

    gate_up(2, 0)
    gate_up(2, 1)
    reduce_hop(0)
    gate_up(2, 2)
    go(hidden_send(2))
    spread_end(1)
    gate_up(1, 0)
    hidden_send(2).wait_recv()
    open_start()
    gate_up(1, 1)
    reduce_end(0)
    gate_up(1, 2)
    go(hidden_send(1))
    hidden_send(1).wait_recv()
    reduce_start(1)
    reduce_own(1)
    reduce_hop(1)
    open_end()
    combine(0)
    reduce_end(1)
    total = moe_own[...]
    for k in range(3):
        moe_copy(k).wait_recv()
        total = total + moe_in[k].astype(F32)
    moe_own[...] = total
    combine(1)

    mixed = moe_own[...]
    squares[7] = square_sums(mixed)

    def square_copy(k):
        return remote(squares.at[7], squares.at[k], q_send.at[k], q_recv.at[k], {"mp": mp_peers[k]})

    for k in range(7):
        go(square_copy(k))
    summed = squares[7]
    for k in range(7):
        square_copy(k).wait_recv()
        summed = summed + squares[k]
    result[...] = (mixed * as_columns(lax.rsqrt(summed / D + eps_norm)) * gain[...]).astype(BF)
    for copy in sent:
        copy.wait_send()


def experts(send, normed, picks, weight, hidden, gain, wg, wu, wd, collective_id):
    anyspace = pl.BlockSpec(memory_space=pl.ANY)
    return pl.pallas_call(
        experts_kernel,
        out_shape=jax.ShapeDtypeStruct((128, FW), BF),
        in_specs=vmem(6) + [anyspace] * 3,
        out_specs=vmem(1)[0],
        scratch_shapes=[
            pltpu.VMEM((NCH, RC, D), BF),
            pltpu.VMEM((D, HID), BF),
            pltpu.VMEM((D, HID), BF),
            pltpu.VMEM((2, HID, D // 2), BF),
            pltpu.VMEM((NCH, 2, RC, HID), BF),
            pltpu.VMEM((NA, 3, RC, FW), BF),
            pltpu.VMEM((NA, RC, FW), F32),
            pltpu.VMEM((NA, 2, RC // 2, FW), BF),
            pltpu.VMEM((NA, 2, RC // 2, FW), BF),
            pltpu.VMEM((NA, 2, RC, FW), BF),
            pltpu.VMEM((NA, RC, FW), BF),
            pltpu.VMEM((NA, E, 2, SL, FW), BF),
            pltpu.VMEM((4, 128, FW), BF),
            pltpu.VMEM((E, SL, 4 * FW), BF),
            pltpu.VMEM((RC, 4 * FW), BF),
            pltpu.VMEM((E, 2, SL, 4 * FW), BF),
            pltpu.VMEM((3, 128, FW), BF),
            pltpu.VMEM((3, 128, FW), BF),
            pltpu.VMEM((128, FW), F32),
            pltpu.VMEM((8, 8, 128), F32),
            DMA((20,)),
            DMA((4,)),
            DMA((4,)),
            DMA((NCH, NDP - 1)),
            DMA((NCH, NDP - 1)),
            DMA((4,)),
            DMA((NA, 2, 2)),
            DMA((NA, 2, 2)),
            DMA((NA, 2)),
            DMA((NA, 2)),
            DMA((NCH, 4)),
            DMA((NCH, 4)),
            DMA((NCH,)),
            DMA((NCH,)),
            DMA((NA, 2)),
            DMA((NA, 2)),
            DMA((NA, 2, 2)),
            DMA((NA, 2, 2)),
            DMA((NCH, NDP - 1)),
            DMA((NCH, NDP - 1)),
            DMA((NCH,)),
            DMA((3,)),
            DMA((3,)),
            DMA((3,)),
            DMA((3,)),
            DMA((7,)),
            DMA((7,)),
        ],
        compiler_params=comm_params(collective_id),
        name="experts",
    )(send, normed, picks, weight, hidden, gain, wg, wu, wd)


def local(
    residual,
    queries,
    new_keys,
    new_values,
    cache_keys,
    cache_values,
    cache_len,
    page_order,
    out_proj,
    attn_gain,
    routes,
    route_weight,
    gate_proj,
    up_proj,
    down_proj,
    final_gain,
):
    send, normed, hidden, picks = attend(
        queries,
        new_keys,
        new_values,
        cache_keys.reshape(-1, HD),
        cache_values.reshape(-1, HD),
        cache_len.reshape(8, 128),
        page_order.reshape(16, 128),
        out_proj,
        residual,
        attn_gain.reshape(32, 128),
        routes.T,
        0,
    )
    return experts(
        send,
        normed,
        picks,
        route_weight.T,
        hidden,
        final_gain[None, :],
        gate_proj,
        up_proj,
        down_proj,
        1,
    )


def solution(mesh):
    return jax.shard_map(
        local,
        mesh=mesh,
        in_specs=(
            P("dp", "mp"),
            P("dp", "mp"),
            P("dp", "mp"),
            P("dp", "mp"),
            P("dp", None, "mp"),
            P("dp", None, "mp"),
            P(),
            P(),
            P("mp", None),
            P(),
            P("dp", None),
            P("dp", None),
            P(None, ("dp", "mp")),
            P(None, ("dp", "mp")),
            P(("dp", "mp"), None),
            P("mp"),
        ),
        out_specs=P("dp", "mp"),
        check_vma=False,
    )
```

```python
import functools

import jax
import jax.numpy as jnp
from jax import lax
from jax.experimental import pallas as pl
from jax.experimental.pallas import tpu as pltpu
from jax.sharding import PartitionSpec as P

D = 4096
HQ = 32
KVH = 8
HD = 128
E = 8
PAGE = 16
DEC = 64
PRE = 64
C = 48
NDP = 16
NCH = 3
NA = 2
NB = 2
SL = C // NCH
RC = NDP * SL
FW = 512
HID = 768

MESH = pl.DeviceIdType.MESH
DMA = pltpu.SemaphoreType.DMA
BF = jnp.bfloat16
F32 = jnp.float32

neg_big = -1e30
eps_norm = 1e-05


def remote(src, dst, send_sem, recv_sem, device):
    return pltpu.make_async_remote_copy(
        src_ref=src,
        dst_ref=dst,
        send_sem=send_sem,
        recv_sem=recv_sem,
        device_id=device,
        device_id_type=MESH,
    )


def greet(devices):
    barrier = pltpu.get_barrier_semaphore()
    for device in devices:
        pl.semaphore_signal(barrier, inc=1, device_id=device, device_id_type=MESH)
    pl.semaphore_wait(barrier, len(devices))


def comm_params(collective_id):
    return pltpu.CompilerParams(
        collective_id=collective_id, has_side_effects=True, vmem_limit_bytes=60 << 20
    )


def iota(shape, axis):
    return lax.broadcasted_iota(jnp.int32, shape, axis)


def square_sums(rows):
    ones = jnp.ones((8, FW), F32)
    return lax.dot_general(
        ones,
        rows * rows,
        (((1,), (1,)), ((), ())),
        precision=lax.Precision.HIGHEST,
        preferred_element_type=F32,
    )


def as_columns(row):
    wide = jnp.broadcast_to(row[0:1, :], (128, 128)).T
    return jnp.concatenate([wide] * (FW // 128), axis=1)


def to_columns(stack):
    return stack.T


def layer_kernel(
    queries,
    new_keys,
    new_values,
    keys,
    values,
    lengths,
    order,
    out_proj,
    residual,
    attn_gain,
    routes,
    weight,
    final_gain,
    wg,
    wu,
    wd,
    result,
    q_all,
    keys_v,
    values_v,
    proj_v,
    owners,
    scores,
    weights,
    page_q,
    page_w,
    val_out,
    val_in,
    stat_out,
    stat_in,
    attn,
    proj_part,
    got,
    squares,
    hidden,
    picks,
    send,
    x_all,
    wg_v,
    wu_v,
    wd_v,
    hid,
    part,
    own_part,
    hop_in,
    hop_out,
    fin,
    out,
    ret,
    tokens,
    send_b,
    part_b,
    ret_b,
    moe_out,
    moe_in,
    moe_own,
    l_sems,
    s1,
    r1,
    s2,
    r2,
    vs,
    vr,
    ts,
    tr,
    ps,
    pr,
    w_sems,
    a_own,
    r_own,
    wp_send,
    wp_recv,
    a_send,
    a_recv,
    g_send,
    g_recv,
    f_send,
    f_recv,
    p_send,
    p_recv,
    h_send,
    h_recv,
    t_send,
    t_recv,
    n_send,
    n_recv,
    r_send,
    r_recv,
    k_send,
    k_recv,
    m_send,
    m_recv,
    q_send,
    q_recv,
):
    dp = lax.axis_index("dp")
    mp = lax.axis_index("mp")
    z, y = dp // 4, lax.rem(dp, 4)
    scale = HD ** (-0.5)
    peers = [lax.rem(dp + k, NDP) for k in range(1, NDP)]
    mp_peers = [lax.rem(mp + k, 8) for k in range(1, 8)]
    x, c = mp // 2, lax.rem(mp, 2)
    xr, xo, xl = lax.rem(x + 1, 4), lax.rem(x + 2, 4), lax.rem(x + 3, 4)
    mr, mo, ml = xr * 2 + c, xo * 2 + c, xl * 2 + c
    right, left, mate = {"mp": mr}, {"mp": ml}, {"mp": x * 2 + 1 - c}
    sides = (right, left)
    x_peers = [{"mp": lax.rem(x + k, 4) * 2 + c} for k in range(1, 4)]
    half = RC // 2

    def wide(owner):
        return pl.ds(pl.multiple_of((lax.rem(owner, 2) * 4 + owner // 2) * FW, FW), FW)

    def columns(owner):
        return pl.ds(pl.multiple_of(owner * FW, FW), FW)

    dp_rows = pl.ds(pl.multiple_of(dp * SL, SL), SL)
    c_cols = pl.ds(pl.multiple_of(c * 4 * FW, 4 * FW), 4 * FW)
    mate_cols = pl.ds(pl.multiple_of((1 - c) * 4 * FW, 4 * FW), 4 * FW)

    w_copies = []
    for w, (src, dst) in enumerate(((wg, wg_v), (wu, wu_v))):
        for core in range(2):
            for chip in range(4):
                w_copies.append(
                    pltpu.make_async_copy(
                        src.at[pl.ds((chip * 2 + core) * FW, FW), :],
                        dst.at[pl.ds((core * 4 + chip) * FW, FW), :],
                        w_sems.at[w * 8 + core * 4 + chip],
                    )
                )
    for j in range(4):
        w_copies.append(
            pltpu.make_async_copy(
                wd.at[:, pl.ds(pl.multiple_of(j * 1024 + c * FW, FW), FW)],
                wd_v.at[0, :, pl.ds(j * FW, FW)],
                w_sems.at[16 + j],
            )
        )
    loads = [
        pltpu.make_async_copy(keys, keys_v, l_sems.at[0]),
        pltpu.make_async_copy(values, values_v, l_sems.at[1]),
        pltpu.make_async_copy(out_proj, proj_v, l_sems.at[2]),
    ]
    q_rows = DEC // 2

    def q_half(owner, h):
        return q_all.at[pl.ds(pl.multiple_of(owner * DEC + h * q_rows, q_rows), q_rows), :]

    own_q = pltpu.make_async_copy(
        queries.at[pl.ds(0, DEC), :],
        q_all.at[pl.ds(pl.multiple_of(dp * DEC, DEC), DEC), :],
        l_sems.at[3],
    )
    own_q.start()
    loads[2].start()
    loads[0].start()
    loads[1].start()
    own_q.wait()
    for copy in w_copies:
        copy.start()
    greet([{"dp": p} for p in peers] + [{"mp": p} for p in mp_peers])
    sent = []

    def go(copy):
        copy.start()
        sent.append(copy)

    def group(along, step, across):
        zz = lax.rem(z + (step if along == 0 else across) + 8, 4)
        yy = lax.rem(y + (across if along == 0 else step) + 8, 4)
        return zz * 4 + yy

    def first(h, k):
        return remote(q_half(dp, h), q_half(dp, h), s1.at[h, k - 1], r1.at[h, k - 1], {"dp": group(h, k, 0)})

    def second(h, j, k):
        owner = group(h, -j, 0)
        return remote(
            q_half(owner, h), q_half(owner, h), s2.at[h, j, k - 1], r2.at[h, j, k - 1], {"dp": group(h, 0, k)}
        )

    for k in (1, 3, 2):
        for h in range(2):
            go(first(h, k))
    for h in range(2):
        for k in range(1, 4):
            go(second(h, 0, k))
    mate_w = []
    for j in range(4):
        mate_w.append(
            remote(
                wd.at[:, pl.ds(pl.multiple_of(j * 1024 + (1 - c) * FW, FW), FW)],
                wd_v.at[1, :, pl.ds(j * FW, FW)],
                wp_send.at[j],
                wp_recv.at[j],
                mate,
            )
        )
        go(mate_w[j])

    lane = iota((128, 128), 1)
    row = iota((128, 128), 0)
    counts = lax.shift_right_logical(lengths[...] + (PAGE - 1), 4)
    upto = (row <= lane).astype(BF)
    within = jnp.dot(counts.astype(F32).astype(BF), upto, preferred_element_type=F32)
    place = jnp.zeros((128, 128), F32)
    ids = dp * 128 + row
    for q in range(16):
        place = place + jnp.where(order[q : q + 1, :] == ids, (lane + q * 128).astype(F32), 0.0)
    place = jnp.sum(place, axis=1, keepdims=True)
    before = jnp.zeros((1, 1), F32)
    passed = jnp.zeros((128, 128), F32)
    ends = []
    for i in range(8):
        ends.append(within[i : i + 1, :] + before)
        before = before + within[i : i + 1, 127:128]
        passed = passed + jnp.where(ends[i] <= place, 1.0, 0.0)
    owner = jnp.sum(passed, axis=1, keepdims=True)

    for k in range(1, 4):
        for h in range(2):
            remote(q_half(dp, h), q_half(group(h, -k, 0), h), s1.at[h, k - 1], r1.at[h, k - 1], {"dp": peers[0]}).wait_recv()
            for kk in range(1, 4):
                go(second(h, k, kk))

    begin = jnp.zeros((128, 128), F32)
    length = jnp.zeros((128, 128), F32)
    for i in range(8):
        mine = (lane + i * 128).astype(F32) == owner
        cnt = counts[i : i + 1, :].astype(F32)
        begin = begin + jnp.where(mine, ends[i] - cnt, 0.0)
        length = length + jnp.where(mine, lengths[i : i + 1, :].astype(F32), 0.0)
        owners[:, i * 128 : (i + 1) * 128] = jnp.where(mine, 1.0, 0.0).astype(BF)
    begin = jnp.sum(begin, axis=1, keepdims=True)
    length = jnp.sum(length, axis=1, keepdims=True)
    valid = length - (place - begin) * PAGE
    key_ok = (lax.shift_right_logical(lane, 4) == (row & 7)) & ((lane & 15).astype(F32) < valid)
    owner_row = jnp.broadcast_to(owner, (128, 128)).T
    same = owner_row == owner
    leader = jnp.sum(jnp.where(same & (lane < row), 1.0, 0.0), axis=1, keepdims=True) == 0.0

    below = (lane < row).astype(BF)
    route = [
        jnp.broadcast_to(routes[k : k + 1, :].astype(F32), (128, 128)).T[:, 0:1].astype(jnp.int32) for k in range(2)
    ]
    named = [(lane == r).astype(F32) for r in route]
    ahead = [jnp.dot(below, n.astype(BF), preferred_element_type=F32) for n in named]
    ahead[1] = ahead[1] + jnp.sum(named[0], axis=0, keepdims=True)
    cells = iota((128, E * C), 1)
    for k in range(2):
        slot = jnp.sum(named[k] * ahead[k], axis=1, keepdims=True).astype(jnp.int32)
        target = lax.shift_right_logical(slot, 4) * (E * SL) + route[k] * SL + (slot & (SL - 1))
        picks[k] = jnp.where(cells == target, 1.0, 0.0).astype(BF)

    causal = iota((PRE, PRE), 0) >= iota((PRE, PRE), 1)
    for g in range(4):
        cols = slice(g * HD, (g + 1) * HD)
        s = lax.dot_general(
            queries[DEC:, cols], new_keys[DEC:, :], (((1,), (1,)), ((), ())), preferred_element_type=F32
        )
        s = jnp.where(causal, s * scale, neg_big)
        w = jnp.where(causal, jnp.exp(s - jnp.max(s, axis=1, keepdims=True)), 0.0)
        den = jnp.sum(w, axis=1, keepdims=True)
        num = jnp.dot(w.astype(BF), new_values[DEC:, :], preferred_element_type=F32)
        attn[DEC:, cols] = (num / den).astype(BF)
    loads[2].wait()

    def project(t):
        rows = slice(t * 64, (t + 1) * 64)
        a = attn[rows, :]
        for k, p in enumerate(mp_peers):
            cols = pl.ds(pl.multiple_of(p * FW, FW), FW)
            proj_part[t, k] = jnp.dot(a, proj_v[:, cols], preferred_element_type=F32).astype(BF)
            go(remote(proj_part.at[t, k], got.at[t, k], ps.at[t, k], pr.at[t, k], {"mp": p}))
        cols = pl.ds(pl.multiple_of(mp * FW, FW), FW)
        own = jnp.dot(a, proj_v[:, cols], preferred_element_type=F32)
        hidden[rows, :] = own + residual[rows, :].astype(F32)

    def collect(t):
        rows = slice(t * 64, (t + 1) * 64)
        total = hidden[rows, :]
        for k in range(7):
            remote(proj_part.at[t, k], got.at[t, k], ps.at[t, k], pr.at[t, k], {"mp": mp_peers[k]}).wait_recv()
            total = total + got[t, k].astype(F32)
        hidden[rows, :] = total

    project(1)

    own_cols = jnp.zeros((64, 128), F32)
    lane64 = iota((64, 128), 1)
    for g in range(4):
        prod = queries[:DEC, g * HD : (g + 1) * HD].astype(F32) * new_keys[:DEC, :].astype(F32)
        own_cols = jnp.where(lane64 == g, jnp.sum(prod, axis=1, keepdims=True) * scale, own_cols)
    own_score = to_columns(jnp.concatenate([own_cols, jnp.zeros((64, 128), F32)], axis=0))[0:8, :]

    for j in range(4):
        for k in range(1, 4):
            for h in range(2):
                remote(
                    q_half(dp, h), q_half(group(h, -j, -k), h), s2.at[h, j, k - 1], r2.at[h, j, k - 1], {"dp": peers[0]}
                ).wait_recv()

    page_q[...] = jnp.dot(owners[...], q_all[...], preferred_element_type=F32)
    loads[0].wait()
    loads[1].wait()
    for k in range(16):
        qk = jnp.concatenate([page_q[8 * k : 8 * k + 8, g * HD : (g + 1) * HD] for g in range(4)], axis=0)
        s = lax.dot_general(
            qk.astype(BF), keys_v[128 * k : 128 * (k + 1), :], (((1,), (1,)), ((), ())), preferred_element_type=F32
        )
        for g in range(4):
            scores[g, 8 * k : 8 * k + 8, :] = s[8 * g : 8 * g + 8, :]
    tops = jnp.zeros((128, 128), F32)
    sums = []
    for g in range(4):
        s = jnp.where(key_ok, scores[g] * scale, neg_big)
        m = jnp.max(s, axis=1, keepdims=True)
        w = jnp.where(key_ok, jnp.exp(s - m), 0.0)
        weights[g] = w
        sums.append(jnp.sum(w, axis=1, keepdims=True))
        tops = jnp.where(lane == g, m, tops)
    for k in range(16):
        wk = jnp.concatenate([weights[g, 8 * k : 8 * k + 8, :] for g in range(4)], axis=0)
        v = jnp.dot(wk.astype(BF), values_v[128 * k : 128 * (k + 1), :], preferred_element_type=F32)
        for g in range(4):
            scores[g, 8 * k : 8 * k + 8, :] = v[8 * g : 8 * g + 8, :]
    top_rows = tops.T
    stat = jnp.zeros((128, 128), F32)
    for g in range(4):
        top = jnp.max(jnp.where(same, top_rows[g : g + 1, :], neg_big), axis=1, keepdims=True)
        factor = jnp.exp(tops[:, g : g + 1] - top)
        page_w[:, g * HD : (g + 1) * HD] = (scores[g] * factor).astype(BF)
        stat = jnp.where(lane == g, jnp.where(leader, top, 0.0), stat)
        stat = jnp.where(lane == 4 + g, sums[g] * factor, stat)
    stat8 = stat.T[0:8, :]
    for i in range(8):
        stat_out[i] = jnp.dot(
            stat8,
            owners[:, i * 128 : (i + 1) * 128].astype(F32),
            precision=lax.Precision.HIGHEST,
            preferred_element_type=F32,
        )
    for i in range(4):
        val_out[i * 256 : (i + 1) * 256, :] = lax.dot_general(
            owners[:, i * 256 : (i + 1) * 256], page_w[...], (((0,), (0,)), ((), ())), preferred_element_type=F32
        ).astype(BF)

    def val_rows(p):
        return val_out.at[pl.ds(pl.multiple_of(p * DEC, DEC), DEC), :]

    def swap_stat(k):
        p = peers[k]
        return remote(stat_out.at[p // 2], stat_in.at[k], ts.at[k], tr.at[k], {"dp": p})

    def swap_val(k):
        p = peers[k]
        return remote(val_rows(p), val_in.at[k], vs.at[k], vr.at[k], {"dp": p})

    for k in range(NDP - 1):
        go(swap_stat(k))
        go(swap_val(k))

    def square_copy(t, k):
        return remote(squares.at[t, 7], squares.at[t, k], q_send.at[t, k], q_recv.at[t, k], {"mp": mp_peers[k]})

    def row_scales(t, rows):
        squares[t, 7] = square_sums(rows)
        for k in range(7):
            go(square_copy(t, k))
        summed = squares[t, 7]
        for k in range(7):
            square_copy(t, k).wait_recv()
            summed = summed + squares[t, k]
        return as_columns(lax.rsqrt(summed / D + eps_norm))

    def token_copy(t, k):
        rows = tokens.at[x, pl.ds(t * 64, 64), :]
        return remote(rows, rows, k_send.at[t, k], k_recv.at[t, k], x_peers[k])

    gain_rows = attn_gain[pl.ds(mp * 4, 4), :]
    gain_cols = jnp.concatenate([gain_rows[i : i + 1, :] for i in range(4)], axis=1)
    nothing = jnp.zeros((64, FW), F32)

    def finish(t):
        mine = hidden[t * 64 : (t + 1) * 64, :]
        scales = row_scales(t, jnp.concatenate([nothing, mine] if t else [mine, nothing], axis=0))
        scales = scales[t * 64 : (t + 1) * 64, :]
        tokens[x, t * 64 : (t + 1) * 64, :] = (mine * scales * gain_cols).astype(BF)
        for k in (0, 2, 1):
            go(token_copy(t, k))

    collect(1)
    finish(1)
    for k in range(NDP - 1):
        swap_stat(k).wait_recv()
    stat_in[NDP - 1] = stat_out[dp // 2]
    odd = lax.rem(dp, 2) == 1
    got_stats = stat_in[...].reshape(128, 128)
    got_stats = jnp.where(odd, pltpu.roll(got_stats, 64, 1), got_stats).reshape(NDP, 8, 128)
    l_in = pltpu.roll(got_stats, 4, 1)
    m_in = jnp.where(l_in > 0.0, got_stats, neg_big)
    top = jnp.maximum(jnp.max(m_in, axis=0), own_score)
    f_in = jnp.where(l_in > 0.0, jnp.exp(jnp.minimum(m_in - top[None], 0.0)), 0.0)
    f_own = jnp.exp(own_score - top)
    inv = 1.0 / (jnp.sum(l_in * f_in, axis=0) + f_own)
    f_cols = to_columns((f_in * inv[None]).reshape(128, 128))
    own_f = to_columns(jnp.concatenate([f_own * inv, jnp.zeros((120, 128), F32)], axis=0))
    nums = [own_f[:DEC, g : g + 1] * new_values[:DEC, :].astype(F32) for g in range(4)]
    mine = val_out[pl.ds(pl.multiple_of(dp * DEC, DEC), DEC), :]
    for k in range(NDP):
        if k < NDP - 1:
            swap_val(k).wait_recv()
        v = (val_in[k] if k < NDP - 1 else mine).astype(F32)
        for g in range(4):
            nums[g] = nums[g] + v[:, g * HD : (g + 1) * HD] * f_cols[:DEC, 8 * k + g : 8 * k + g + 1]
    for g in range(4):
        attn[:DEC, g * HD : (g + 1) * HD] = nums[g].astype(BF)
    project(0)
    collect(0)

    finish(0)

    def block(ch, h, owner):
        return x_all.at[ch, pl.ds(h * half, half), wide(owner)]

    def whole(ch, owner):
        return x_all.at[ch, :, wide(owner)]

    def neighbour(ch, side, h):
        return remote(block(ch, h, mp), block(ch, h, mp), g_send.at[ch, side, h], g_recv.at[ch, side, h], sides[side])

    def onward(ch, side):
        owner = (ml, mr)[side]
        return remote(
            block(ch, side, owner), block(ch, side, owner), f_send.at[ch, side], f_recv.at[ch, side], sides[side]
        )

    def to_mate(ch, which):
        owner = (mp, ml, mr, mo)[which]
        return remote(whole(ch, owner), whole(ch, owner), p_send.at[ch, which], p_recv.at[ch, which], mate)

    def slice_copy(ch, k):
        p = peers[k]
        return remote(
            send.at[ch, p // 2], x_all.at[ch, dp_rows, wide(mp)], a_send.at[ch, k], a_recv.at[ch, k], {"dp": p}
        )

    def slice_own(ch):
        return pltpu.make_async_copy(send.at[ch, dp // 2], x_all.at[ch, dp_rows, wide(mp)], a_own.at[ch])

    def spread_own(ch):
        for k in range(NDP - 1):
            slice_copy(ch, k).wait_recv()
        slice_own(ch).wait()
        for h in range(2):
            go(neighbour(ch, 0, h))
            go(neighbour(ch, 1, 1 - h))
        go(to_mate(ch, 0))

    def spread_on(ch):
        for side in range(2):
            neighbour(ch, side, side).wait_recv()
            go(onward(ch, side))

    def spread_rest(ch):
        for side in range(2):
            neighbour(ch, side, 1 - side).wait_recv()
            go(to_mate(ch, 1 + side))

    def spread_far(ch):
        for side in range(2):
            onward(ch, side).wait_recv()
        go(to_mate(ch, 3))

    def spread_end(ch):
        for which in range(4):
            to_mate(ch, which).wait_recv()

    def whole_copy(k):
        p = peers[k]
        return remote(send_b.at[p // 2], x_all.at[2, dp_rows, c_cols], a_send.at[2, k], a_recv.at[2, k], {"dp": p})

    def whole_own():
        return pltpu.make_async_copy(send_b.at[dp // 2], x_all.at[2, dp_rows, c_cols], a_own.at[2])

    def whole_mate():
        return remote(x_all.at[2, :, c_cols], x_all.at[2, :, c_cols], p_send.at[2, 0], p_recv.at[2, 0], mate)

    def whole_start():
        for t in range(2):
            for k in range(3):
                token_copy(t, k).wait_recv()
        dispatch = picks[0, :, NA * 128 :] + picks[1, :, NA * 128 :]
        for chip in range(4):
            rows = lax.dot_general(
                dispatch, tokens[chip], (((0,), (0,)), ((), ())), preferred_element_type=F32
            ).astype(BF)
            send_b[:, :, chip * FW : (chip + 1) * FW] = rows.reshape(E, SL, FW)
        whole_own().start()
        for k in range(NDP - 1):
            go(whole_copy(k))

    def whole_spread():
        for k in range(NDP - 1):
            whole_copy(k).wait_recv()
        whole_own().wait()
        go(whole_mate())

    def hidden_send(ch):
        return remote(hid.at[ch, 0], hid.at[ch, 1], h_send.at[ch], h_recv.at[ch], mate)

    def gate_up(ch, n):
        cols = pl.ds(n * 256, 256)
        rows = x_all[ch]
        g = jnp.dot(rows, wg_v[:, cols], preferred_element_type=F32)
        u = jnp.dot(rows, wu_v[:, cols], preferred_element_type=F32)
        hid[ch, 0, :, cols] = (g / (1.0 + jnp.exp(-g)) * u).astype(BF)

    def down(ch, chip):
        cols = columns(chip)
        return jnp.dot(hid[ch, 0], wd_v[0, :, cols], preferred_element_type=F32) + jnp.dot(
            hid[ch, 1], wd_v[1, :, cols], preferred_element_type=F32
        )

    def rows_of(h):
        return pl.ds(h * half, half)

    def hop(ch, side):
        return remote(
            part.at[ch, 0, rows_of(side)], hop_in.at[ch, side], t_send.at[ch, side], t_recv.at[ch, side], sides[side]
        )

    def near(ch, side, h, src):
        return remote(src, fin.at[ch, side, rows_of(h)], n_send.at[ch, side, h], n_recv.at[ch, side, h], sides[side])

    def reduce_start(ch):
        part[ch, 0] = down(ch, xo).astype(BF)
        for side in range(2):
            go(hop(ch, side))
        for side in range(2):
            part[ch, 1 + side] = down(ch, (xr, xl)[side]).astype(BF)
            go(near(ch, side, 1 - side, part.at[ch, 1 + side, rows_of(1 - side)]))

    def reduce_own(ch):
        own_part[ch] = down(ch, x)

    def reduce_hop(ch):
        for side in range(2):
            hop(ch, side).wait_recv()
            hop_out[ch, side] = (
                part[ch, 1 + side, rows_of(side), :].astype(F32) + hop_in[ch, side].astype(F32)
            ).astype(BF)
            go(near(ch, side, side, hop_out.at[ch, side]))

    e_of, j_of = dp // 2, lax.rem(dp, 2)

    def back_copy(ch, k):
        p = peers[k]
        rows = pl.ds(pl.multiple_of(p * SL, SL), SL)
        return remote(out.at[ch, rows], ret.at[ch, e_of, j_of], r_send.at[ch, k], r_recv.at[ch, k], {"dp": p})

    def back_own(ch):
        return pltpu.make_async_copy(out.at[ch, dp_rows], ret.at[ch, e_of, j_of], r_own.at[ch])

    def reduce_end(ch):
        for side in range(2):
            for h in range(2):
                near(ch, side, h, hop_out.at[ch, side]).wait_recv()
        total = own_part[ch] + fin[ch, 0].astype(F32) + fin[ch, 1].astype(F32)
        out[ch] = total.astype(BF)
        back_own(ch).start()
        for k in range(NDP - 1):
            go(back_copy(ch, k))

    def open_copy(k):
        p = peers[k]
        rows = pl.ds(pl.multiple_of(p * SL, SL), SL)
        return remote(part_b.at[rows], ret_b.at[e_of, j_of], r_send.at[2, k], r_recv.at[2, k], {"dp": p})

    def open_own():
        return pltpu.make_async_copy(part_b.at[dp_rows], ret_b.at[e_of, j_of], r_own.at[2])

    def open_start():
        for chip in range(4):
            part_b[:, chip * FW : (chip + 1) * FW] = down(2, chip).astype(BF)
        open_own().start()
        for k in range(NDP - 1):
            go(open_copy(k))

    def shares(k):
        wide_w = jnp.broadcast_to(weight[k : k + 1, :], (128, 128)).T
        return jnp.concatenate([wide_w] * (FW // 128), axis=1)

    def moe_copy(k):
        return remote(moe_out.at[k], moe_in.at[k], m_send.at[k], m_recv.at[k], x_peers[k])

    def open_end():
        for k in range(NDP - 1):
            open_copy(k).wait_recv()
        open_own().wait()
        w = [shares(k) for k in range(2)]

        def mix(chip):
            both = [ret_b[:, j, :, columns(chip)].reshape(128, FW) for j in range(2)]
            total = jnp.zeros((128, FW), F32)
            for k in range(2):
                pick = picks[k, :, NA * 128 :]
                rows = jnp.dot(pick, both[0], preferred_element_type=F32)
                rows = rows + jnp.dot(pick, both[1], preferred_element_type=F32)
                total = total + w[k] * rows
            return total

        for k in (1, 0, 2):
            moe_out[k] = mix(lax.rem(x + 1 + k, 4)).astype(BF)
            go(moe_copy(k))
        moe_own[...] = mix(x) + hidden[...]

    def combine(ch):
        for k in range(NDP - 1):
            back_copy(ch, k).wait_recv()
        back_own(ch).wait()
        total = moe_own[...]
        for k in range(2):
            pick = picks[k, :, ch * 128 : (ch + 1) * 128]
            rows = jnp.dot(pick, ret[ch, :, 0].reshape(128, FW), preferred_element_type=F32)
            rows = rows + jnp.dot(pick, ret[ch, :, 1].reshape(128, FW), preferred_element_type=F32)
            total = total + shares(k) * rows
        moe_own[...] = total

    dispatch = picks[0] + picks[1]
    for ch in range(NA):
        rows = lax.dot_general(
            dispatch[:, ch * 128 : (ch + 1) * 128], tokens[x], (((0,), (0,)), ((), ())), preferred_element_type=F32
        ).astype(BF)
        send[ch] = rows.reshape(E, SL, FW)
        slice_own(ch).start()
        for k in range(NDP - 1):
            go(slice_copy(ch, k))
    spread_own(0)
    whole_start()
    spread_on(0)
    spread_own(1)
    spread_rest(0)
    spread_far(0)
    for copy in w_copies[:16]:
        copy.wait()
    spread_end(0)

    gate_up(0, 0)
    spread_on(1)
    gate_up(0, 1)
    whole_spread()
    gate_up(0, 2)
    go(hidden_send(0))
    spread_rest(1)
    for copy in w_copies[16:]:
        copy.wait()
    for copy in mate_w:
        copy.wait_recv()
    hidden_send(0).wait_recv()
    reduce_start(0)
    reduce_own(0)
    spread_far(1)
    whole_mate().wait_recv()

    gate_up(2, 0)
    gate_up(2, 1)
    reduce_hop(0)
    gate_up(2, 2)
    go(hidden_send(2))
    spread_end(1)
    gate_up(1, 0)
    hidden_send(2).wait_recv()
    open_start()
    gate_up(1, 1)
    reduce_end(0)
    gate_up(1, 2)
    go(hidden_send(1))
    hidden_send(1).wait_recv()
    reduce_start(1)
    reduce_own(1)
    reduce_hop(1)
    open_end()
    combine(0)
    reduce_end(1)
    total = moe_own[...]
    for k in range(3):
        moe_copy(k).wait_recv()
        total = total + moe_in[k].astype(F32)
    moe_own[...] = total
    combine(1)

    mixed = moe_own[...]
    result[...] = (mixed * row_scales(2, mixed) * final_gain[...]).astype(BF)
    for copy in sent:
        copy.wait_send()


V = pltpu.VMEM


def layer(operands, collective_id):
    spaces = [pltpu.VMEM] * 3 + [pl.ANY] * 2 + [pltpu.VMEM] * 2 + [pl.ANY] + [pltpu.VMEM] * 5 + [pl.ANY] * 3
    return pl.pallas_call(
        layer_kernel,
        out_shape=jax.ShapeDtypeStruct((128, FW), BF),
        in_specs=[pl.BlockSpec(memory_space=space) for space in spaces],
        out_specs=pl.BlockSpec(memory_space=pltpu.VMEM),
        scratch_shapes=[
            V((NDP * DEC, FW), BF),
            V((2048, HD), BF),
            V((2048, HD), BF),
            V((FW, D), BF),
            V((128, NDP * DEC), BF),
            V((4, 128, 128), F32),
            V((4, 128, 128), F32),
            V((128, FW), F32),
            V((128, FW), BF),
            V((NDP * DEC, FW), BF),
            V((NDP - 1, DEC, FW), BF),
            V((8, 8, 128), F32),
            V((NDP, 8, 128), F32),
            V((128, FW), BF),
            V((2, 7, 64, FW), BF),
            V((2, 7, 64, FW), BF),
            V((3, 8, 8, 128), F32),
            V((128, FW), F32),
            V((2, 128, E * C), BF),
            V((NA, E, SL, FW), BF),
            V((NCH, RC, D), BF),
            V((D, HID), BF),
            V((D, HID), BF),
            V((2, HID, D // 2), BF),
            V((NCH, 2, RC, HID), BF),
            V((NA, 3, RC, FW), BF),
            V((NA, RC, FW), F32),
            V((NA, 2, RC // 2, FW), BF),
            V((NA, 2, RC // 2, FW), BF),
            V((NA, 2, RC, FW), BF),
            V((NA, RC, FW), BF),
            V((NA, E, 2, SL, FW), BF),
            V((4, 128, FW), BF),
            V((E, SL, 4 * FW), BF),
            V((RC, 4 * FW), BF),
            V((E, 2, SL, 4 * FW), BF),
            V((3, 128, FW), BF),
            V((3, 128, FW), BF),
            V((128, FW), F32),
            DMA((4,)),
            DMA((2, 3)),
            DMA((2, 3)),
            DMA((2, 4, 3)),
            DMA((2, 4, 3)),
            DMA((NDP - 1,)),
            DMA((NDP - 1,)),
            DMA((NDP - 1,)),
            DMA((NDP - 1,)),
            DMA((2, 7)),
            DMA((2, 7)),
            DMA((20,)),
            DMA((3,)),
            DMA((NCH,)),
            DMA((4,)),
            DMA((4,)),
            DMA((NCH, NDP - 1)),
            DMA((NCH, NDP - 1)),
            DMA((NA, 2, 2)),
            DMA((NA, 2, 2)),
            DMA((NA, 2)),
            DMA((NA, 2)),
            DMA((NCH, 4)),
            DMA((NCH, 4)),
            DMA((NCH,)),
            DMA((NCH,)),
            DMA((NA, 2)),
            DMA((NA, 2)),
            DMA((NA, 2, 2)),
            DMA((NA, 2, 2)),
            DMA((NCH, NDP - 1)),
            DMA((NCH, NDP - 1)),
            DMA((2, 3)),
            DMA((2, 3)),
            DMA((3,)),
            DMA((3,)),
            DMA((3, 7)),
            DMA((3, 7)),
        ],
        compiler_params=comm_params(collective_id),
        name="layer",
    )(*operands)


def local(
    residual,
    queries,
    new_keys,
    new_values,
    cache_keys,
    cache_values,
    cache_len,
    page_order,
    out_proj,
    attn_gain,
    routes,
    route_weight,
    gate_proj,
    up_proj,
    down_proj,
    final_gain,
):
    return layer(
        (
            queries,
            new_keys,
            new_values,
            cache_keys.reshape(-1, HD),
            cache_values.reshape(-1, HD),
            cache_len.reshape(8, 128),
            page_order.reshape(16, 128),
            out_proj,
            residual,
            attn_gain.reshape(32, 128),
            routes.T,
            route_weight.T,
            final_gain[None, :],
            gate_proj,
            up_proj,
            down_proj,
        ),
        0,
    )


def solution(mesh):
    return jax.shard_map(
        local,
        mesh=mesh,
        in_specs=(
            P("dp", "mp"),
            P("dp", "mp"),
            P("dp", "mp"),
            P("dp", "mp"),
            P("dp", None, "mp"),
            P("dp", None, "mp"),
            P(),
            P(),
            P("mp", None),
            P(),
            P("dp", None),
            P("dp", None),
            P(None, ("dp", "mp")),
            P(None, ("dp", "mp")),
            P(("dp", "mp"), None),
            P("mp"),
        ),
        out_specs=P("dp", "mp"),
        check_vma=False,
    )
```

```python
import functools

import jax
import jax.numpy as jnp
from jax import lax
from jax.experimental import pallas as pl
from jax.experimental.pallas import tpu as pltpu
from jax.sharding import PartitionSpec as P

D = 4096
HQ = 32
KVH = 8
HD = 128
E = 8
PAGE = 16
DEC = 64
PRE = 64
C = 48
NDP = 16
NCH = 3
NA = 2
NB = 2
SL = C // NCH
RC = NDP * SL
FW = 512
HID = 768

MESH = pl.DeviceIdType.MESH
DMA = pltpu.SemaphoreType.DMA
BF = jnp.bfloat16
F32 = jnp.float32

neg_big = -1e30
eps_norm = 1e-05


def remote(src, dst, send_sem, recv_sem, device):
    return pltpu.make_async_remote_copy(
        src_ref=src,
        dst_ref=dst,
        send_sem=send_sem,
        recv_sem=recv_sem,
        device_id=device,
        device_id_type=MESH,
    )


def greet(devices):
    barrier = pltpu.get_barrier_semaphore()
    for device in devices:
        pl.semaphore_signal(barrier, inc=1, device_id=device, device_id_type=MESH)
    pl.semaphore_wait(barrier, len(devices))


def comm_params(collective_id):
    return pltpu.CompilerParams(
        collective_id=collective_id, has_side_effects=True, vmem_limit_bytes=60 << 20
    )


def iota(shape, axis):
    return lax.broadcasted_iota(jnp.int32, shape, axis)


def square_sums(rows):
    ones = jnp.ones((8, FW), F32)
    return lax.dot_general(
        ones,
        rows * rows,
        (((1,), (1,)), ((), ())),
        precision=lax.Precision.HIGHEST,
        preferred_element_type=F32,
    )


def as_columns(row):
    wide = jnp.broadcast_to(row[0:1, :], (128, 128)).T
    return jnp.concatenate([wide] * (FW // 128), axis=1)


def to_columns(stack):
    return stack.T


def layer_kernel(
    queries,
    new_keys,
    new_values,
    keys,
    values,
    lengths,
    order,
    out_proj,
    residual,
    attn_gain,
    routes,
    weight,
    final_gain,
    wg,
    wu,
    wd,
    result,
    q_all,
    keys_v,
    values_v,
    proj_v,
    owners,
    scores,
    weights,
    page_q,
    page_w,
    val_out,
    val_in,
    stat_out,
    stat_in,
    attn,
    proj_part,
    got,
    squares,
    hidden,
    picks,
    send,
    x_all,
    wg_v,
    wu_v,
    wd_v,
    hid,
    part,
    own_part,
    hop_in,
    hop_out,
    fin,
    out,
    ret,
    tokens,
    send_b,
    part_b,
    ret_b,
    moe_out,
    moe_in,
    moe_own,
    scale_out,
    scale_in,
    l_sems,
    s1,
    r1,
    s2,
    r2,
    vs,
    vr,
    ts,
    tr,
    ps,
    pr,
    w_sems,
    a_own,
    r_own,
    wp_send,
    wp_recv,
    a_send,
    a_recv,
    g_send,
    g_recv,
    f_send,
    f_recv,
    p_send,
    p_recv,
    h_send,
    h_recv,
    t_send,
    t_recv,
    n_send,
    n_recv,
    r_send,
    r_recv,
    k_send,
    k_recv,
    m_send,
    m_recv,
    q_send,
    q_recv,
    c_send,
    c_recv,
    c_own,
):
    dp = lax.axis_index("dp")
    mp = lax.axis_index("mp")
    z, y = dp // 4, lax.rem(dp, 4)
    scale = HD ** (-0.5)
    offsets = ((2, 2), (2, 3), (3, 2), (2, 1), (1, 2), (2, 0), (0, 2), (3, 1), (1, 3), (3, 3), (1, 1), (3, 0), (0, 3), (1, 0), (0, 1))
    peers = [lax.rem(z + a, 4) * 4 + lax.rem(y + b, 4) for a, b in offsets]
    mp_peers = [lax.rem(mp + k, 8) for k in range(1, 8)]
    x, c = mp // 2, lax.rem(mp, 2)
    xr, xo, xl = lax.rem(x + 1, 4), lax.rem(x + 2, 4), lax.rem(x + 3, 4)
    mr, mo, ml = xr * 2 + c, xo * 2 + c, xl * 2 + c
    right, left, mate = {"mp": mr}, {"mp": ml}, {"mp": x * 2 + 1 - c}
    sides = (right, left)
    x_peers = [{"mp": lax.rem(x + k, 4) * 2 + c} for k in range(1, 4)]
    half = RC // 2

    def wide(owner):
        return pl.ds(pl.multiple_of((lax.rem(owner, 2) * 4 + owner // 2) * FW, FW), FW)

    def columns(owner):
        return pl.ds(pl.multiple_of(owner * FW, FW), FW)

    dp_rows = pl.ds(pl.multiple_of(dp * SL, SL), SL)
    c_cols = pl.ds(pl.multiple_of(c * 4 * FW, 4 * FW), 4 * FW)
    mate_cols = pl.ds(pl.multiple_of((1 - c) * 4 * FW, 4 * FW), 4 * FW)

    w_copies = []
    for w, (src, dst) in enumerate(((wg, wg_v), (wu, wu_v))):
        for core in range(2):
            for chip in range(4):
                w_copies.append(
                    pltpu.make_async_copy(
                        src.at[pl.ds((chip * 2 + core) * FW, FW), :],
                        dst.at[pl.ds((core * 4 + chip) * FW, FW), :],
                        w_sems.at[w * 8 + core * 4 + chip],
                    )
                )
    for j in range(4):
        w_copies.append(
            pltpu.make_async_copy(
                wd.at[:, pl.ds(pl.multiple_of(j * 1024 + c * FW, FW), FW)],
                wd_v.at[0, :, pl.ds(j * FW, FW)],
                w_sems.at[16 + j],
            )
        )
    loads = [
        pltpu.make_async_copy(keys, keys_v, l_sems.at[0]),
        pltpu.make_async_copy(values, values_v, l_sems.at[1]),
        pltpu.make_async_copy(out_proj, proj_v, l_sems.at[2]),
    ]
    q_rows = DEC // 2

    def q_half(owner, h):
        return q_all.at[pl.ds(pl.multiple_of(owner * DEC + h * q_rows, q_rows), q_rows), :]

    own_q = pltpu.make_async_copy(
        queries.at[pl.ds(0, DEC), :],
        q_all.at[pl.ds(pl.multiple_of(dp * DEC, DEC), DEC), :],
        l_sems.at[3],
    )
    own_q.start()
    loads[2].start()
    loads[0].start()
    loads[1].start()
    own_q.wait()
    for copy in w_copies:
        copy.start()
    greet([{"dp": p} for p in peers] + [{"mp": p} for p in mp_peers])
    sent = []

    def go(copy):
        copy.start()
        sent.append(copy)

    def group(along, step, across):
        zz = lax.rem(z + (step if along == 0 else across) + 8, 4)
        yy = lax.rem(y + (across if along == 0 else step) + 8, 4)
        return zz * 4 + yy

    def first(h, k):
        return remote(q_half(dp, h), q_half(dp, h), s1.at[h, k - 1], r1.at[h, k - 1], {"dp": group(h, k, 0)})

    def second(h, j, k):
        owner = group(h, -j, 0)
        return remote(
            q_half(owner, h), q_half(owner, h), s2.at[h, j, k - 1], r2.at[h, j, k - 1], {"dp": group(h, 0, k)}
        )

    for k in (1, 3, 2):
        for h in range(2):
            go(first(h, k))
    for h in range(2):
        for k in range(1, 4):
            go(second(h, 0, k))
    mate_w = []
    for j in range(4):
        mate_w.append(
            remote(
                wd.at[:, pl.ds(pl.multiple_of(j * 1024 + (1 - c) * FW, FW), FW)],
                wd_v.at[1, :, pl.ds(j * FW, FW)],
                wp_send.at[j],
                wp_recv.at[j],
                mate,
            )
        )
        go(mate_w[j])

    lane = iota((128, 128), 1)
    row = iota((128, 128), 0)
    counts = lax.shift_right_logical(lengths[...] + (PAGE - 1), 4)
    upto = (row <= lane).astype(BF)
    within = jnp.dot(counts.astype(F32).astype(BF), upto, preferred_element_type=F32)
    place = jnp.zeros((128, 128), F32)
    ids = dp * 128 + row
    for q in range(16):
        place = place + jnp.where(order[q : q + 1, :] == ids, (lane + q * 128).astype(F32), 0.0)
    place = jnp.sum(place, axis=1, keepdims=True)
    before = jnp.zeros((1, 1), F32)
    passed = jnp.zeros((128, 128), F32)
    ends = []
    for i in range(8):
        ends.append(within[i : i + 1, :] + before)
        before = before + within[i : i + 1, 127:128]
        passed = passed + jnp.where(ends[i] <= place, 1.0, 0.0)
    owner = jnp.sum(passed, axis=1, keepdims=True)

    for k in range(1, 4):
        for h in range(2):
            remote(q_half(dp, h), q_half(group(h, -k, 0), h), s1.at[h, k - 1], r1.at[h, k - 1], {"dp": peers[0]}).wait_recv()
            for kk in range(1, 4):
                go(second(h, k, kk))

    begin = jnp.zeros((128, 128), F32)
    length = jnp.zeros((128, 128), F32)
    for i in range(8):
        mine = (lane + i * 128).astype(F32) == owner
        cnt = counts[i : i + 1, :].astype(F32)
        begin = begin + jnp.where(mine, ends[i] - cnt, 0.0)
        length = length + jnp.where(mine, lengths[i : i + 1, :].astype(F32), 0.0)
        owners[:, i * 128 : (i + 1) * 128] = jnp.where(mine, 1.0, 0.0).astype(BF)
    begin = jnp.sum(begin, axis=1, keepdims=True)
    length = jnp.sum(length, axis=1, keepdims=True)
    valid = length - (place - begin) * PAGE
    key_ok = (lax.shift_right_logical(lane, 4) == (row & 7)) & ((lane & 15).astype(F32) < valid)
    owner_row = jnp.broadcast_to(owner, (128, 128)).T
    same = owner_row == owner
    leader = jnp.sum(jnp.where(same & (lane < row), 1.0, 0.0), axis=1, keepdims=True) == 0.0

    below = (lane < row).astype(BF)
    route = [
        jnp.broadcast_to(routes[k : k + 1, :].astype(F32), (128, 128)).T[:, 0:1].astype(jnp.int32) for k in range(2)
    ]
    named = [(lane == r).astype(F32) for r in route]
    ahead = [jnp.dot(below, n.astype(BF), preferred_element_type=F32) for n in named]
    ahead[1] = ahead[1] + jnp.sum(named[0], axis=0, keepdims=True)
    cells = iota((128, E * C), 1)
    for k in range(2):
        slot = jnp.sum(named[k] * ahead[k], axis=1, keepdims=True).astype(jnp.int32)
        target = lax.shift_right_logical(slot, 4) * (E * SL) + route[k] * SL + (slot & (SL - 1))
        picks[k] = jnp.where(cells == target, 1.0, 0.0).astype(BF)

    causal = iota((PRE, PRE), 0) >= iota((PRE, PRE), 1)
    for g in range(4):
        cols = slice(g * HD, (g + 1) * HD)
        s = lax.dot_general(
            queries[DEC:, cols], new_keys[DEC:, :], (((1,), (1,)), ((), ())), preferred_element_type=F32
        )
        s = jnp.where(causal, s * scale, neg_big)
        w = jnp.where(causal, jnp.exp(s - jnp.max(s, axis=1, keepdims=True)), 0.0)
        den = jnp.sum(w, axis=1, keepdims=True)
        num = jnp.dot(w.astype(BF), new_values[DEC:, :], preferred_element_type=F32)
        attn[DEC:, cols] = (num / den).astype(BF)
    loads[2].wait()

    pieces = ((0, 32), (32, 32), (64, 64))

    def piece_copy(i, k):
        rows = pl.ds(*pieces[i])
        return remote(
            proj_part.at[k, rows], got.at[k, rows], ps.at[i, k], pr.at[i, k], {"mp": mp_peers[k]}
        )

    def project(i):
        rows = pl.ds(*pieces[i])
        a = attn[rows, :]
        for k, p in enumerate(mp_peers):
            cols = pl.ds(pl.multiple_of(p * FW, FW), FW)
            proj_part[k, rows] = jnp.dot(a, proj_v[:, cols], preferred_element_type=F32).astype(BF)
            go(piece_copy(i, k))
        cols = pl.ds(pl.multiple_of(mp * FW, FW), FW)
        own = jnp.dot(a, proj_v[:, cols], preferred_element_type=F32)
        hidden[rows, :] = own + residual[rows, :].astype(F32)

    def collect(i):
        rows = pl.ds(*pieces[i])
        total = hidden[rows, :]
        for k in range(7):
            piece_copy(i, k).wait_recv()
            total = total + got[k, rows].astype(F32)
        hidden[rows, :] = total

    project(2)

    own_cols = jnp.zeros((64, 128), F32)
    lane64 = iota((64, 128), 1)
    for g in range(4):
        prod = queries[:DEC, g * HD : (g + 1) * HD].astype(F32) * new_keys[:DEC, :].astype(F32)
        own_cols = jnp.where(lane64 == g, jnp.sum(prod, axis=1, keepdims=True) * scale, own_cols)
    own_score = to_columns(jnp.concatenate([own_cols, jnp.zeros((64, 128), F32)], axis=0))[0:8, :]

    for j in range(4):
        for k in range(1, 4):
            for h in range(2):
                remote(
                    q_half(dp, h), q_half(group(h, -j, -k), h), s2.at[h, j, k - 1], r2.at[h, j, k - 1], {"dp": peers[0]}
                ).wait_recv()

    page_q[...] = jnp.dot(owners[...], q_all[...], preferred_element_type=F32)
    loads[0].wait()
    loads[1].wait()
    for k in range(16):
        qk = jnp.concatenate([page_q[8 * k : 8 * k + 8, g * HD : (g + 1) * HD] for g in range(4)], axis=0)
        s = lax.dot_general(
            qk.astype(BF), keys_v[128 * k : 128 * (k + 1), :], (((1,), (1,)), ((), ())), preferred_element_type=F32
        )
        for g in range(4):
            scores[g, 8 * k : 8 * k + 8, :] = s[8 * g : 8 * g + 8, :]
    tops = jnp.zeros((128, 128), F32)
    sums = []
    for g in range(4):
        s = jnp.where(key_ok, scores[g] * scale, neg_big)
        m = jnp.max(s, axis=1, keepdims=True)
        w = jnp.where(key_ok, jnp.exp(s - m), 0.0)
        weights[g] = w
        sums.append(jnp.sum(w, axis=1, keepdims=True))
        tops = jnp.where(lane == g, m, tops)
    for k in range(16):
        wk = jnp.concatenate([weights[g, 8 * k : 8 * k + 8, :] for g in range(4)], axis=0)
        v = jnp.dot(wk.astype(BF), values_v[128 * k : 128 * (k + 1), :], preferred_element_type=F32)
        for g in range(4):
            scores[g, 8 * k : 8 * k + 8, :] = v[8 * g : 8 * g + 8, :]
    top_rows = tops.T
    stat = jnp.zeros((128, 128), F32)
    for g in range(4):
        top = jnp.max(jnp.where(same, top_rows[g : g + 1, :], neg_big), axis=1, keepdims=True)
        factor = jnp.exp(tops[:, g : g + 1] - top)
        page_w[:, g * HD : (g + 1) * HD] = (scores[g] * factor).astype(BF)
        stat = jnp.where(lane == g, jnp.where(leader, top, 0.0), stat)
        stat = jnp.where(lane == 4 + g, sums[g] * factor, stat)
    stat8 = stat.T[0:8, :]
    for i in range(8):
        stat_out[i] = jnp.dot(
            stat8,
            owners[:, i * 128 : (i + 1) * 128].astype(F32),
            precision=lax.Precision.HIGHEST,
            preferred_element_type=F32,
        )
    for i in range(4):
        val_out[i * 256 : (i + 1) * 256, :] = lax.dot_general(
            owners[:, i * 256 : (i + 1) * 256], page_w[...], (((0,), (0,)), ((), ())), preferred_element_type=F32
        ).astype(BF)

    def swap_stat(k):
        p = peers[k]
        return remote(stat_out.at[p // 2], stat_in.at[k], ts.at[k], tr.at[k], {"dp": p})

    def swap_val(h, k):
        p = peers[k]
        rows = pl.ds(pl.multiple_of(p * DEC + h * 32, 32), 32)
        return remote(val_out.at[rows, :], val_in.at[k, pl.ds(h * 32, 32), :], vs.at[h, k], vr.at[h, k], {"dp": p})

    for k in range(NDP - 1):
        go(swap_stat(k))
        go(swap_val(0, k))
    for k in range(NDP - 1):
        go(swap_val(1, k))

    def square_copy(t, k):
        return remote(squares.at[t, 7], squares.at[t, k], q_send.at[t, k], q_recv.at[t, k], {"mp": mp_peers[k]})

    def squares_start(t, rows):
        squares[t, 7] = square_sums(rows)
        for k in range(7):
            go(square_copy(t, k))

    def squares_end(t):
        summed = squares[t, 7]
        for k in range(7):
            square_copy(t, k).wait_recv()
            summed = summed + squares[t, k]
        return as_columns(lax.rsqrt(summed / D + eps_norm))

    def token_copy(i, k):
        rows = tokens.at[x, pl.ds(*pieces[i]), :]
        return remote(rows, rows, k_send.at[i, k], k_recv.at[i, k], x_peers[k])

    gain_rows = attn_gain[pl.ds(mp * 4, 4), :]
    gain_cols = jnp.concatenate([gain_rows[i : i + 1, :] for i in range(4)], axis=1)

    def finish(i):
        rows = pl.ds(*pieces[i])
        tokens[x, rows, :] = (hidden[rows, :] * gain_cols).astype(BF)
        for k in (0, 2, 1):
            go(token_copy(i, k))

    collect(2)
    finish(2)
    for k in range(NDP - 1):
        swap_stat(k).wait_recv()
    stat_in[NDP - 1] = stat_out[dp // 2]
    odd = lax.rem(dp, 2) == 1
    got_stats = stat_in[...].reshape(128, 128)
    got_stats = jnp.where(odd, pltpu.roll(got_stats, 64, 1), got_stats).reshape(NDP, 8, 128)
    l_in = pltpu.roll(got_stats, 4, 1)
    m_in = jnp.where(l_in > 0.0, got_stats, neg_big)
    top = jnp.maximum(jnp.max(m_in, axis=0), own_score)
    f_in = jnp.where(l_in > 0.0, jnp.exp(jnp.minimum(m_in - top[None], 0.0)), 0.0)
    f_own = jnp.exp(own_score - top)
    inv = 1.0 / (jnp.sum(l_in * f_in, axis=0) + f_own)
    f_cols = to_columns((f_in * inv[None]).reshape(128, 128))
    own_f = to_columns(jnp.concatenate([f_own * inv, jnp.zeros((120, 128), F32)], axis=0))
    for h in range(2):
        rows = slice(h * 32, (h + 1) * 32)
        nums = [own_f[rows, g : g + 1] * new_values[rows, :].astype(F32) for g in range(4)]
        mine = val_out[pl.ds(pl.multiple_of(dp * DEC + h * 32, 32), 32), :]
        for k in range(NDP):
            if k < NDP - 1:
                swap_val(h, k).wait_recv()
            v = (val_in[k, rows] if k < NDP - 1 else mine).astype(F32)
            for g in range(4):
                nums[g] = nums[g] + v[:, g * HD : (g + 1) * HD] * f_cols[rows, 8 * k + g : 8 * k + g + 1]
        for g in range(4):
            attn[rows, g * HD : (g + 1) * HD] = nums[g].astype(BF)
        project(h)
    for h in range(2):
        collect(h)
        finish(h)

    def block(ch, h, owner):
        return x_all.at[ch, pl.ds(h * half, half), wide(owner)]

    def whole(ch, owner):
        return x_all.at[ch, :, wide(owner)]

    def neighbour(ch, side, h):
        return remote(block(ch, h, mp), block(ch, h, mp), g_send.at[ch, side, h], g_recv.at[ch, side, h], sides[side])

    def onward(ch, side):
        owner = (ml, mr)[side]
        return remote(
            block(ch, side, owner), block(ch, side, owner), f_send.at[ch, side], f_recv.at[ch, side], sides[side]
        )

    def to_mate(ch, which):
        owner = (mp, ml, mr, mo)[which]
        return remote(whole(ch, owner), whole(ch, owner), p_send.at[ch, which], p_recv.at[ch, which], mate)

    def slice_copy(ch, k):
        p = peers[k]
        return remote(
            send.at[ch, p // 2], x_all.at[ch, dp_rows, wide(mp)], a_send.at[ch, k], a_recv.at[ch, k], {"dp": p}
        )

    def slice_own(ch):
        return pltpu.make_async_copy(send.at[ch, dp // 2], x_all.at[ch, dp_rows, wide(mp)], a_own.at[ch])

    def spread_own(ch):
        for k in range(NDP - 1):
            slice_copy(ch, k).wait_recv()
        slice_own(ch).wait()
        for h in range(2):
            go(neighbour(ch, 0, h))
            go(neighbour(ch, 1, 1 - h))
        go(to_mate(ch, 0))

    def spread_on(ch):
        for side in range(2):
            neighbour(ch, side, side).wait_recv()
            go(onward(ch, side))

    def spread_rest(ch):
        for side in range(2):
            neighbour(ch, side, 1 - side).wait_recv()
            go(to_mate(ch, 1 + side))

    def spread_far(ch):
        for side in range(2):
            onward(ch, side).wait_recv()
        go(to_mate(ch, 3))

    def spread_end(ch):
        for which in range(4):
            to_mate(ch, which).wait_recv()

    def whole_copy(k):
        p = peers[k]
        return remote(send_b.at[p // 2], x_all.at[2, dp_rows, c_cols], a_send.at[2, k], a_recv.at[2, k], {"dp": p})

    def whole_own():
        return pltpu.make_async_copy(send_b.at[dp // 2], x_all.at[2, dp_rows, c_cols], a_own.at[2])

    def whole_mate():
        return remote(x_all.at[2, :, c_cols], x_all.at[2, :, c_cols], p_send.at[2, 0], p_recv.at[2, 0], mate)

    def whole_start():
        for i in range(3):
            for k in range(3):
                token_copy(i, k).wait_recv()
        dispatch = picks[0, :, NA * 128 :] + picks[1, :, NA * 128 :]
        for chip in range(4):
            rows = lax.dot_general(
                dispatch, tokens[chip], (((0,), (0,)), ((), ())), preferred_element_type=F32
            ).astype(BF)
            send_b[:, :, chip * FW : (chip + 1) * FW] = rows.reshape(E, SL, FW)
        whole_own().start()
        for k in range(NDP - 1):
            go(whole_copy(k))

    def whole_spread():
        for k in range(NDP - 1):
            whole_copy(k).wait_recv()
        whole_own().wait()
        go(whole_mate())

    def scale_copy(k):
        p = peers[k]
        return remote(
            scale_out.at[:, p // 2], scale_in.at[:, dp_rows, :], c_send.at[k], c_recv.at[k], {"dp": p}
        )

    def scale_own():
        return pltpu.make_async_copy(scale_out.at[:, dp // 2], scale_in.at[:, dp_rows, :], c_own)

    def scale_start():
        scales = squares_end(0)[:, :128]
        upper = scales.astype(BF)
        lower = (scales - upper.astype(F32)).astype(BF)
        both = jnp.where(iota((128, 128), 1) < 64, upper.astype(F32), lower.astype(F32)).astype(BF)
        for ch in range(NCH):
            rows = lax.dot_general(
                dispatch[:, ch * 128 : (ch + 1) * 128], both, (((0,), (0,)), ((), ())), preferred_element_type=F32
            ).astype(BF)
            scale_out[ch] = rows.reshape(E, SL, 128)
        scale_own().start()
        for k in range(NDP - 1):
            go(scale_copy(k))

    def scale_end():
        for k in range(NDP - 1):
            scale_copy(k).wait_recv()
        scale_own().wait()

    def hidden_send(ch):
        return remote(hid.at[ch, 0], hid.at[ch, 1], h_send.at[ch], h_recv.at[ch], mate)

    def gate_up(ch, n):
        cols = pl.ds(n * 256, 256)
        rows = x_all[ch]
        scales = scale_in[ch, :, 0:1].astype(F32) + scale_in[ch, :, 64:65].astype(F32)
        g = jnp.dot(rows, wg_v[:, cols], preferred_element_type=F32) * scales
        u = jnp.dot(rows, wu_v[:, cols], preferred_element_type=F32) * scales
        hid[ch, 0, :, cols] = (g / (1.0 + jnp.exp(-g)) * u).astype(BF)

    def down(ch, chip):
        cols = columns(chip)
        return jnp.dot(hid[ch, 0], wd_v[0, :, cols], preferred_element_type=F32) + jnp.dot(
            hid[ch, 1], wd_v[1, :, cols], preferred_element_type=F32
        )

    def rows_of(h):
        return pl.ds(h * half, half)

    def hop(ch, side):
        return remote(
            part.at[ch, 0, rows_of(side)], hop_in.at[ch, side], t_send.at[ch, side], t_recv.at[ch, side], sides[side]
        )

    def near(ch, side, h, src):
        return remote(src, fin.at[ch, side, rows_of(h)], n_send.at[ch, side, h], n_recv.at[ch, side, h], sides[side])

    def reduce_start(ch):
        part[ch, 0] = down(ch, xo).astype(BF)
        for side in range(2):
            go(hop(ch, side))
        for side in range(2):
            part[ch, 1 + side] = down(ch, (xr, xl)[side]).astype(BF)
            go(near(ch, side, 1 - side, part.at[ch, 1 + side, rows_of(1 - side)]))

    def reduce_own(ch):
        own_part[ch] = down(ch, x)

    def reduce_hop(ch):
        for side in range(2):
            hop(ch, side).wait_recv()
            hop_out[ch, side] = (
                part[ch, 1 + side, rows_of(side), :].astype(F32) + hop_in[ch, side].astype(F32)
            ).astype(BF)
            go(near(ch, side, side, hop_out.at[ch, side]))

    e_of, j_of = dp // 2, lax.rem(dp, 2)

    def back_copy(ch, k):
        p = peers[k]
        rows = pl.ds(pl.multiple_of(p * SL, SL), SL)
        return remote(out.at[ch, rows], ret.at[ch, e_of, j_of], r_send.at[ch, k], r_recv.at[ch, k], {"dp": p})

    def back_own(ch):
        return pltpu.make_async_copy(out.at[ch, dp_rows], ret.at[ch, e_of, j_of], r_own.at[ch])

    def reduce_end(ch):
        for side in range(2):
            for h in range(2):
                near(ch, side, h, hop_out.at[ch, side]).wait_recv()
        total = own_part[ch] + fin[ch, 0].astype(F32) + fin[ch, 1].astype(F32)
        out[ch] = total.astype(BF)
        back_own(ch).start()
        for k in range(NDP - 1):
            go(back_copy(ch, k))

    def open_copy(k):
        p = peers[k]
        rows = pl.ds(pl.multiple_of(p * SL, SL), SL)
        return remote(part_b.at[rows], ret_b.at[e_of, j_of], r_send.at[2, k], r_recv.at[2, k], {"dp": p})

    def open_own():
        return pltpu.make_async_copy(part_b.at[dp_rows], ret_b.at[e_of, j_of], r_own.at[2])

    def open_start():
        for chip in range(4):
            part_b[:, chip * FW : (chip + 1) * FW] = down(2, chip).astype(BF)
        open_own().start()
        for k in range(NDP - 1):
            go(open_copy(k))

    def shares(k):
        wide_w = jnp.broadcast_to(weight[k : k + 1, :], (128, 128)).T
        return jnp.concatenate([wide_w] * (FW // 128), axis=1)

    def moe_copy(k):
        return remote(moe_out.at[k], moe_in.at[k], m_send.at[k], m_recv.at[k], x_peers[k])

    def open_end():
        for k in range(NDP - 1):
            open_copy(k).wait_recv()
        open_own().wait()
        w = [shares(k) for k in range(2)]

        def mix(chip):
            both = [ret_b[:, j, :, columns(chip)].reshape(128, FW) for j in range(2)]
            total = jnp.zeros((128, FW), F32)
            for k in range(2):
                pick = picks[k, :, NA * 128 :]
                rows = jnp.dot(pick, both[0], preferred_element_type=F32)
                rows = rows + jnp.dot(pick, both[1], preferred_element_type=F32)
                total = total + w[k] * rows
            return total

        for k in (1, 0, 2):
            moe_out[k] = mix(lax.rem(x + 1 + k, 4)).astype(BF)
            go(moe_copy(k))
        moe_own[...] = mix(x) + hidden[...]

    def combine(ch):
        for k in range(NDP - 1):
            back_copy(ch, k).wait_recv()
        back_own(ch).wait()
        total = moe_own[...]
        for k in range(2):
            pick = picks[k, :, ch * 128 : (ch + 1) * 128]
            rows = jnp.dot(pick, ret[ch, :, 0].reshape(128, FW), preferred_element_type=F32)
            rows = rows + jnp.dot(pick, ret[ch, :, 1].reshape(128, FW), preferred_element_type=F32)
            total = total + shares(k) * rows
        moe_own[...] = total

    dispatch = picks[0] + picks[1]
    for ch in range(NA):
        rows = lax.dot_general(
            dispatch[:, ch * 128 : (ch + 1) * 128], tokens[x], (((0,), (0,)), ((), ())), preferred_element_type=F32
        ).astype(BF)
        send[ch] = rows.reshape(E, SL, FW)
        slice_own(ch).start()
        for k in range(NDP - 1):
            go(slice_copy(ch, k))
    squares_start(0, hidden[...])
    spread_own(0)
    scale_start()
    whole_start()
    spread_on(0)
    spread_own(1)
    spread_rest(0)
    spread_far(0)
    for copy in w_copies[:16]:
        copy.wait()
    spread_end(0)
    scale_end()

    gate_up(0, 0)
    spread_on(1)
    gate_up(0, 1)
    whole_spread()
    gate_up(0, 2)
    go(hidden_send(0))
    spread_rest(1)
    for copy in w_copies[16:]:
        copy.wait()
    for copy in mate_w:
        copy.wait_recv()
    hidden_send(0).wait_recv()
    reduce_start(0)
    reduce_own(0)
    spread_far(1)
    whole_mate().wait_recv()

    gate_up(2, 0)
    gate_up(2, 1)
    reduce_hop(0)
    gate_up(2, 2)
    go(hidden_send(2))
    spread_end(1)
    gate_up(1, 0)
    hidden_send(2).wait_recv()
    open_start()
    gate_up(1, 1)
    reduce_end(0)
    gate_up(1, 2)
    go(hidden_send(1))
    hidden_send(1).wait_recv()
    reduce_start(1)
    reduce_own(1)
    reduce_hop(1)
    open_end()
    combine(0)
    reduce_end(1)
    total = moe_own[...]
    for k in range(3):
        moe_copy(k).wait_recv()
        total = total + moe_in[k].astype(F32)
    moe_own[...] = total
    combine(1)

    mixed = moe_own[...]
    squares_start(1, mixed)
    result[...] = (mixed * squares_end(1) * final_gain[...]).astype(BF)
    for copy in sent:
        copy.wait_send()


V = pltpu.VMEM


def layer(operands, collective_id):
    spaces = [pltpu.VMEM] * 3 + [pl.ANY] * 2 + [pltpu.VMEM] * 2 + [pl.ANY] + [pltpu.VMEM] * 5 + [pl.ANY] * 3
    return pl.pallas_call(
        layer_kernel,
        out_shape=jax.ShapeDtypeStruct((128, FW), BF),
        in_specs=[pl.BlockSpec(memory_space=space) for space in spaces],
        out_specs=pl.BlockSpec(memory_space=pltpu.VMEM),
        scratch_shapes=[
            V((NDP * DEC, FW), BF),
            V((2048, HD), BF),
            V((2048, HD), BF),
            V((FW, D), BF),
            V((128, NDP * DEC), BF),
            V((4, 128, 128), F32),
            V((4, 128, 128), F32),
            V((128, FW), F32),
            V((128, FW), BF),
            V((NDP * DEC, FW), BF),
            V((NDP - 1, DEC, FW), BF),
            V((8, 8, 128), F32),
            V((NDP, 8, 128), F32),
            V((128, FW), BF),
            V((7, 128, FW), BF),
            V((7, 128, FW), BF),
            V((2, 8, 8, 128), F32),
            V((128, FW), F32),
            V((2, 128, E * C), BF),
            V((NA, E, SL, FW), BF),
            V((NCH, RC, D), BF),
            V((D, HID), BF),
            V((D, HID), BF),
            V((2, HID, D // 2), BF),
            V((NCH, 2, RC, HID), BF),
            V((NA, 3, RC, FW), BF),
            V((NA, RC, FW), F32),
            V((NA, 2, RC // 2, FW), BF),
            V((NA, 2, RC // 2, FW), BF),
            V((NA, 2, RC, FW), BF),
            V((NA, RC, FW), BF),
            V((NA, E, 2, SL, FW), BF),
            V((4, 128, FW), BF),
            V((E, SL, 4 * FW), BF),
            V((RC, 4 * FW), BF),
            V((E, 2, SL, 4 * FW), BF),
            V((3, 128, FW), BF),
            V((3, 128, FW), BF),
            V((128, FW), F32),
            V((NCH, E, SL, 128), BF),
            V((NCH, RC, 128), BF),
            DMA((4,)),
            DMA((2, 3)),
            DMA((2, 3)),
            DMA((2, 4, 3)),
            DMA((2, 4, 3)),
            DMA((2, NDP - 1)),
            DMA((2, NDP - 1)),
            DMA((NDP - 1,)),
            DMA((NDP - 1,)),
            DMA((3, 7)),
            DMA((3, 7)),
            DMA((20,)),
            DMA((3,)),
            DMA((NCH,)),
            DMA((4,)),
            DMA((4,)),
            DMA((NCH, NDP - 1)),
            DMA((NCH, NDP - 1)),
            DMA((NA, 2, 2)),
            DMA((NA, 2, 2)),
            DMA((NA, 2)),
            DMA((NA, 2)),
            DMA((NCH, 4)),
            DMA((NCH, 4)),
            DMA((NCH,)),
            DMA((NCH,)),
            DMA((NA, 2)),
            DMA((NA, 2)),
            DMA((NA, 2, 2)),
            DMA((NA, 2, 2)),
            DMA((NCH, NDP - 1)),
            DMA((NCH, NDP - 1)),
            DMA((3, 3)),
            DMA((3, 3)),
            DMA((3,)),
            DMA((3,)),
            DMA((2, 7)),
            DMA((2, 7)),
            DMA((NDP - 1,)),
            DMA((NDP - 1,)),
            DMA,
        ],
        compiler_params=comm_params(collective_id),
        name="layer",
    )(*operands)


def local(
    residual,
    queries,
    new_keys,
    new_values,
    cache_keys,
    cache_values,
    cache_len,
    page_order,
    out_proj,
    attn_gain,
    routes,
    route_weight,
    gate_proj,
    up_proj,
    down_proj,
    final_gain,
):
    return layer(
        (
            queries,
            new_keys,
            new_values,
            cache_keys.reshape(-1, HD),
            cache_values.reshape(-1, HD),
            cache_len.reshape(8, 128),
            page_order.reshape(16, 128),
            out_proj,
            residual,
            attn_gain.reshape(32, 128),
            routes.T,
            route_weight.T,
            final_gain[None, :],
            gate_proj,
            up_proj,
            down_proj,
        ),
        0,
    )


def solution(mesh):
    return jax.shard_map(
        local,
        mesh=mesh,
        in_specs=(
            P("dp", "mp"),
            P("dp", "mp"),
            P("dp", "mp"),
            P("dp", "mp"),
            P("dp", None, "mp"),
            P("dp", None, "mp"),
            P(),
            P(),
            P("mp", None),
            P(),
            P("dp", None),
            P("dp", None),
            P(None, ("dp", "mp")),
            P(None, ("dp", "mp")),
            P(("dp", "mp"), None),
            P("mp"),
        ),
        out_specs=P("dp", "mp"),
        check_vma=False,
    )
```

```python
import functools

import jax
import jax.numpy as jnp
from jax import lax
from jax.experimental import pallas as pl
from jax.experimental.pallas import tpu as pltpu
from jax.sharding import PartitionSpec as P

D = 4096
HQ = 32
KVH = 8
HD = 128
E = 8
PAGE = 16
DEC = 64
PRE = 64
C = 48
NDP = 16
NCH = 3
NA = 2
NB = 2
SL = C // NCH
RC = NDP * SL
FW = 512
HID = 768

MESH = pl.DeviceIdType.MESH
DMA = pltpu.SemaphoreType.DMA
BF = jnp.bfloat16
F32 = jnp.float32

neg_big = -1e30
eps_norm = 1e-05


def remote(src, dst, send_sem, recv_sem, device):
    return pltpu.make_async_remote_copy(
        src_ref=src,
        dst_ref=dst,
        send_sem=send_sem,
        recv_sem=recv_sem,
        device_id=device,
        device_id_type=MESH,
    )


def greet(devices):
    barrier = pltpu.get_barrier_semaphore()
    for device in devices:
        pl.semaphore_signal(barrier, inc=1, device_id=device, device_id_type=MESH)
    pl.semaphore_wait(barrier, len(devices))


def comm_params(collective_id):
    return pltpu.CompilerParams(
        collective_id=collective_id, has_side_effects=True, vmem_limit_bytes=60 << 20
    )


def iota(shape, axis):
    return lax.broadcasted_iota(jnp.int32, shape, axis)


def square_sums(rows):
    ones = jnp.ones((8, FW), F32)
    return lax.dot_general(
        ones,
        rows * rows,
        (((1,), (1,)), ((), ())),
        precision=lax.Precision.HIGHEST,
        preferred_element_type=F32,
    )


def as_columns(row):
    wide = jnp.broadcast_to(row[0:1, :], (128, 128)).T
    return jnp.concatenate([wide] * (FW // 128), axis=1)


def to_columns(stack):
    return stack.T


def layer_kernel(
    queries,
    new_keys,
    new_values,
    keys,
    values,
    lengths,
    order,
    out_proj,
    residual,
    attn_gain,
    routes,
    weight,
    final_gain,
    wg,
    wu,
    wd,
    result,
    q_all,
    keys_v,
    values_v,
    proj_v,
    owners,
    scores,
    weights,
    page_q,
    page_w,
    val_out,
    val_in,
    stat_out,
    stat_in,
    attn,
    proj_part,
    got,
    squares,
    hidden,
    picks,
    send,
    x_all,
    wg_v,
    wu_v,
    wd_v,
    hid,
    part,
    own_part,
    hop_in,
    hop_out,
    fin,
    out,
    ret,
    tokens,
    send_b,
    part_b,
    ret_b,
    moe_out,
    moe_in,
    moe_own,
    scale_out,
    scale_in,
    l_sems,
    s1,
    r1,
    s2,
    r2,
    vs,
    vr,
    ts,
    tr,
    ps,
    pr,
    w_sems,
    a_own,
    r_own,
    wp_send,
    wp_recv,
    a_send,
    a_recv,
    g_send,
    g_recv,
    f_send,
    f_recv,
    p_send,
    p_recv,
    h_send,
    h_recv,
    t_send,
    t_recv,
    n_send,
    n_recv,
    r_send,
    r_recv,
    k_send,
    k_recv,
    m_send,
    m_recv,
    q_send,
    q_recv,
    c_send,
    c_recv,
    c_own,
):
    dp = lax.axis_index("dp")
    mp = lax.axis_index("mp")
    z, y = dp // 4, lax.rem(dp, 4)
    scale = HD ** (-0.5)
    offsets = ((2, 2), (2, 3), (3, 2), (2, 1), (1, 2), (2, 0), (0, 2), (3, 1), (1, 3), (3, 3), (1, 1), (3, 0), (0, 3), (1, 0), (0, 1))
    peers = [lax.rem(z + a, 4) * 4 + lax.rem(y + b, 4) for a, b in offsets]
    mp_offsets = ((2, 0), (2, 1), (1, 0), (3, 0), (1, 1), (3, 1), (0, 1))
    mp_peers = [lax.rem(mp // 2 + a, 4) * 2 + lax.rem(mp + b, 2) for a, b in mp_offsets]
    x, c = mp // 2, lax.rem(mp, 2)
    xr, xo, xl = lax.rem(x + 1, 4), lax.rem(x + 2, 4), lax.rem(x + 3, 4)
    mr, mo, ml = xr * 2 + c, xo * 2 + c, xl * 2 + c
    right, left, mate = {"mp": mr}, {"mp": ml}, {"mp": x * 2 + 1 - c}
    sides = (right, left)
    x_peers = [{"mp": lax.rem(x + k, 4) * 2 + c} for k in range(1, 4)]
    half = RC // 2

    def wide(owner):
        return pl.ds(pl.multiple_of((lax.rem(owner, 2) * 4 + owner // 2) * FW, FW), FW)

    def columns(owner):
        return pl.ds(pl.multiple_of(owner * FW, FW), FW)

    dp_rows = pl.ds(pl.multiple_of(dp * SL, SL), SL)
    c_cols = pl.ds(pl.multiple_of(c * 4 * FW, 4 * FW), 4 * FW)
    mate_cols = pl.ds(pl.multiple_of((1 - c) * 4 * FW, 4 * FW), 4 * FW)

    w_copies = []
    for w, (src, dst) in enumerate(((wg, wg_v), (wu, wu_v))):
        for core in range(2):
            for chip in range(4):
                w_copies.append(
                    pltpu.make_async_copy(
                        src.at[pl.ds((chip * 2 + core) * FW, FW), :],
                        dst.at[pl.ds((core * 4 + chip) * FW, FW), :],
                        w_sems.at[w * 8 + core * 4 + chip],
                    )
                )
    for j in range(4):
        w_copies.append(
            pltpu.make_async_copy(
                wd.at[:, pl.ds(pl.multiple_of(j * 1024 + c * FW, FW), FW)],
                wd_v.at[0, :, pl.ds(j * FW, FW)],
                w_sems.at[16 + j],
            )
        )
    loads = [
        pltpu.make_async_copy(keys, keys_v, l_sems.at[0]),
        pltpu.make_async_copy(values, values_v, l_sems.at[1]),
        pltpu.make_async_copy(out_proj, proj_v, l_sems.at[2]),
    ]
    q_rows = DEC // 2

    def q_half(owner, h):
        return q_all.at[pl.ds(pl.multiple_of(owner * DEC + h * q_rows, q_rows), q_rows), :]

    own_q = pltpu.make_async_copy(
        queries.at[pl.ds(0, DEC), :],
        q_all.at[pl.ds(pl.multiple_of(dp * DEC, DEC), DEC), :],
        l_sems.at[3],
    )
    own_q.start()
    loads[2].start()
    loads[0].start()
    loads[1].start()
    own_q.wait()
    for copy in w_copies:
        copy.start()
    greet([{"dp": p} for p in peers] + [{"mp": p} for p in mp_peers])
    sent = []

    def go(copy):
        copy.start()
        sent.append(copy)

    def group(along, step, across):
        zz = lax.rem(z + (step if along == 0 else across) + 8, 4)
        yy = lax.rem(y + (across if along == 0 else step) + 8, 4)
        return zz * 4 + yy

    def first(h, k):
        return remote(q_half(dp, h), q_half(dp, h), s1.at[h, k - 1], r1.at[h, k - 1], {"dp": group(h, k, 0)})

    def second(h, j, k):
        owner = group(h, -j, 0)
        return remote(
            q_half(owner, h), q_half(owner, h), s2.at[h, j, k - 1], r2.at[h, j, k - 1], {"dp": group(h, 0, k)}
        )

    for k in (2, 1, 3):
        for h in range(2):
            go(first(h, k))
    for k in (2, 1, 3):
        for h in range(2):
            go(second(h, 0, k))
    mate_w = []
    for j in range(4):
        mate_w.append(
            remote(
                wd.at[:, pl.ds(pl.multiple_of(j * 1024 + (1 - c) * FW, FW), FW)],
                wd_v.at[1, :, pl.ds(j * FW, FW)],
                wp_send.at[j],
                wp_recv.at[j],
                mate,
            )
        )
        go(mate_w[j])

    lane = iota((128, 128), 1)
    row = iota((128, 128), 0)
    counts = lax.shift_right_logical(lengths[...] + (PAGE - 1), 4)
    upto = (row <= lane).astype(BF)
    within = jnp.dot(counts.astype(F32).astype(BF), upto, preferred_element_type=F32)
    place = jnp.zeros((128, 128), F32)
    ids = dp * 128 + row
    for q in range(16):
        place = place + jnp.where(order[q : q + 1, :] == ids, (lane + q * 128).astype(F32), 0.0)
    place = jnp.sum(place, axis=1, keepdims=True)
    before = jnp.zeros((1, 1), F32)
    passed = jnp.zeros((128, 128), F32)
    ends = []
    for i in range(8):
        ends.append(within[i : i + 1, :] + before)
        before = before + within[i : i + 1, 127:128]
        passed = passed + jnp.where(ends[i] <= place, 1.0, 0.0)
    owner = jnp.sum(passed, axis=1, keepdims=True)

    for k in range(1, 4):
        for h in range(2):
            remote(q_half(dp, h), q_half(group(h, -k, 0), h), s1.at[h, k - 1], r1.at[h, k - 1], {"dp": peers[0]}).wait_recv()
            for kk in (2, 1, 3):
                go(second(h, k, kk))

    begin = jnp.zeros((128, 128), F32)
    length = jnp.zeros((128, 128), F32)
    for i in range(8):
        mine = (lane + i * 128).astype(F32) == owner
        cnt = counts[i : i + 1, :].astype(F32)
        begin = begin + jnp.where(mine, ends[i] - cnt, 0.0)
        length = length + jnp.where(mine, lengths[i : i + 1, :].astype(F32), 0.0)
        owners[:, i * 128 : (i + 1) * 128] = jnp.where(mine, 1.0, 0.0).astype(BF)
    begin = jnp.sum(begin, axis=1, keepdims=True)
    length = jnp.sum(length, axis=1, keepdims=True)
    valid = length - (place - begin) * PAGE
    key_ok = (lax.shift_right_logical(lane, 4) == (row & 7)) & ((lane & 15).astype(F32) < valid)
    owner_row = jnp.broadcast_to(owner, (128, 128)).T
    same = owner_row == owner
    leader = jnp.sum(jnp.where(same & (lane < row), 1.0, 0.0), axis=1, keepdims=True) == 0.0

    below = (lane < row).astype(BF)
    route = [
        jnp.broadcast_to(routes[k : k + 1, :].astype(F32), (128, 128)).T[:, 0:1].astype(jnp.int32) for k in range(2)
    ]
    named = [(lane == r).astype(F32) for r in route]
    ahead = [jnp.dot(below, n.astype(BF), preferred_element_type=F32) for n in named]
    ahead[1] = ahead[1] + jnp.sum(named[0], axis=0, keepdims=True)
    cells = iota((128, E * C), 1)
    for k in range(2):
        slot = jnp.sum(named[k] * ahead[k], axis=1, keepdims=True).astype(jnp.int32)
        target = lax.shift_right_logical(slot, 4) * (E * SL) + route[k] * SL + (slot & (SL - 1))
        picks[k] = jnp.where(cells == target, 1.0, 0.0).astype(BF)

    causal = iota((PRE, PRE), 0) >= iota((PRE, PRE), 1)
    for g in range(4):
        cols = slice(g * HD, (g + 1) * HD)
        s = lax.dot_general(
            queries[DEC:, cols], new_keys[DEC:, :], (((1,), (1,)), ((), ())), preferred_element_type=F32
        )
        s = jnp.where(causal, s * scale, neg_big)
        w = jnp.where(causal, jnp.exp(s - jnp.max(s, axis=1, keepdims=True)), 0.0)
        den = jnp.sum(w, axis=1, keepdims=True)
        num = jnp.dot(w.astype(BF), new_values[DEC:, :], preferred_element_type=F32)
        attn[DEC:, cols] = (num / den).astype(BF)
    loads[2].wait()

    pieces = ((0, 32), (32, 32), (64, 64))

    def piece_copy(i, k):
        rows = pl.ds(*pieces[i])
        return remote(
            proj_part.at[k, rows], got.at[k, rows], ps.at[i, k], pr.at[i, k], {"mp": mp_peers[k]}
        )

    def project(i):
        rows = pl.ds(*pieces[i])
        a = attn[rows, :]
        for k, p in enumerate(mp_peers):
            cols = pl.ds(pl.multiple_of(p * FW, FW), FW)
            proj_part[k, rows] = jnp.dot(a, proj_v[:, cols], preferred_element_type=F32).astype(BF)
            go(piece_copy(i, k))
        cols = pl.ds(pl.multiple_of(mp * FW, FW), FW)
        own = jnp.dot(a, proj_v[:, cols], preferred_element_type=F32)
        hidden[rows, :] = own + residual[rows, :].astype(F32)

    def collect(i):
        rows = pl.ds(*pieces[i])
        total = hidden[rows, :]
        for k in range(7):
            piece_copy(i, k).wait_recv()
            total = total + got[k, rows].astype(F32)
        hidden[rows, :] = total

    project(2)

    own_cols = jnp.zeros((64, 128), F32)
    lane64 = iota((64, 128), 1)
    for g in range(4):
        prod = queries[:DEC, g * HD : (g + 1) * HD].astype(F32) * new_keys[:DEC, :].astype(F32)
        own_cols = jnp.where(lane64 == g, jnp.sum(prod, axis=1, keepdims=True) * scale, own_cols)
    own_score = to_columns(jnp.concatenate([own_cols, jnp.zeros((64, 128), F32)], axis=0))[0:8, :]

    for j in range(4):
        for k in range(1, 4):
            for h in range(2):
                remote(
                    q_half(dp, h), q_half(group(h, -j, -k), h), s2.at[h, j, k - 1], r2.at[h, j, k - 1], {"dp": peers[0]}
                ).wait_recv()

    page_q[...] = jnp.dot(owners[...], q_all[...], preferred_element_type=F32)
    loads[0].wait()
    loads[1].wait()
    for k in range(16):
        qk = jnp.concatenate([page_q[8 * k : 8 * k + 8, g * HD : (g + 1) * HD] for g in range(4)], axis=0)
        s = lax.dot_general(
            qk.astype(BF), keys_v[128 * k : 128 * (k + 1), :], (((1,), (1,)), ((), ())), preferred_element_type=F32
        )
        for g in range(4):
            scores[g, 8 * k : 8 * k + 8, :] = s[8 * g : 8 * g + 8, :]
    tops = jnp.zeros((128, 128), F32)
    sums = []
    for g in range(4):
        s = jnp.where(key_ok, scores[g] * scale, neg_big)
        m = jnp.max(s, axis=1, keepdims=True)
        w = jnp.where(key_ok, jnp.exp(s - m), 0.0)
        weights[g] = w
        sums.append(jnp.sum(w, axis=1, keepdims=True))
        tops = jnp.where(lane == g, m, tops)
    for k in range(16):
        wk = jnp.concatenate([weights[g, 8 * k : 8 * k + 8, :] for g in range(4)], axis=0)
        v = jnp.dot(wk.astype(BF), values_v[128 * k : 128 * (k + 1), :], preferred_element_type=F32)
        for g in range(4):
            scores[g, 8 * k : 8 * k + 8, :] = v[8 * g : 8 * g + 8, :]
    top_rows = tops.T
    stat = jnp.zeros((128, 128), F32)
    for g in range(4):
        top = jnp.max(jnp.where(same, top_rows[g : g + 1, :], neg_big), axis=1, keepdims=True)
        factor = jnp.exp(tops[:, g : g + 1] - top)
        page_w[:, g * HD : (g + 1) * HD] = (scores[g] * factor).astype(BF)
        stat = jnp.where(lane == g, jnp.where(leader, top, 0.0), stat)
        stat = jnp.where(lane == 4 + g, sums[g] * factor, stat)
    stat8 = stat.T[0:8, :]
    for i in range(8):
        stat_out[i] = jnp.dot(
            stat8,
            owners[:, i * 128 : (i + 1) * 128].astype(F32),
            precision=lax.Precision.HIGHEST,
            preferred_element_type=F32,
        )
    for i in range(4):
        val_out[i * 256 : (i + 1) * 256, :] = lax.dot_general(
            owners[:, i * 256 : (i + 1) * 256], page_w[...], (((0,), (0,)), ((), ())), preferred_element_type=F32
        ).astype(BF)

    def swap_stat(k):
        p = peers[k]
        return remote(stat_out.at[p // 2], stat_in.at[k], ts.at[k], tr.at[k], {"dp": p})

    def swap_val(h, k):
        p = peers[k]
        rows = pl.ds(pl.multiple_of(p * DEC + h * 32, 32), 32)
        return remote(val_out.at[rows, :], val_in.at[k, pl.ds(h * 32, 32), :], vs.at[h, k], vr.at[h, k], {"dp": p})

    for k in range(NDP - 1):
        go(swap_stat(k))
        go(swap_val(0, k))
    for k in range(NDP - 1):
        go(swap_val(1, k))

    def square_copy(t, k):
        return remote(squares.at[t, 7], squares.at[t, k], q_send.at[t, k], q_recv.at[t, k], {"mp": mp_peers[k]})

    def squares_start(t, rows):
        squares[t, 7] = square_sums(rows)
        for k in range(7):
            go(square_copy(t, k))

    def squares_end(t):
        summed = squares[t, 7]
        for k in range(7):
            square_copy(t, k).wait_recv()
            summed = summed + squares[t, k]
        return as_columns(lax.rsqrt(summed / D + eps_norm))

    def token_copy(i, k):
        rows = tokens.at[x, pl.ds(*pieces[i]), :]
        return remote(rows, rows, k_send.at[i, k], k_recv.at[i, k], x_peers[k])

    gain_rows = attn_gain[pl.ds(mp * 4, 4), :]
    gain_cols = jnp.concatenate([gain_rows[i : i + 1, :] for i in range(4)], axis=1)

    def finish(i):
        rows = pl.ds(*pieces[i])
        tokens[x, rows, :] = (hidden[rows, :] * gain_cols).astype(BF)
        for k in (1, 0, 2):
            go(token_copy(i, k))

    collect(2)
    finish(2)
    for k in range(NDP - 1):
        swap_stat(k).wait_recv()
    stat_in[NDP - 1] = stat_out[dp // 2]
    odd = lax.rem(dp, 2) == 1
    got_stats = stat_in[...].reshape(128, 128)
    got_stats = jnp.where(odd, pltpu.roll(got_stats, 64, 1), got_stats).reshape(NDP, 8, 128)
    l_in = pltpu.roll(got_stats, 4, 1)
    m_in = jnp.where(l_in > 0.0, got_stats, neg_big)
    top = jnp.maximum(jnp.max(m_in, axis=0), own_score)
    f_in = jnp.where(l_in > 0.0, jnp.exp(jnp.minimum(m_in - top[None], 0.0)), 0.0)
    f_own = jnp.exp(own_score - top)
    inv = 1.0 / (jnp.sum(l_in * f_in, axis=0) + f_own)
    f_cols = to_columns((f_in * inv[None]).reshape(128, 128))
    own_f = to_columns(jnp.concatenate([f_own * inv, jnp.zeros((120, 128), F32)], axis=0))
    for h in range(2):
        rows = slice(h * 32, (h + 1) * 32)
        nums = [own_f[rows, g : g + 1] * new_values[rows, :].astype(F32) for g in range(4)]
        mine = val_out[pl.ds(pl.multiple_of(dp * DEC + h * 32, 32), 32), :]
        for k in range(NDP):
            if k < NDP - 1:
                swap_val(h, k).wait_recv()
            v = (val_in[k, rows] if k < NDP - 1 else mine).astype(F32)
            for g in range(4):
                nums[g] = nums[g] + v[:, g * HD : (g + 1) * HD] * f_cols[rows, 8 * k + g : 8 * k + g + 1]
        for g in range(4):
            attn[rows, g * HD : (g + 1) * HD] = nums[g].astype(BF)
        project(h)
    for h in range(2):
        collect(h)
        finish(h)

    def block(ch, h, owner):
        return x_all.at[ch, pl.ds(h * half, half), wide(owner)]

    def whole(ch, owner):
        return x_all.at[ch, :, wide(owner)]

    def neighbour(ch, side, h):
        return remote(block(ch, h, mp), block(ch, h, mp), g_send.at[ch, side, h], g_recv.at[ch, side, h], sides[side])

    def onward(ch, side):
        owner = (ml, mr)[side]
        return remote(
            block(ch, side, owner), block(ch, side, owner), f_send.at[ch, side], f_recv.at[ch, side], sides[side]
        )

    def to_mate(ch, which):
        owner = (mp, ml, mr, mo)[which]
        return remote(whole(ch, owner), whole(ch, owner), p_send.at[ch, which], p_recv.at[ch, which], mate)

    def slice_copy(ch, k):
        p = peers[k]
        return remote(
            send.at[ch, p // 2], x_all.at[ch, dp_rows, wide(mp)], a_send.at[ch, k], a_recv.at[ch, k], {"dp": p}
        )

    def slice_own(ch):
        return pltpu.make_async_copy(send.at[ch, dp // 2], x_all.at[ch, dp_rows, wide(mp)], a_own.at[ch])

    def spread_own(ch):
        for k in range(NDP - 1):
            slice_copy(ch, k).wait_recv()
        slice_own(ch).wait()
        for h in range(2):
            go(neighbour(ch, 0, h))
            go(neighbour(ch, 1, 1 - h))
        go(to_mate(ch, 0))

    def spread_on(ch):
        for side in range(2):
            neighbour(ch, side, side).wait_recv()
            go(onward(ch, side))

    def spread_rest(ch):
        for side in range(2):
            neighbour(ch, side, 1 - side).wait_recv()
            go(to_mate(ch, 1 + side))

    def spread_far(ch):
        for side in range(2):
            onward(ch, side).wait_recv()
        go(to_mate(ch, 3))

    def spread_end(ch):
        for which in range(4):
            to_mate(ch, which).wait_recv()

    def whole_copy(k):
        p = peers[k]
        return remote(send_b.at[p // 2], x_all.at[2, dp_rows, c_cols], a_send.at[2, k], a_recv.at[2, k], {"dp": p})

    def whole_own():
        return pltpu.make_async_copy(send_b.at[dp // 2], x_all.at[2, dp_rows, c_cols], a_own.at[2])

    def whole_mate():
        return remote(x_all.at[2, :, c_cols], x_all.at[2, :, c_cols], p_send.at[2, 0], p_recv.at[2, 0], mate)

    def whole_start():
        for i in range(3):
            for k in range(3):
                token_copy(i, k).wait_recv()
        dispatch = picks[0, :, NA * 128 :] + picks[1, :, NA * 128 :]
        for chip in range(4):
            rows = lax.dot_general(
                dispatch, tokens[chip], (((0,), (0,)), ((), ())), preferred_element_type=F32
            ).astype(BF)
            send_b[:, :, chip * FW : (chip + 1) * FW] = rows.reshape(E, SL, FW)
        whole_own().start()
        for k in range(NDP - 1):
            go(whole_copy(k))

    def whole_spread():
        for k in range(NDP - 1):
            whole_copy(k).wait_recv()
        whole_own().wait()
        go(whole_mate())

    def scale_copy(k):
        p = peers[k]
        return remote(
            scale_out.at[:, p // 2], scale_in.at[:, dp_rows, :], c_send.at[k], c_recv.at[k], {"dp": p}
        )

    def scale_own():
        return pltpu.make_async_copy(scale_out.at[:, dp // 2], scale_in.at[:, dp_rows, :], c_own)

    def scale_start():
        scales = squares_end(0)[:, :128]
        upper = scales.astype(BF)
        lower = (scales - upper.astype(F32)).astype(BF)
        both = jnp.where(iota((128, 128), 1) < 64, upper.astype(F32), lower.astype(F32)).astype(BF)
        for ch in range(NCH):
            rows = lax.dot_general(
                dispatch[:, ch * 128 : (ch + 1) * 128], both, (((0,), (0,)), ((), ())), preferred_element_type=F32
            ).astype(BF)
            scale_out[ch] = rows.reshape(E, SL, 128)
        scale_own().start()
        for k in range(NDP - 1):
            go(scale_copy(k))

    def scale_end():
        for k in range(NDP - 1):
            scale_copy(k).wait_recv()
        scale_own().wait()

    def hidden_send(ch):
        return remote(hid.at[ch, 0], hid.at[ch, 1], h_send.at[ch], h_recv.at[ch], mate)

    def gate_up(ch, n):
        cols = pl.ds(n * 256, 256)
        rows = x_all[ch]
        scales = scale_in[ch, :, 0:1].astype(F32) + scale_in[ch, :, 64:65].astype(F32)
        g = jnp.dot(rows, wg_v[:, cols], preferred_element_type=F32) * scales
        u = jnp.dot(rows, wu_v[:, cols], preferred_element_type=F32) * scales
        hid[ch, 0, :, cols] = (g / (1.0 + jnp.exp(-g)) * u).astype(BF)

    def down(ch, chip):
        cols = columns(chip)
        return jnp.dot(hid[ch, 0], wd_v[0, :, cols], preferred_element_type=F32) + jnp.dot(
            hid[ch, 1], wd_v[1, :, cols], preferred_element_type=F32
        )

    def rows_of(h):
        return pl.ds(h * half, half)

    def hop(ch, side):
        return remote(
            part.at[ch, 0, rows_of(side)], hop_in.at[ch, side], t_send.at[ch, side], t_recv.at[ch, side], sides[side]
        )

    def near(ch, side, h, src):
        return remote(src, fin.at[ch, side, rows_of(h)], n_send.at[ch, side, h], n_recv.at[ch, side, h], sides[side])

    def reduce_start(ch):
        part[ch, 0] = down(ch, xo).astype(BF)
        for side in range(2):
            go(hop(ch, side))
        for side in range(2):
            part[ch, 1 + side] = down(ch, (xr, xl)[side]).astype(BF)
            go(near(ch, side, 1 - side, part.at[ch, 1 + side, rows_of(1 - side)]))

    def reduce_own(ch):
        own_part[ch] = down(ch, x)

    def reduce_hop(ch):
        for side in range(2):
            hop(ch, side).wait_recv()
            hop_out[ch, side] = (
                part[ch, 1 + side, rows_of(side), :].astype(F32) + hop_in[ch, side].astype(F32)
            ).astype(BF)
            go(near(ch, side, side, hop_out.at[ch, side]))

    e_of, j_of = dp // 2, lax.rem(dp, 2)

    def back_copy(ch, k):
        p = peers[k]
        rows = pl.ds(pl.multiple_of(p * SL, SL), SL)
        return remote(out.at[ch, rows], ret.at[ch, e_of, j_of], r_send.at[ch, k], r_recv.at[ch, k], {"dp": p})

    def back_own(ch):
        return pltpu.make_async_copy(out.at[ch, dp_rows], ret.at[ch, e_of, j_of], r_own.at[ch])

    def reduce_end(ch):
        for side in range(2):
            for h in range(2):
                near(ch, side, h, hop_out.at[ch, side]).wait_recv()
        total = own_part[ch] + fin[ch, 0].astype(F32) + fin[ch, 1].astype(F32)
        out[ch] = total.astype(BF)
        back_own(ch).start()
        for k in range(NDP - 1):
            go(back_copy(ch, k))

    def open_copy(k):
        p = peers[k]
        rows = pl.ds(pl.multiple_of(p * SL, SL), SL)
        return remote(part_b.at[rows], ret_b.at[e_of, j_of], r_send.at[2, k], r_recv.at[2, k], {"dp": p})

    def open_own():
        return pltpu.make_async_copy(part_b.at[dp_rows], ret_b.at[e_of, j_of], r_own.at[2])

    def open_start():
        for chip in range(4):
            part_b[:, chip * FW : (chip + 1) * FW] = down(2, chip).astype(BF)
        open_own().start()
        for k in range(NDP - 1):
            go(open_copy(k))

    def shares(k):
        wide_w = jnp.broadcast_to(weight[k : k + 1, :], (128, 128)).T
        return jnp.concatenate([wide_w] * (FW // 128), axis=1)

    def moe_copy(k):
        return remote(moe_out.at[k], moe_in.at[k], m_send.at[k], m_recv.at[k], x_peers[k])

    def open_end():
        for k in range(NDP - 1):
            open_copy(k).wait_recv()
        open_own().wait()
        w = [shares(k) for k in range(2)]

        def mix(chip):
            both = [ret_b[:, j, :, columns(chip)].reshape(128, FW) for j in range(2)]
            total = jnp.zeros((128, FW), F32)
            for k in range(2):
                pick = picks[k, :, NA * 128 :]
                rows = jnp.dot(pick, both[0], preferred_element_type=F32)
                rows = rows + jnp.dot(pick, both[1], preferred_element_type=F32)
                total = total + w[k] * rows
            return total

        for k in (1, 0, 2):
            moe_out[k] = mix(lax.rem(x + 1 + k, 4)).astype(BF)
            go(moe_copy(k))
        moe_own[...] = mix(x) + hidden[...]

    def combine(ch):
        for k in range(NDP - 1):
            back_copy(ch, k).wait_recv()
        back_own(ch).wait()
        total = moe_own[...]
        for k in range(2):
            pick = picks[k, :, ch * 128 : (ch + 1) * 128]
            rows = jnp.dot(pick, ret[ch, :, 0].reshape(128, FW), preferred_element_type=F32)
            rows = rows + jnp.dot(pick, ret[ch, :, 1].reshape(128, FW), preferred_element_type=F32)
            total = total + shares(k) * rows
        moe_own[...] = total

    dispatch = picks[0] + picks[1]
    for ch in range(NA):
        rows = lax.dot_general(
            dispatch[:, ch * 128 : (ch + 1) * 128], tokens[x], (((0,), (0,)), ((), ())), preferred_element_type=F32
        ).astype(BF)
        send[ch] = rows.reshape(E, SL, FW)
        slice_own(ch).start()
        for k in range(NDP - 1):
            go(slice_copy(ch, k))
    squares_start(0, hidden[...])
    spread_own(0)
    scale_start()
    whole_start()
    spread_on(0)
    spread_own(1)
    spread_rest(0)
    spread_far(0)
    for copy in w_copies[:16]:
        copy.wait()
    spread_end(0)
    scale_end()

    gate_up(0, 0)
    spread_on(1)
    gate_up(0, 1)
    whole_spread()
    gate_up(0, 2)
    go(hidden_send(0))
    spread_rest(1)
    for copy in w_copies[16:]:
        copy.wait()
    for copy in mate_w:
        copy.wait_recv()
    hidden_send(0).wait_recv()
    reduce_start(0)
    reduce_own(0)
    spread_far(1)
    whole_mate().wait_recv()

    gate_up(2, 0)
    gate_up(2, 1)
    reduce_hop(0)
    gate_up(2, 2)
    go(hidden_send(2))
    spread_end(1)
    gate_up(1, 0)
    hidden_send(2).wait_recv()
    open_start()
    gate_up(1, 1)
    reduce_end(0)
    gate_up(1, 2)
    go(hidden_send(1))
    hidden_send(1).wait_recv()
    reduce_start(1)
    reduce_own(1)
    reduce_hop(1)
    open_end()
    combine(0)
    reduce_end(1)
    total = moe_own[...]
    for k in range(3):
        moe_copy(k).wait_recv()
        total = total + moe_in[k].astype(F32)
    moe_own[...] = total
    combine(1)

    mixed = moe_own[...]
    squares_start(1, mixed)
    result[...] = (mixed * squares_end(1) * final_gain[...]).astype(BF)
    for copy in sent:
        copy.wait_send()


V = pltpu.VMEM


def layer(operands, collective_id):
    spaces = [pltpu.VMEM] * 3 + [pl.ANY] * 2 + [pltpu.VMEM] * 2 + [pl.ANY] + [pltpu.VMEM] * 5 + [pl.ANY] * 3
    return pl.pallas_call(
        layer_kernel,
        out_shape=jax.ShapeDtypeStruct((128, FW), BF),
        in_specs=[pl.BlockSpec(memory_space=space) for space in spaces],
        out_specs=pl.BlockSpec(memory_space=pltpu.VMEM),
        scratch_shapes=[
            V((NDP * DEC, FW), BF),
            V((2048, HD), BF),
            V((2048, HD), BF),
            V((FW, D), BF),
            V((128, NDP * DEC), BF),
            V((4, 128, 128), F32),
            V((4, 128, 128), F32),
            V((128, FW), F32),
            V((128, FW), BF),
            V((NDP * DEC, FW), BF),
            V((NDP - 1, DEC, FW), BF),
            V((8, 8, 128), F32),
            V((NDP, 8, 128), F32),
            V((128, FW), BF),
            V((7, 128, FW), BF),
            V((7, 128, FW), BF),
            V((2, 8, 8, 128), F32),
            V((128, FW), F32),
            V((2, 128, E * C), BF),
            V((NA, E, SL, FW), BF),
            V((NCH, RC, D), BF),
            V((D, HID), BF),
            V((D, HID), BF),
            V((2, HID, D // 2), BF),
            V((NCH, 2, RC, HID), BF),
            V((NA, 3, RC, FW), BF),
            V((NA, RC, FW), F32),
            V((NA, 2, RC // 2, FW), BF),
            V((NA, 2, RC // 2, FW), BF),
            V((NA, 2, RC, FW), BF),
            V((NA, RC, FW), BF),
            V((NA, E, 2, SL, FW), BF),
            V((4, 128, FW), BF),
            V((E, SL, 4 * FW), BF),
            V((RC, 4 * FW), BF),
            V((E, 2, SL, 4 * FW), BF),
            V((3, 128, FW), BF),
            V((3, 128, FW), BF),
            V((128, FW), F32),
            V((NCH, E, SL, 128), BF),
            V((NCH, RC, 128), BF),
            DMA((4,)),
            DMA((2, 3)),
            DMA((2, 3)),
            DMA((2, 4, 3)),
            DMA((2, 4, 3)),
            DMA((2, NDP - 1)),
            DMA((2, NDP - 1)),
            DMA((NDP - 1,)),
            DMA((NDP - 1,)),
            DMA((3, 7)),
            DMA((3, 7)),
            DMA((20,)),
            DMA((3,)),
            DMA((NCH,)),
            DMA((4,)),
            DMA((4,)),
            DMA((NCH, NDP - 1)),
            DMA((NCH, NDP - 1)),
            DMA((NA, 2, 2)),
            DMA((NA, 2, 2)),
            DMA((NA, 2)),
            DMA((NA, 2)),
            DMA((NCH, 4)),
            DMA((NCH, 4)),
            DMA((NCH,)),
            DMA((NCH,)),
            DMA((NA, 2)),
            DMA((NA, 2)),
            DMA((NA, 2, 2)),
            DMA((NA, 2, 2)),
            DMA((NCH, NDP - 1)),
            DMA((NCH, NDP - 1)),
            DMA((3, 3)),
            DMA((3, 3)),
            DMA((3,)),
            DMA((3,)),
            DMA((2, 7)),
            DMA((2, 7)),
            DMA((NDP - 1,)),
            DMA((NDP - 1,)),
            DMA,
        ],
        compiler_params=comm_params(collective_id),
        name="layer",
    )(*operands)


def local(
    residual,
    queries,
    new_keys,
    new_values,
    cache_keys,
    cache_values,
    cache_len,
    page_order,
    out_proj,
    attn_gain,
    routes,
    route_weight,
    gate_proj,
    up_proj,
    down_proj,
    final_gain,
):
    return layer(
        (
            queries,
            new_keys,
            new_values,
            cache_keys.reshape(-1, HD),
            cache_values.reshape(-1, HD),
            cache_len.reshape(8, 128),
            page_order.reshape(16, 128),
            out_proj,
            residual,
            attn_gain.reshape(32, 128),
            routes.T,
            route_weight.T,
            final_gain[None, :],
            gate_proj,
            up_proj,
            down_proj,
        ),
        0,
    )


def solution(mesh):
    return jax.shard_map(
        local,
        mesh=mesh,
        in_specs=(
            P("dp", "mp"),
            P("dp", "mp"),
            P("dp", "mp"),
            P("dp", "mp"),
            P("dp", None, "mp"),
            P("dp", None, "mp"),
            P(),
            P(),
            P("mp", None),
            P(),
            P("dp", None),
            P("dp", None),
            P(None, ("dp", "mp")),
            P(None, ("dp", "mp")),
            P(("dp", "mp"), None),
            P("mp"),
        ),
        out_specs=P("dp", "mp"),
        check_vma=False,
    )
```
